128 devices in a mesh: req: 16 (over z, x), tp: 8 (over y, core).
Axes of the slice: x: 4, y: 4, z: 4, core: 2. Of those that a mesh axis runs over, the one named last changes fastest.
Arguments:
- tokens: bfloat16 [8192, 5120], P('req'), may hold values from -6 to 6
- norm_gain: bfloat16 [5120], replicated, may hold values from 0.099609375 to 1.8984375
- w_query: bfloat16 [5120, 5120], P(None, 'tp'), may hold values from -0.078125 to 0.078125
- q_bias: bfloat16 [5120], P('tp'), may hold values from -3 to 3
- w_key_value: bfloat16 [5120, 2048], P(None, 'tp'), may hold values from -0.078125 to 0.078125
- kv_bias: bfloat16 [2048], P('tp'), may hold values from -3 to 3
- w_out: bfloat16 [5120, 5120], P('tp'), may hold values from -0.078125 to 0.078125
- prompt_lengths: int32 [16, 4], replicated, may hold values from 1 to 256, as said below
- request_prompt: int32 [768], replicated, may hold values from 0 to 63, as said below
- cache_slot: int32 [16, 48], P('req'), may hold values from 0 to 47, each once within a row
Outputs:
- attended: bfloat16 [8192, 5120], P(('req', 'tp'))
- prompt_cache: bfloat16 [768, 256, 2048], P('req', None, 'tp')
The draws below stay inside these ranges and needn't reach their ends.
Inputs may be any that keep to these rules, and one draw needn't show every extreme that they name: `request_prompt`: of the 48 requests of one index of req, at most 6 read prompts of one stream, and for every index of req some stream is read by exactly 6 of them. `prompt_lengths`: each stream's lengths sum to 512; one of them, at a place drawn for each stream, is exactly 256, and the others split the rest at drawn points. `cache_slot`: each row is a permutation.
All inputs are finite; a program needn't handle non-finite values.
Results may differ from the reference program's by a relative error of at most 0.0095.
Values may be sent and summed in bfloat16 or wider, within the bound.
A program may use at most 128 MiB of HBM per device.

```python
import math
import jax
import jax.numpy as jnp
from jax import lax

D = 5120
HEADS = 40
KV_HEADS = 8
HEAD_DIM = 128
TOK_DEV = 512
PROMPTS_DEV = 4
FAN = 12
MAXLEN = 256
TOKENS = 8192
REQUESTS = 768
REQ_DEV = 48
CAP = 6
N_REQ = 16
N_TP = 8


def draw_prompt_lengths(key, part):
    rest_rows = TOK_DEV - MAXLEN

    def one_row(row_key):
        key_cuts, key_place = jax.random.split(row_key, 2)
        cut_points = jnp.sort(jax.random.permutation(key_cuts, rest_rows - 1)[:PROMPTS_DEV - 2].astype(jnp.int32) + 1)
        bounds = jnp.concatenate([jnp.zeros((1,), jnp.int32), cut_points, jnp.full((1,), rest_rows, jnp.int32)])
        pieces = bounds[1:] - bounds[:-1]
        longest_at = jax.random.randint(key_place, (), 0, PROMPTS_DEV, dtype=jnp.int32)
        places = jnp.arange(PROMPTS_DEV, dtype=jnp.int32)
        source_index = jnp.clip(places - (places > longest_at).astype(jnp.int32), 0, PROMPTS_DEV - 2)
        return jnp.where(places == longest_at, MAXLEN, pieces[source_index]).astype(jnp.int32)
    row_keys = jax.random.split(jax.random.fold_in(key, 11), N_REQ)
    return jax.vmap(one_row)(row_keys).astype(jnp.int32)


def draw_request_prompt(key, part):
    row_requests = FAN * PROMPTS_DEV
    ticket_total = N_REQ * CAP

    def one_row(row_key):
        key_pick, key_noise, key_mix, key_within = jax.random.split(row_key, 4)
        forced = jax.random.randint(key_pick, (), 0, N_REQ, dtype=jnp.int32)
        ticket_ids = jnp.arange(ticket_total, dtype=jnp.int32)
        noise_draw = jax.random.randint(key_noise, (ticket_total,), 1, 1 << 20, dtype=jnp.int32)
        ranking = jnp.where(ticket_ids // CAP == forced, ticket_ids, noise_draw * ticket_total + ticket_ids)
        chosen = jnp.argsort(ranking)[:row_requests].astype(jnp.int32)
        mixing = jax.random.randint(key_mix, (row_requests,), 0, 1 << 20, dtype=jnp.int32) * row_requests + jnp.arange(row_requests, dtype=jnp.int32)
        shuffled = chosen[jnp.argsort(mixing)]
        stream_ids = shuffled // CAP
        within = jax.random.randint(key_within, (row_requests,), 0, PROMPTS_DEV, dtype=jnp.int32)
        return stream_ids * PROMPTS_DEV + within
    row_keys = jax.random.split(jax.random.fold_in(key, 7), N_REQ)
    return jax.vmap(one_row)(row_keys).reshape(-1).astype(jnp.int32)


def levels(own_key, dims, cuts, least, high):
    def one(dim, blocks):
        draws = jax.random.uniform(jax.random.fold_in(jax.random.fold_in(own_key, 6), dim), (blocks,), jnp.float32, least / len(cuts), high / len(cuts))
        return jnp.repeat(jnp.exp(draws), dims[dim] // blocks).reshape((-1,) + (1,) * (len(dims) - dim - 1))

    loudness = one(*cuts[0])
    for cut in cuts[1:]:
        loudness = loudness * one(*cut)
    return loudness


def bell_draw(key, extent, deviation, limit, cuts=(), held_as=jnp.bfloat16):
    result = deviation * jax.random.normal(key, extent, jnp.float32)
    if cuts:
        result = result * levels(key, extent, cuts, -0.22, 0.18)
    return jnp.clip(result, -limit, limit).astype(held_as)


def setup_inputs(seed: int = 0) -> dict:
    splits = jax.random.split(jax.random.key(seed), 11)
    return {
        "tokens": bell_draw(splits[0], (TOKENS, D), 1.0, 6.0, ((0, 16),)),
        "norm_gain": jnp.clip(1.0 + 0.18 * jax.random.normal(splits[1], (D,), jnp.float32), 0.099609375, 1.8984375).astype(jnp.bfloat16),
        "w_query": bell_draw(splits[2], (D, HEADS * HEAD_DIM), D ** -0.5, 0.078125, ((1, 8),)),
        "q_bias": bell_draw(splits[3], (HEADS * HEAD_DIM,), 0.5, 3.0, ((0, 8),)),
        "w_key_value": bell_draw(splits[4], (D, KV_HEADS * 2 * HEAD_DIM), D ** -0.5, 0.078125, ((1, 8),)),
        "kv_bias": bell_draw(splits[5], (KV_HEADS * 2 * HEAD_DIM,), 0.5, 3.0, ((0, 8),)),
        "w_out": bell_draw(splits[6], (HEADS * HEAD_DIM, D), (HEADS * HEAD_DIM) ** -0.5, 0.078125, ((0, 8),)),
        "prompt_lengths": draw_prompt_lengths(jax.random.fold_in(splits[10], 71), 0),
        "request_prompt": draw_request_prompt(jax.random.fold_in(splits[10], 71), 0),
        "cache_slot": jax.vmap(lambda own: jax.random.permutation(own, REQ_DEV))(jax.random.split(splits[9], N_REQ)).reshape((N_REQ, REQ_DEV)).astype(jnp.int32),
    }


epsilon = 1e-06
rope_base = 1000000.0

def rotary(values, positions):
    half_dim = HEAD_DIM // 2
    inverse_freq = rope_base ** (-(jnp.arange(half_dim, dtype=jnp.float32) * 2.0 / HEAD_DIM))
    angles = positions.astype(jnp.float32)[:, None] * inverse_freq[None, :]
    cosine = jnp.cos(angles)[:, None, :]
    sine_part = jnp.sin(angles)[:, None, :]
    former = values[..., :half_dim]
    latter = values[..., half_dim:]
    return jnp.concatenate([former * cosine - latter * sine_part, latter * cosine + former * sine_part], axis=-1)

def prompt_layout(lengths, row_count):
    prompt_ends = jnp.cumsum(lengths, dtype=jnp.int32)
    starts = prompt_ends - lengths
    places = jnp.arange(row_count, dtype=jnp.int32)
    member = lax.optimization_barrier(jnp.sum((places[:, None] >= prompt_ends[None, :]).astype(jnp.int32), axis=1, dtype=jnp.int32))
    chosen = member[:, None] == jnp.arange(lengths.shape[0], dtype=jnp.int32)[None, :]
    positions = places - lax.optimization_barrier(jnp.sum(jnp.where(chosen, starts[None, :], 0), axis=1, dtype=jnp.int32))
    return (member, positions, starts)

def attend(queries, key_value, member):
    row_count = queries.shape[0]
    head_count = queries.shape[1]
    kv_count = key_value.shape[1]
    grouped = queries.reshape(row_count, kv_count, head_count // kv_count, HEAD_DIM).astype(jnp.float32)
    scores = jnp.einsum('qhgd,khd->hgqk', grouped, key_value[:, :, 0].astype(jnp.float32)) / math.sqrt(HEAD_DIM)
    places = jnp.arange(row_count, dtype=jnp.int32)
    allowed = (member[:, None] == member[None, :]) & (places[None, :] <= places[:, None])
    powers = jnp.where(allowed, jnp.exp(scores), 0.0)
    weights = (powers / lax.optimization_barrier(jnp.sum(powers, axis=-1, keepdims=True))).astype(jnp.bfloat16)
    mixed = jnp.einsum('hgqk,khd->qhgd', weights.astype(jnp.float32), key_value[:, :, 1].astype(jnp.float32))
    return mixed.reshape(row_count, head_count * HEAD_DIM).astype(jnp.bfloat16)

def stream_layer(stream_rows, stream_lengths, norm_gain, w_query, q_bias, w_key_value, kv_bias, w_out):
    member, positions, starts = prompt_layout(stream_lengths, TOK_DEV)
    widened = stream_rows.astype(jnp.float32)
    inverse_rms = lax.rsqrt(lax.optimization_barrier(jnp.mean(widened * widened, axis=1, keepdims=True)) + epsilon)
    normed = (widened * inverse_rms * norm_gain.astype(jnp.float32)[None, :]).astype(jnp.bfloat16)
    projected = jnp.dot(normed, w_query, preferred_element_type=jnp.float32) + q_bias.astype(jnp.float32)[None, :]
    queries = rotary(projected.reshape(TOK_DEV, HEADS, HEAD_DIM), positions).astype(jnp.bfloat16)
    paired = jnp.dot(normed, w_key_value, preferred_element_type=jnp.float32) + kv_bias.astype(jnp.float32)[None, :]
    paired = paired.reshape(TOK_DEV, KV_HEADS, 2, HEAD_DIM)
    rotated = rotary(paired[:, :, 0], positions)
    key_value = jnp.stack([rotated, paired[:, :, 1]], axis=2).astype(jnp.bfloat16)
    context = attend(queries, key_value, member)
    group_cols = HEADS * HEAD_DIM // N_TP
    total = widened
    for group in range(N_TP):
        lower = group * group_cols
        partial_sum = jnp.dot(context[:, lower:lower + group_cols], w_out[lower:lower + group_cols], preferred_element_type=jnp.float32).astype(jnp.bfloat16)
        partial_sum = lax.optimization_barrier(partial_sum)
        total = total + partial_sum.astype(jnp.float32)
    return (total.astype(jnp.bfloat16), key_value.reshape(TOK_DEV, KV_HEADS * 2 * HEAD_DIM))

def reference(tokens, norm_gain, w_query, q_bias, w_key_value, kv_bias, w_out, prompt_lengths, request_prompt, cache_slot):
    streams = tokens.reshape(N_REQ, TOK_DEV, D)

    def one_stream(inputs):
        return stream_layer(inputs[0], inputs[1], norm_gain, w_query, q_bias, w_key_value, kv_bias, w_out)
    attended, stream_kv = lax.map(one_stream, (streams, prompt_lengths))
    attended = attended.reshape(TOKENS, D)
    kv_width = KV_HEADS * 2 * HEAD_DIM
    padded = jnp.concatenate([stream_kv, jnp.zeros((N_REQ, MAXLEN, kv_width), jnp.bfloat16)], axis=1)
    all_starts = jnp.cumsum(prompt_lengths, axis=1, dtype=jnp.int32) - prompt_lengths
    holders = jnp.arange(REQUESTS, dtype=jnp.int32) // REQ_DEV
    targets = holders * REQ_DEV + cache_slot.reshape(-1).astype(jnp.int32)
    sources = jnp.argsort(targets).astype(jnp.int32)

    def one_slot(request):
        prompt_id = request_prompt[request]
        stream_id = prompt_id // PROMPTS_DEV
        within = prompt_id % PROMPTS_DEV
        start_row = all_starts[stream_id, within].astype(jnp.int32)
        length = prompt_lengths[stream_id, within]
        segment_rows = lax.dynamic_slice_in_dim(padded[stream_id], start_row, MAXLEN, 0)
        live_rows = jnp.arange(MAXLEN, dtype=jnp.int32) < length
        return jnp.where(live_rows[:, None], segment_rows, jnp.zeros_like(segment_rows))
    prompt_cache = lax.map(one_slot, sources)
    return (attended, prompt_cache)
```

```python
import math

import jax
import jax.numpy as jnp
from jax import lax
from jax.experimental import pallas as pl
from jax.experimental.pallas import tpu as pltpu
from jax.sharding import PartitionSpec as P

HEAD_DIM = 128
PROMPTS_DEV = 4
FAN = 12
ALIGN = 16

epsilon = 1e-06
rope_base = 1000000.0


def rotary(values, positions):
    half_dim = HEAD_DIM // 2
    inverse_freq = rope_base ** (-(jnp.arange(half_dim, dtype=jnp.float32) * 2.0 / HEAD_DIM))
    angles = positions.astype(jnp.float32)[:, None] * inverse_freq[None, :]
    cosine = jnp.cos(angles)[:, None, :]
    sine_part = jnp.sin(angles)[:, None, :]
    former = values[..., :half_dim]
    latter = values[..., half_dim:]
    return jnp.concatenate(
        [former * cosine - latter * sine_part, latter * cosine + former * sine_part], axis=-1
    )


def prompt_layout(lengths, row_count):
    prompt_ends = jnp.cumsum(lengths, dtype=jnp.int32)
    starts = prompt_ends - lengths
    places = jnp.arange(row_count, dtype=jnp.int32)
    member = jnp.sum(
        (places[:, None] >= prompt_ends[None, :]).astype(jnp.int32), axis=1, dtype=jnp.int32
    )
    chosen = member[:, None] == jnp.arange(lengths.shape[0], dtype=jnp.int32)[None, :]
    positions = places - jnp.sum(jnp.where(chosen, starts[None, :], 0), axis=1, dtype=jnp.int32)
    padded = (lengths + ALIGN - 1) // ALIGN * ALIGN
    padded_starts = jnp.cumsum(padded, dtype=jnp.int32) - padded
    packed_rows = positions + jnp.sum(
        jnp.where(chosen, padded_starts[None, :], 0), axis=1, dtype=jnp.int32
    )
    return (member, positions, packed_rows)


def attend(queries, keys, values, member):
    row_count = queries.shape[0]
    head_count = queries.shape[1]
    kv_count = keys.shape[1]
    grouped = queries.reshape(row_count, kv_count, head_count // kv_count, HEAD_DIM)
    scores = jnp.einsum(
        "qhgd,khd->hgqk", grouped, keys, preferred_element_type=jnp.float32
    ) / math.sqrt(HEAD_DIM)
    places = jnp.arange(row_count, dtype=jnp.int32)
    allowed = (member[:, None] == member[None, :]) & (places[None, :] <= places[:, None])
    powers = jnp.where(allowed, jnp.exp(scores), 0.0)
    weights = (powers / jnp.sum(powers, axis=-1, keepdims=True)).astype(jnp.bfloat16)
    mixed = jnp.einsum("hgqk,khd->qhgd", weights, values, preferred_element_type=jnp.float32)
    return mixed.reshape(row_count, head_count * HEAD_DIM).astype(jnp.bfloat16)


def place_kernel(packed_rows, lengths_ref, prompts_ref, slots_ref, kv_ref, out_ref, held, staged,
                 in_sem, out_sem):
    requests, slot_rows = staged.shape[0], staged.shape[1]
    source_rows = kv_ref.shape[1]
    load = pltpu.make_async_copy(kv_ref, held.at[:, pl.ds(0, source_rows)], in_sem)
    load.start()
    me = lax.axis_index("req")
    held[:, pl.ds(source_rows, slot_rows)] = jnp.zeros((2, slot_rows, HEAD_DIM), held.dtype)
    load.wait()
    rows = lax.broadcasted_iota(jnp.int32, (slot_rows, HEAD_DIM), 0)

    def one(r, carry):
        prompt = prompts_ref[me * requests + r]
        stream = prompt // PROMPTS_DEV
        within = prompt - stream * PROMPTS_DEV
        start = stream * packed_rows
        for j in range(PROMPTS_DEV - 1):
            padded = (lengths_ref[stream, j] + (ALIGN - 1)) // ALIGN * ALIGN
            start = start + jnp.where(j < within, padded, 0)
        start = pl.multiple_of(start, ALIGN)
        live = rows < lengths_ref[stream, within]
        for part in range(2):
            slab = held[part, pl.ds(start, slot_rows), :]
            staged[r, :, part * HEAD_DIM:(part + 1) * HEAD_DIM] = jnp.where(
                live, slab, jnp.zeros_like(slab)
            )
        pltpu.make_async_copy(staged.at[r], out_ref.at[slots_ref[0, r]], out_sem.at[r]).start()
        return carry

    lax.fori_loop(0, requests, one, 0)

    def done(r, carry):
        pltpu.make_async_copy(staged.at[r], out_ref.at[slots_ref[0, r]], out_sem.at[r]).wait()
        return carry

    lax.fori_loop(0, requests, done, 0)


def place(kv_all, prompt_lengths, request_prompt, cache_slot, slot_rows, packed_rows):
    requests = cache_slot.shape[1]
    smem = pl.BlockSpec(memory_space=pltpu.SMEM)
    source_rows = kv_all.shape[1]
    return pl.pallas_call(
        lambda *refs: place_kernel(packed_rows, *refs),
        out_shape=jax.ShapeDtypeStruct((requests, slot_rows, 2 * HEAD_DIM), jnp.bfloat16),
        in_specs=[smem, smem, smem, pl.BlockSpec(memory_space=pl.ANY)],
        out_specs=pl.BlockSpec(memory_space=pl.ANY),
        scratch_shapes=[
            pltpu.VMEM((2, source_rows + slot_rows, HEAD_DIM), jnp.bfloat16),
            pltpu.VMEM((requests, slot_rows, 2 * HEAD_DIM), jnp.bfloat16),
            pltpu.SemaphoreType.DMA(()),
            pltpu.SemaphoreType.DMA((requests,)),
        ],
        compiler_params=pltpu.CompilerParams(vmem_limit_bytes=24 << 20),
        name="place",
    )(prompt_lengths, request_prompt, cache_slot, kv_all)


def on_device(
    tokens,
    norm_gain,
    w_query,
    q_bias,
    w_key_value,
    kv_bias,
    w_out,
    prompt_lengths,
    request_prompt,
    cache_slot,
):
    row_count = tokens.shape[0]
    slot_rows = row_count // 2
    tp_count = lax.axis_size("tp")
    my_stream = lax.axis_index("req")
    head_count = w_query.shape[1] // HEAD_DIM
    kv_count = w_key_value.shape[1] // (2 * HEAD_DIM)
    my_lengths = lax.dynamic_index_in_dim(prompt_lengths, my_stream, 0, keepdims=False)
    member, positions, packed_rows = prompt_layout(my_lengths, row_count)
    packed_count = row_count + 2 * ALIGN
    widened = tokens.astype(jnp.float32)
    inverse_rms = lax.rsqrt(jnp.mean(widened * widened, axis=1, keepdims=True) + epsilon)
    normed = (widened * inverse_rms * norm_gain.astype(jnp.float32)[None, :]).astype(jnp.bfloat16)
    paired = (
        jnp.dot(normed, w_key_value, preferred_element_type=jnp.float32)
        + kv_bias.astype(jnp.float32)[None, :]
    )
    paired = paired.reshape(row_count, kv_count, 2, HEAD_DIM)
    keys = rotary(paired[:, :, 0], positions).astype(jnp.bfloat16)
    values = paired[:, :, 1].astype(jnp.bfloat16)
    spread = (
        packed_rows[None, :] == jnp.arange(packed_count, dtype=jnp.int32)[:, None]
    ).astype(jnp.bfloat16)
    packed = jnp.dot(
        spread, jnp.concatenate([keys[:, 0], values[:, 0]], axis=1),
        preferred_element_type=jnp.float32,
    ).astype(jnp.bfloat16)
    packed = jnp.stack([packed[:, :HEAD_DIM], packed[:, HEAD_DIM:]], axis=0)
    kv_all = lax.all_gather(packed, "req", axis=1, tiled=True)
    prompt_cache = place(
        kv_all, prompt_lengths, request_prompt, cache_slot, slot_rows, packed_count
    )
    projected = (
        jnp.dot(normed, w_query, preferred_element_type=jnp.float32)
        + q_bias.astype(jnp.float32)[None, :]
    )
    queries = rotary(projected.reshape(row_count, head_count, HEAD_DIM), positions).astype(
        jnp.bfloat16
    )
    context = attend(queries, keys, values, member)
    share = row_count // tp_count
    summed = lax.psum_scatter(
        jnp.dot(context, w_out, preferred_element_type=jnp.float32).astype(jnp.bfloat16),
        "tp",
        scatter_dimension=0,
        tiled=True,
    ).astype(jnp.float32)
    residual_rows = lax.dynamic_slice_in_dim(tokens, lax.axis_index("tp") * share, share, 0)
    attended = (residual_rows.astype(jnp.float32) + summed).astype(jnp.bfloat16)
    return (attended, prompt_cache)


def solution(mesh):
    placed = (
        P("req", None),
        P(),
        P(None, "tp"),
        P("tp"),
        P(None, "tp"),
        P("tp"),
        P("tp", None),
        P(),
        P(),
        P("req", None),
    )
    return jax.shard_map(
        on_device,
        mesh=mesh,
        in_specs=placed,
        out_specs=(P(("req", "tp"), None), P("req", None, "tp")),
        check_vma=False,
    )
```

```python
import math

import jax
import jax.numpy as jnp
import numpy as np
from jax import lax
from jax.experimental import pallas as pl
from jax.experimental.pallas import tpu as pltpu
from jax.sharding import PartitionSpec as P

HEAD_DIM = 128
PROMPTS_DEV = 4
FAN = 12
ALIGN = 16

epsilon = 1e-06
rope_base = 1000000.0

SIDE = 4
TP = 8
ROWS = 512
BLOCK = 128
SHARE = 64
PACKED = ROWS + 2 * ALIGN
HALF = PACKED // 2
KSTEPS = 4
WINDOW = 384
MESH = pl.DeviceIdType.MESH

FIRST = ((-1, 0, 0, PACKED), (1, 0, 0, PACKED), (2, 0, 0, HALF), (2, 0, HALF, HALF))
HELD = (0, -1, 1, 2)
ARRIVALS = FIRST + tuple(
    (a, b, lo, size)
    for a in HELD
    for b, lo, size in ((-1, 0, PACKED), (1, 0, PACKED), (2, 0, HALF), (2, HALF, HALF))
)


def rope_tables(rows):
    half_dim = HEAD_DIM // 2
    inverse_freq = rope_base ** (-(np.arange(half_dim, dtype=np.float64) * 2.0 / HEAD_DIM))
    angles = np.arange(rows, dtype=np.float64)[:, None] * inverse_freq[None, :]
    angles = np.concatenate([angles, angles], axis=1)
    return np.cos(angles).astype(np.float32), np.sin(angles).astype(np.float32)


def layer_kernel(
    lengths_ref, gain_ref, qb_ref, kvb_ref, cos_ref, sin_ref, tokens, w_q, w_kv, w_out,
    kv_out, red_out,
    a_v, wkv_v, wq_v, wo_v, cs_v, scale_v, kvacc_v, kv_v, pk_v, qacc_v, q_v, bias_v, ctx_v,
    part_v, pair_v, sum_v, ring_v,
    tok_sem, wkv_sem, wq_sem, wo_sem, own_sem, gsend, grecv, psend, precv, rsend, rrecv,
):
    req, tp = lax.axis_index("req"), lax.axis_index("tp")
    z, x = lax.div(req, SIDE), lax.rem(req, SIDE)
    y, core = lax.div(tp, 2), lax.rem(tp, 2)
    kc = a_v.shape[2]
    width = SIDE * kc

    def turn(at, by):
        return lax.rem(at + (by + SIDE), SIDE)

    def peer(dz=0, dx=0, dy=0, flip=False):
        there = (1 - core) if flip else core
        return {"req": turn(z, dz) * SIDE + turn(x, dx), "tp": turn(y, dy) * 2 + there}

    barrier = pltpu.get_barrier_semaphore()
    neighbours = [
        peer(dz=1), peer(dz=-1), peer(dx=1), peer(dx=-1), peer(dy=1), peer(dy=-1), peer(flip=True)
    ]
    for there in neighbours:
        pl.semaphore_signal(barrier, inc=1, device_id=there, device_id_type=MESH)

    def tok_copy(i):
        return pltpu.make_async_copy(tokens.at[:, pl.ds(i * kc, kc)], a_v.at[i], tok_sem.at[i])

    def wkv_copy(i):
        return pltpu.make_async_copy(
            w_kv.at[pl.ds(i * kc, kc)], wkv_v.at[pl.ds(i * kc, kc)], wkv_sem.at[i]
        )

    def wq_copy(i):
        return pltpu.make_async_copy(
            w_q.at[pl.ds(i * kc, kc)], wq_v.at[pl.ds(i * kc, kc)], wq_sem.at[i]
        )

    wo_copy = pltpu.make_async_copy(w_out, wo_v, wo_sem)
    for i in range(KSTEPS):
        tok_copy(i).start()
        wkv_copy(i).start()
    for i in range(KSTEPS):
        wq_copy(i).start()
    wo_copy.start()

    lens = [lengths_ref[req, j] for j in range(PROMPTS_DEV)]
    starts = [0]
    for j in range(PROMPTS_DEV - 1):
        starts.append(starts[-1] + lens[j])

    base_cos = [cos_ref[pl.ds(starts[j], 1), :] for j in range(PROMPTS_DEV)]
    base_sin = [sin_ref[pl.ds(starts[j], 1), :] for j in range(PROMPTS_DEV)]

    def by_prompt(row, picks):
        out = picks[0]
        for j in range(1, PROMPTS_DEV):
            out = jnp.where(row >= starts[j], picks[j], out)
        return out

    @pl.loop(0, ROWS // 64)
    def _(i):
        at = pl.ds(i * 64, 64)
        row = lax.broadcasted_iota(jnp.int32, (64, HEAD_DIM), 0) + i * 64
        lane = lax.broadcasted_iota(jnp.int32, (64, HEAD_DIM), 1)
        bc, bs = by_prompt(row, base_cos), by_prompt(row, base_sin)
        ac, asn = cos_ref[at, :], sin_ref[at, :]
        cs_v[0, at, :] = ac * bc + asn * bs
        sine = asn * bc - ac * bs
        cs_v[1, at, :] = jnp.where(lane < HEAD_DIM // 2, -sine, sine)
        scale_v[at, :] = jnp.zeros((64, HEAD_DIM), jnp.float32)
        kvacc_v[at, :] = jnp.zeros((64, 2 * HEAD_DIM), jnp.float32)

    def rope(value, at):
        return value * cs_v[0, at, :] + pltpu.roll(value, HEAD_DIM // 2, 1) * cs_v[1, at, :]

    def kv_step(i, carry):
        tok_copy(i).wait()
        gain = gain_ref[i]

        @pl.loop(0, ROWS // 32)
        def _(j):
            at = pl.ds(j * 32, 32)
            part = a_v[i, at, :]
            wide = part.astype(jnp.float32)
            squares = scale_v[at, :]
            for g in range(kc // HEAD_DIM):
                piece = wide[:, g * HEAD_DIM:(g + 1) * HEAD_DIM]
                squares = squares + piece * piece
            scale_v[at, :] = squares
            a_v[i, at, :] = (wide * gain).astype(jnp.bfloat16)

        wkv_copy(i).wait()
        kvacc_v[...] += jnp.dot(
            a_v[i], wkv_v[pl.ds(i * kc, kc), :], preferred_element_type=jnp.float32
        )
        return carry

    lax.fori_loop(0, KSTEPS, kv_step, 0)

    kvb = kvb_ref[...].astype(jnp.float32)

    @pl.loop(0, ROWS // 64)
    def _(i):
        at = pl.ds(i * 64, 64)
        mean = jnp.sum(scale_v[at, :], axis=1, keepdims=True) / width
        inverse = jnp.broadcast_to(lax.rsqrt(mean + epsilon), (64, HEAD_DIM))
        scale_v[at, :] = inverse
        keys = kvacc_v[at, :HEAD_DIM] * inverse + kvb[:, :HEAD_DIM]
        kv_v[at, :HEAD_DIM] = rope(keys, at).astype(jnp.bfloat16)
        values = kvacc_v[at, HEAD_DIM:] * inverse + kvb[:, HEAD_DIM:]
        kv_v[at, HEAD_DIM:] = values.astype(jnp.bfloat16)

    column = lax.broadcasted_iota(jnp.int32, (1, ROWS), 1)
    target = column
    for j in range(PROMPTS_DEV - 1):
        extra = lax.div(lens[j] + (ALIGN - 1), ALIGN) * ALIGN - lens[j]
        target = target + jnp.where(column >= starts[j + 1], extra, 0)
    for part in range(2):
        line = lax.broadcasted_iota(jnp.int32, (HALF, ROWS), 0) + part * HALF
        spread = jnp.where(line == target, 1.0, 0.0).astype(jnp.bfloat16)
        moved = jnp.dot(spread, kv_v[...], preferred_element_type=jnp.float32)
        for s in range(2):
            pk_v[s, part * HALF:(part + 1) * HALF, :] = moved[
                :, s * HEAD_DIM:(s + 1) * HEAD_DIM
            ].astype(jnp.bfloat16)

    pl.semaphore_wait(barrier, len(neighbours))

    def origin(s, a, b):
        dz, dx = (b, a) if s == 0 else (a, b)
        return turn(z, dz) * SIDE + turn(x, dx)

    def landing(s, a, b, lo, size):
        return kv_out.at[s, origin(s, a, b), pl.ds(lo, size)]

    def gather_copy(s, event, a, b, lo, size, ring, step):
        source = pk_v.at[s, pl.ds(lo, size)] if (a, b) == (0, 0) else landing(s, a, b, lo, size)
        along_x = (ring == 0) == (s == 0)
        there = peer(dx=step) if along_x else peer(dz=step)
        return pltpu.make_async_remote_copy(
            src_ref=source, dst_ref=landing(s, a, b, lo, size),
            send_sem=gsend.at[s, event], recv_sem=grecv.at[s, event],
            device_id=there, device_id_type=MESH,
        )

    def outgoing(s, event):
        ring = 0 if event < 4 else 1
        a, b, lo, size = ARRIVALS[event]
        kind = event % 4
        step = 1 if kind in (0, 2) else -1
        if ring == 0:
            a = a + step if kind < 2 else (-1 if kind == 2 else 1)
        else:
            b = b + step if kind < 2 else (-1 if kind == 2 else 1)
        return gather_copy(s, event, a, b, lo, size, ring, step)

    def gather_send(*events):
        for event in events:
            for s in range(2):
                outgoing(s, event).start()

    def gather_wait(*events):
        for event in events:
            for s in range(2):
                place_at = landing(s, *ARRIVALS[event])
                pltpu.make_async_remote_copy(
                    src_ref=place_at, dst_ref=place_at,
                    send_sem=gsend.at[s, event], recv_sem=grecv.at[s, event],
                    device_id=peer(dx=1), device_id_type=MESH,
                ).wait_recv()

    own_copies = [
        pltpu.make_async_copy(pk_v.at[s], kv_out.at[s, req], own_sem.at[s]) for s in range(2)
    ]
    gather_send(0, 1, 4, 5)
    for copy in own_copies:
        copy.start()

    def q_step(i, carry):
        wq_copy(i).wait()
        product = jnp.dot(
            a_v[i], wq_v[pl.ds(i * kc, kc), :], preferred_element_type=jnp.float32
        )

        @pl.when(i == 0)
        def _():
            qacc_v[...] = product

        @pl.when(i > 0)
        def _():
            qacc_v[...] += product

        return carry

    lax.fori_loop(0, KSTEPS, q_step, 0)
    heads = qacc_v.shape[1] // HEAD_DIM
    qb = qb_ref[...].astype(jnp.float32)

    @pl.loop(0, ROWS // 64)
    def _(i):
        at = pl.ds(i * 64, 64)
        inverse = scale_v[at, :]
        for h in range(heads):
            cols = slice(h * HEAD_DIM, (h + 1) * HEAD_DIM)
            q_v[at, cols] = rope(qacc_v[at, cols] * inverse + qb[:, cols], at).astype(jnp.bfloat16)

    gather_wait(0, 1)
    gather_send(2, 3, 8, 9, 12, 13)

    half_width = part_v.shape[3]
    mine = pl.ds(pl.multiple_of(core * SHARE, SHARE), SHARE)
    other = pl.ds(pl.multiple_of((1 - core) * SHARE, SHARE), SHARE)

    def pair_copy(s):
        return pltpu.make_async_remote_copy(
            src_ref=part_v.at[s, :, other, :], dst_ref=pair_v.at[s],
            send_sem=psend.at[s], recv_sem=precv.at[s],
            device_id=peer(flip=True), device_id_type=MESH,
        )

    def ring_copy(k):
        source, target_ref, dy = (
            (sum_v.at[0, 0], ring_v.at[0], 1),
            (sum_v.at[0, 1], ring_v.at[1], -1),
            (sum_v.at[1, 1], red_out.at[1, 1], 1),
            (sum_v.at[2, 0], red_out.at[2, 0], -1),
            (sum_v.at[1, 0], red_out.at[1, 0], 1),
            (sum_v.at[2, 1], red_out.at[2, 1], -1),
        )[k]
        return pltpu.make_async_remote_copy(
            src_ref=source, dst_ref=target_ref, send_sem=rsend.at[k], recv_sem=rrecv.at[k],
            device_id=peer(dy=dy), device_id_type=MESH,
        )

    def pair_sum(s):
        pair_copy(s).wait_recv()

        @pl.loop(0, SHARE // 16)
        def _(i):
            for h in range(2):
                at = pl.ds(i * 16, 16)
                own = part_v[s, h, pl.ds(pl.multiple_of(core * SHARE + i * 16, 16), 16), :]
                sum_v[s, h, at, :] = own + pair_v[s, h, at, :]

    factor = math.log2(math.e) / math.sqrt(HEAD_DIM)

    def block_step(s, carry):
        chip = turn(y, 2 - s + 3 * lax.div(s, 2) - 2 * lax.div(s, 3))
        q0 = pl.multiple_of(chip * BLOCK, BLOCK)
        k0 = pl.multiple_of(lax.div(chip, 3) * BLOCK, BLOCK)
        row = lax.broadcasted_iota(jnp.int32, (BLOCK, WINDOW), 0) + q0
        col = lax.broadcasted_iota(jnp.int32, (BLOCK, WINDOW), 1) + k0
        begin = by_prompt(row, starts)
        bias_v[...] = jnp.where((col <= row) & (col >= begin), 0.0, -1e30)
        for h in range(heads):
            cols = slice(h * HEAD_DIM, (h + 1) * HEAD_DIM)
            scores = lax.dot_general(
                q_v[pl.ds(q0, BLOCK), cols], kv_v[pl.ds(k0, WINDOW), :HEAD_DIM],
                (((1,), (1,)), ((), ())), preferred_element_type=jnp.float32,
            )
            scores = scores * factor + bias_v[...]
            powers = jnp.exp2(scores - jnp.max(scores, axis=1, keepdims=True))
            total = jnp.sum(powers, axis=1, keepdims=True)
            mixed = jnp.dot(
                powers.astype(jnp.bfloat16), kv_v[pl.ds(k0, WINDOW), HEAD_DIM:],
                preferred_element_type=jnp.float32,
            )
            ctx_v[:, cols] = (mixed / total).astype(jnp.bfloat16)

        @pl.when(s == 0)
        def _():
            wo_copy.wait()

        @pl.when(s == 1)
        def _():
            pair_sum(0)
            ring_copy(0).start()
            ring_copy(1).start()
            gather_wait(4, 5)
            gather_send(6, 7)

        @pl.when(s == 2)
        def _():
            pair_sum(1)
            ring_copy(2).start()
            gather_wait(2, 3)
            gather_send(16, 17)

        @pl.when(s == 3)
        def _():
            pair_sum(2)
            ring_copy(3).start()
            gather_wait(8, 9, 12, 13)
            gather_send(10, 11, 14, 15)

        for h in range(2):
            @pl.loop(0, half_width // 512)
            def _(n):
                at = pl.multiple_of(n * 512, 512)
                part_v[s, h, :, pl.ds(at, 512)] = jnp.dot(
                    ctx_v[...], wo_v[:, pl.ds(h * half_width + at, 512)],
                    preferred_element_type=jnp.float32,
                ).astype(jnp.bfloat16)

        pair_copy(s).start()
        return carry

    lax.fori_loop(0, SIDE, block_step, 0)

    def fold(k, s, h):
        ring_copy(k).wait_recv()

        @pl.loop(0, SHARE // 16)
        def _(i):
            at = pl.ds(i * 16, 16)
            sum_v[s, h, at, :] = sum_v[s, h, at, :] + ring_v[k, at, :]

    fold(0, 1, 0)
    ring_copy(4).start()
    fold(1, 2, 1)
    ring_copy(5).start()
    pair_sum(3)
    final = pltpu.make_async_copy(sum_v.at[3], red_out.at[0], own_sem.at[2])
    final.start()
    gather_wait(16, 17)
    gather_send(18, 19)
    gather_wait(6, 7, 10, 11, 14, 15, 18, 19)
    for k in range(2, 6):
        ring_copy(k).wait_recv()
    final.wait()
    for copy in own_copies:
        copy.wait()
    for event in range(len(ARRIVALS)):
        for s in range(2):
            outgoing(s, event).wait_send()
    for s in range(SIDE):
        pair_copy(s).wait_send()
    for k in range(6):
        ring_copy(k).wait_send()


def layer(tokens, norm_gain, w_query, q_bias, w_key_value, kv_bias, w_out, prompt_lengths):
    rows, width = tokens.shape
    kc = width // KSTEPS
    q_width = w_query.shape[1]
    smem = pl.BlockSpec(memory_space=pltpu.SMEM)
    vmem = pl.BlockSpec(memory_space=pltpu.VMEM)
    hbm = pl.BlockSpec(memory_space=pl.ANY)
    streams = SIDE * SIDE
    cos_table, sin_table = rope_tables(rows)
    bf16, f32 = jnp.bfloat16, jnp.float32
    dma = pltpu.SemaphoreType.DMA
    return pl.pallas_call(
        layer_kernel,
        out_shape=(
            jax.ShapeDtypeStruct((2, streams, PACKED, HEAD_DIM), bf16),
            jax.ShapeDtypeStruct((3, 2, SHARE, width // 2), bf16),
        ),
        in_specs=[smem] + [vmem] * 5 + [hbm] * 4,
        out_specs=(hbm, hbm),
        scratch_shapes=[
            pltpu.VMEM((KSTEPS, rows, kc), bf16),
            pltpu.VMEM((width, 2 * HEAD_DIM), bf16),
            pltpu.VMEM((width, q_width), bf16),
            pltpu.VMEM((q_width, width), bf16),
            pltpu.VMEM((2, rows, HEAD_DIM), f32),
            pltpu.VMEM((rows, HEAD_DIM), f32),
            pltpu.VMEM((rows, 2 * HEAD_DIM), f32),
            pltpu.VMEM((rows, 2 * HEAD_DIM), bf16),
            pltpu.VMEM((2, PACKED, HEAD_DIM), bf16),
            pltpu.VMEM((rows, q_width), f32),
            pltpu.VMEM((rows, q_width), bf16),
            pltpu.VMEM((BLOCK, WINDOW), f32),
            pltpu.VMEM((BLOCK, q_width), bf16),
            pltpu.VMEM((SIDE, 2, BLOCK, width // 2), bf16),
            pltpu.VMEM((SIDE, 2, SHARE, width // 2), bf16),
            pltpu.VMEM((SIDE, 2, SHARE, width // 2), bf16),
            pltpu.VMEM((2, SHARE, width // 2), bf16),
            dma((KSTEPS,)), dma((KSTEPS,)), dma((KSTEPS,)), dma(()), dma((3,)),
            dma((2, len(ARRIVALS))), dma((2, len(ARRIVALS))),
            dma((SIDE,)), dma((SIDE,)), dma((6,)), dma((6,)),
        ],
        compiler_params=pltpu.CompilerParams(
            collective_id=0, has_side_effects=True, vmem_limit_bytes=56 << 20
        ),
        cost_estimate=pl.CostEstimate(
            flops=2 * rows * width * (2 * q_width + 2 * HEAD_DIM), transcendentals=0,
            bytes_accessed=2 * (rows * width + 2 * width * q_width + 2 * width * HEAD_DIM),
        ),
        name="layer",
    )(
        prompt_lengths, norm_gain.reshape(KSTEPS, 1, kc), q_bias.reshape(1, -1),
        kv_bias.reshape(1, -1), jnp.asarray(cos_table), jnp.asarray(sin_table),
        tokens, w_query, w_key_value, w_out,
    )


def place_kernel(lengths_ref, prompts_ref, slots_ref, kv_ref, red_ref, tokens, out_ref, att_ref,
                 held, staged, red_v, tok_v, att_v, in_sem, red_sem, out_sem):
    requests, slot_rows = staged.shape[0], staged.shape[1]
    source_rows = kv_ref.shape[1]
    load = pltpu.make_async_copy(kv_ref, held.at[:, pl.ds(0, source_rows)], in_sem)
    load.start()
    me, tp = lax.axis_index("req"), lax.axis_index("tp")
    red_load = pltpu.make_async_copy(red_ref, red_v, red_sem.at[0])
    red_load.start()
    tok_load = pltpu.make_async_copy(
        tokens.at[pl.ds(pl.multiple_of(tp * SHARE, SHARE), SHARE)], tok_v, red_sem.at[1]
    )
    tok_load.start()
    held[:, pl.ds(source_rows, slot_rows)] = jnp.zeros((2, slot_rows, HEAD_DIM), held.dtype)
    load.wait()
    rows = lax.broadcasted_iota(jnp.int32, (slot_rows, HEAD_DIM), 0)

    def one(r, carry):
        prompt = prompts_ref[me * requests + r]
        stream = lax.div(prompt, PROMPTS_DEV)
        within = prompt - stream * PROMPTS_DEV
        start = stream * PACKED
        for j in range(PROMPTS_DEV - 1):
            padded = lax.div(lengths_ref[stream, j] + (ALIGN - 1), ALIGN) * ALIGN
            start = start + jnp.where(j < within, padded, 0)
        start = pl.multiple_of(start, ALIGN)
        live = rows < lengths_ref[stream, within]
        for part in range(2):
            slab = held[part, pl.ds(start, slot_rows), :]
            staged[r, :, part * HEAD_DIM:(part + 1) * HEAD_DIM] = jnp.where(
                live, slab, jnp.zeros_like(slab)
            )
        pltpu.make_async_copy(staged.at[r], out_ref.at[slots_ref[0, r]], out_sem.at[r]).start()
        return carry

    lax.fori_loop(0, requests, one, 0)
    red_load.wait()
    tok_load.wait()
    half_width = red_v.shape[3]

    @pl.loop(0, SHARE // 16)
    def _(i):
        at = pl.ds(i * 16, 16)
        for h in range(2):
            cols = slice(h * half_width, (h + 1) * half_width)
            total = tok_v[at, cols].astype(jnp.float32)
            for k in range(3):
                total = total + red_v[k, h, at, :].astype(jnp.float32)
            att_v[at, cols] = total.astype(jnp.bfloat16)

    att_store = pltpu.make_async_copy(att_v, att_ref, red_sem.at[2])
    att_store.start()

    def done(r, carry):
        pltpu.make_async_copy(staged.at[r], out_ref.at[slots_ref[0, r]], out_sem.at[r]).wait()
        return carry

    lax.fori_loop(0, requests, done, 0)
    att_store.wait()


def place(kv_all, reduced, tokens, prompt_lengths, request_prompt, cache_slot):
    requests = cache_slot.shape[1]
    slot_rows = ROWS // 2
    width = tokens.shape[1]
    smem = pl.BlockSpec(memory_space=pltpu.SMEM)
    hbm = pl.BlockSpec(memory_space=pl.ANY)
    source_rows = kv_all.shape[1]
    bf16 = jnp.bfloat16
    return pl.pallas_call(
        place_kernel,
        out_shape=(
            jax.ShapeDtypeStruct((requests, slot_rows, 2 * HEAD_DIM), bf16),
            jax.ShapeDtypeStruct((SHARE, width), bf16),
        ),
        in_specs=[smem, smem, smem, hbm, hbm, hbm],
        out_specs=(hbm, hbm),
        scratch_shapes=[
            pltpu.VMEM((2, source_rows + slot_rows, HEAD_DIM), bf16),
            pltpu.VMEM((requests, slot_rows, 2 * HEAD_DIM), bf16),
            pltpu.VMEM((3, 2, SHARE, width // 2), bf16),
            pltpu.VMEM((SHARE, width), bf16),
            pltpu.VMEM((SHARE, width), bf16),
            pltpu.SemaphoreType.DMA(()),
            pltpu.SemaphoreType.DMA((3,)),
            pltpu.SemaphoreType.DMA((requests,)),
        ],
        compiler_params=pltpu.CompilerParams(vmem_limit_bytes=56 << 20),
        name="place",
    )(prompt_lengths, request_prompt, cache_slot, kv_all, reduced, tokens)


def on_device(
    tokens, norm_gain, w_query, q_bias, w_key_value, kv_bias, w_out, prompt_lengths,
    request_prompt, cache_slot,
):
    kv_all, reduced = layer(
        tokens, norm_gain, w_query, q_bias, w_key_value, kv_bias, w_out, prompt_lengths
    )
    kv_all = kv_all.reshape(2, SIDE * SIDE * PACKED, HEAD_DIM)
    prompt_cache, attended = place(
        kv_all, reduced, tokens, prompt_lengths, request_prompt, cache_slot
    )
    return (attended, prompt_cache)


def solution(mesh):
    placed = (
        P("req", None),
        P(),
        P(None, "tp"),
        P("tp"),
        P(None, "tp"),
        P("tp"),
        P("tp", None),
        P(),
        P(),
        P("req", None),
    )
    return jax.shard_map(
        on_device,
        mesh=mesh,
        in_specs=placed,
        out_specs=(P(("req", "tp"), None), P("req", None, "tp")),
        check_vma=False,
    )
```

```python
import math

import jax
import jax.numpy as jnp
import numpy as np
from jax import lax
from jax.experimental import pallas as pl
from jax.experimental.pallas import tpu as pltpu
from jax.sharding import PartitionSpec as P

HEAD_DIM = 128
PROMPTS_DEV = 4
FAN = 12
ALIGN = 16

epsilon = 1e-06
rope_base = 1000000.0

SIDE = 4
TP = 8
ROWS = 512
BLOCK = 128
SHARE = 64
PACKED = ROWS + 2 * ALIGN
SPLIT = PACKED // 2
CUT = 144
KSTEPS = 4
CHUNKS = 5
WINDOW = 384
MESH = pl.DeviceIdType.MESH

FIRST = ((-1, 0, 0, SPLIT), (1, 0, 0, SPLIT), (2, 0, 0, CUT), (2, 0, CUT, SPLIT - CUT))
HELD = (0, -1, 1, 2)
ARRIVALS = FIRST + tuple(
    (a, b, lo, size)
    for a in HELD
    for b, lo, size in ((-1, 0, SPLIT), (1, 0, SPLIT), (2, 0, CUT), (2, CUT, SPLIT - CUT))
)


def rope_tables(rows):
    half_dim = HEAD_DIM // 2
    inverse_freq = rope_base ** (-(np.arange(half_dim, dtype=np.float64) * 2.0 / HEAD_DIM))
    angles = np.arange(rows, dtype=np.float64)[:, None] * inverse_freq[None, :]
    angles = np.concatenate([angles, angles], axis=1)
    return np.cos(angles).astype(np.float32), np.sin(angles).astype(np.float32)


def layer_kernel(
    lengths_ref, gain_ref, qb_ref, kvb_ref, cos_ref, sin_ref, tokens, w_q, w_kv, w_out,
    kv_out, red_out,
    a_v, wkv_v, wq_v, wo_v, cs_v, scale_v, kvacc_v, kv_v, pk_v, qacc_v, q_v, bias_v, score_v,
    power_v, norm_v, ctx_v, part_v, pair_v, sum_v, ring_v,
    tok_sem, wkv_sem, wq_sem, wo_sem, own_sem, gsend, grecv, psend, precv, rsend, rrecv,
):
    req, tp = lax.axis_index("req"), lax.axis_index("tp")
    z, x = lax.div(req, SIDE), lax.rem(req, SIDE)
    y, core = lax.div(tp, 2), lax.rem(tp, 2)
    kc = a_v.shape[2]
    width = SIDE * kc

    def turn(at, by):
        return lax.rem(at + (by + SIDE), SIDE)

    def peer(dz=0, dx=0, dy=0, flip=False):
        there = (1 - core) if flip else core
        return {"req": turn(z, dz) * SIDE + turn(x, dx), "tp": turn(y, dy) * 2 + there}

    barrier = pltpu.get_barrier_semaphore()
    neighbours = [
        peer(dz=1), peer(dz=-1), peer(dx=1), peer(dx=-1), peer(dy=1), peer(dy=-1), peer(flip=True)
    ]
    for there in neighbours:
        pl.semaphore_signal(barrier, inc=1, device_id=there, device_id_type=MESH)

    def tok_copy(i):
        return pltpu.make_async_copy(tokens.at[:, pl.ds(i * kc, kc)], a_v.at[i], tok_sem.at[i])

    def wkv_copy(i):
        return pltpu.make_async_copy(
            w_kv.at[pl.ds(i * kc, kc)], wkv_v.at[pl.ds(i * kc, kc)], wkv_sem.at[i]
        )

    def wq_copy(i):
        return pltpu.make_async_copy(
            w_q.at[pl.ds(i * kc, kc)], wq_v.at[pl.ds(i * kc, kc)], wq_sem.at[i]
        )

    wo_copy = pltpu.make_async_copy(w_out, wo_v, wo_sem)
    for i in range(KSTEPS):
        tok_copy(i).start()
        wkv_copy(i).start()
        wq_copy(i).start()
    wo_copy.start()

    lens = [lengths_ref[j, req] for j in range(PROMPTS_DEV)]
    starts = [0]
    for j in range(PROMPTS_DEV - 1):
        starts.append(starts[-1] + lens[j])

    base_cos = [cos_ref[pl.ds(starts[j], 1), :] for j in range(PROMPTS_DEV)]
    base_sin = [sin_ref[pl.ds(starts[j], 1), :] for j in range(PROMPTS_DEV)]

    def by_prompt(row, picks):
        out = picks[0]
        for j in range(1, PROMPTS_DEV):
            out = jnp.where(row >= starts[j], picks[j], out)
        return out

    @pl.loop(0, ROWS // 64)
    def _(i):
        at = pl.ds(i * 64, 64)
        row = lax.broadcasted_iota(jnp.int32, (64, HEAD_DIM), 0) + i * 64
        lane = lax.broadcasted_iota(jnp.int32, (64, HEAD_DIM), 1)
        bc, bs = by_prompt(row, base_cos), by_prompt(row, base_sin)
        ac, asn = cos_ref[at, :], sin_ref[at, :]
        cs_v[0, at, :] = ac * bc + asn * bs
        sine = asn * bc - ac * bs
        cs_v[1, at, :] = jnp.where(lane < HEAD_DIM // 2, -sine, sine)
        scale_v[at, :] = jnp.zeros((64, HEAD_DIM), jnp.float32)
        kvacc_v[at, :] = jnp.zeros((64, 2 * HEAD_DIM), jnp.float32)
        qacc_v[at, :] = jnp.zeros((64, qacc_v.shape[1]), jnp.float32)

    def rope(value, at):
        return value * cs_v[0, at, :] + pltpu.roll(value, HEAD_DIM // 2, 1) * cs_v[1, at, :]

    def kv_step(i, carry):
        tok_copy(i).wait()
        gain = gain_ref[pl.ds(i * kc, kc)].reshape(1, kc)

        @pl.loop(0, ROWS // 32)
        def _(j):
            at = pl.ds(j * 32, 32)
            part = a_v[i, at, :]
            wide = part.astype(jnp.float32)
            squares = scale_v[at, :]
            for g in range(kc // HEAD_DIM):
                piece = wide[:, g * HEAD_DIM:(g + 1) * HEAD_DIM]
                squares = squares + piece * piece
            scale_v[at, :] = squares
            a_v[i, at, :] = part * gain

        wkv_copy(i).wait()
        kvacc_v[...] += jnp.dot(
            a_v[i], wkv_v[pl.ds(i * kc, kc), :], preferred_element_type=jnp.float32
        )
        wq_copy(i).wait()
        qacc_v[...] += jnp.dot(
            a_v[i], wq_v[pl.ds(i * kc, kc), :], preferred_element_type=jnp.float32
        )
        return carry

    lax.fori_loop(0, KSTEPS, kv_step, 0)

    kvb = kvb_ref[...].astype(jnp.float32).reshape(1, 2 * HEAD_DIM)

    @pl.loop(0, ROWS // 64)
    def _(i):
        at = pl.ds(i * 64, 64)
        mean = jnp.sum(scale_v[at, :], axis=1, keepdims=True) / width
        inverse = jnp.broadcast_to(lax.rsqrt(mean + epsilon), (64, HEAD_DIM))
        scale_v[at, :] = inverse
        keys = kvacc_v[at, :HEAD_DIM] * inverse + kvb[:, :HEAD_DIM]
        kv_v[at, :HEAD_DIM] = rope(keys, at).astype(jnp.bfloat16)
        values = kvacc_v[at, HEAD_DIM:] * inverse + kvb[:, HEAD_DIM:]
        kv_v[at, HEAD_DIM:] = values.astype(jnp.bfloat16)

    column = lax.broadcasted_iota(jnp.int32, (1, ROWS), 1)
    target = column
    for j in range(PROMPTS_DEV - 1):
        extra = lax.div(lens[j] + (ALIGN - 1), ALIGN) * ALIGN - lens[j]
        target = target + jnp.where(column >= starts[j + 1], extra, 0)
    for part in range(2):
        line = lax.broadcasted_iota(jnp.int32, (SPLIT, ROWS), 0) + part * SPLIT
        spread = jnp.where(line == target, 1.0, 0.0).astype(jnp.bfloat16)
        pk_v[part * SPLIT:(part + 1) * SPLIT, :] = jnp.dot(
            spread, kv_v[...], preferred_element_type=jnp.float32
        ).astype(jnp.bfloat16)

    pl.semaphore_wait(barrier, len(neighbours))

    def origin(s, a, b):
        dz, dx = (b, a) if s == 0 else (a, b)
        return turn(z, dz) * SIDE + turn(x, dx)

    def landing(s, a, b, lo, size):
        row = origin(s, a, b) * PACKED + (s * SPLIT + lo)
        return kv_out.at[pl.ds(pl.multiple_of(row, ALIGN), size)]

    def gather_copy(s, event, a, b, lo, size, ring, step):
        source = pk_v.at[pl.ds(s * SPLIT + lo, size)] if (a, b) == (0, 0) else landing(s, a, b, lo, size)
        along_x = (ring == 0) == (s == 0)
        there = peer(dx=step) if along_x else peer(dz=step)
        return pltpu.make_async_remote_copy(
            src_ref=source, dst_ref=landing(s, a, b, lo, size),
            send_sem=gsend.at[s, event], recv_sem=grecv.at[s, event],
            device_id=there, device_id_type=MESH,
        )

    def outgoing(s, event):
        ring = 0 if event < 4 else 1
        a, b, lo, size = ARRIVALS[event]
        kind = event % 4
        step = 1 if kind in (0, 2) else -1
        if ring == 0:
            a = a + step if kind < 2 else (-1 if kind == 2 else 1)
        else:
            b = b + step if kind < 2 else (-1 if kind == 2 else 1)
        return gather_copy(s, event, a, b, lo, size, ring, step)

    def gather_send(*events):
        for event in events:
            for s in range(2):
                outgoing(s, event).start()

    def gather_wait(*events):
        for event in events:
            for s in range(2):
                place_at = landing(s, *ARRIVALS[event])
                pltpu.make_async_remote_copy(
                    src_ref=place_at, dst_ref=place_at,
                    send_sem=gsend.at[s, event], recv_sem=grecv.at[s, event],
                    device_id=peer(dx=1), device_id_type=MESH,
                ).wait_recv()

    own_row = pl.multiple_of(req * PACKED, ALIGN)
    own_copy = pltpu.make_async_copy(pk_v, kv_out.at[pl.ds(own_row, PACKED)], own_sem.at[0])
    gather_send(0, 1, 4, 5)
    own_copy.start()

    heads = q_v.shape[0]
    qb = qb_ref[...].astype(jnp.float32).reshape(1, heads * HEAD_DIM)
    factor = math.log2(math.e) / math.sqrt(HEAD_DIM)

    @pl.loop(0, ROWS // 64)
    def _(i):
        at = pl.ds(i * 64, 64)
        inverse = scale_v[at, :]
        for h in range(heads):
            cols = slice(h * HEAD_DIM, (h + 1) * HEAD_DIM)
            turned = rope(qacc_v[at, cols] * inverse + qb[:, cols], at)
            q_v[h, at, :] = (turned * factor).astype(jnp.bfloat16)

    def attend_step(b, carry):
        q0 = pl.multiple_of(b * BLOCK, BLOCK)
        k0 = pl.multiple_of(lax.div(b, 3) * BLOCK, BLOCK)
        row = lax.broadcasted_iota(jnp.int32, (BLOCK, WINDOW), 0) + q0
        col = lax.broadcasted_iota(jnp.int32, (BLOCK, WINDOW), 1) + k0
        begin = by_prompt(row, starts)
        bias_v[...] = jnp.where((col <= row) & (col >= begin), 0.0, -1e30)
        stacked = q_v[:, pl.ds(q0, BLOCK), :].reshape(heads * BLOCK, HEAD_DIM)
        score_v[...] = lax.dot_general(
            stacked, kv_v[pl.ds(k0, WINDOW), :HEAD_DIM],
            (((1,), (1,)), ((), ())), preferred_element_type=jnp.float32,
        )
        for h in range(heads):
            at = slice(h * BLOCK, (h + 1) * BLOCK)
            scores = score_v[at, :] + bias_v[...]
            powers = jnp.exp2(scores - jnp.max(scores, axis=1, keepdims=True))
            total = jnp.sum(powers, axis=1, keepdims=True)
            power_v[at, :] = powers.astype(jnp.bfloat16)
            norm_v[at, :] = jnp.broadcast_to(1.0 / total, (BLOCK, HEAD_DIM))
        mixed = jnp.dot(
            power_v[...], kv_v[pl.ds(k0, WINDOW), HEAD_DIM:], preferred_element_type=jnp.float32
        ) * norm_v[...]
        for h in range(heads):
            ctx_v[pl.ds(q0, BLOCK), h * HEAD_DIM:(h + 1) * HEAD_DIM] = mixed[
                h * BLOCK:(h + 1) * BLOCK
            ].astype(jnp.bfloat16)
        return carry

    lax.fori_loop(0, ROWS // BLOCK, attend_step, 0)
    gather_wait(0, 1)
    gather_send(2, 3, 8, 9, 12, 13)

    cols = part_v.shape[5]
    right, left, across = turn(y, 1), turn(y, -1), turn(y, 2)

    def pair_copy(c):
        return pltpu.make_async_remote_copy(
            src_ref=part_v.at[c, :, :, 1 - core], dst_ref=pair_v.at[c],
            send_sem=psend.at[c], recv_sem=precv.at[c],
            device_id=peer(flip=True), device_id_type=MESH,
        )

    def ring_copy(c, k):
        source, landing_ref, dy = (
            (sum_v.at[c, 0, across], ring_v.at[c, 0], 1),
            (sum_v.at[c, 1, across], ring_v.at[c, 1], -1),
            (sum_v.at[c, 1, right], red_out.at[1, c, 1], 1),
            (sum_v.at[c, 0, left], red_out.at[2, c, 0], -1),
            (sum_v.at[c, 0, right], red_out.at[1, c, 0], 1),
            (sum_v.at[c, 1, left], red_out.at[2, c, 1], -1),
        )[k]
        return pltpu.make_async_remote_copy(
            src_ref=source, dst_ref=landing_ref, send_sem=rsend.at[c, k], recv_sem=rrecv.at[c, k],
            device_id=peer(dy=dy), device_id_type=MESH,
        )

    def pair_sum(c):
        pair_copy(c).wait_recv()

        @pl.loop(0, SIDE)
        def _(d):
            for h in range(2):
                sum_v[c, h, d] = part_v[c, h, d, core] + pair_v[c, h, d]

        for k in range(4):
            ring_copy(c, k).start()

    def fold(c):
        for h, chip in ((0, right), (1, left)):
            ring_copy(c, h).wait_recv()
            sum_v[c, h, chip] = sum_v[c, h, chip] + ring_v[c, h]
            ring_copy(c, 4 + h).start()

    wo_copy.wait()

    def out_step(c, carry):
        for h in range(2):
            at = pl.multiple_of((2 * c + h) * cols, cols)
            product = jnp.dot(
                ctx_v[...], wo_v[:, pl.ds(at, cols)], preferred_element_type=jnp.float32
            )
            part_v[c, h] = product.astype(jnp.bfloat16).reshape(SIDE, 2, SHARE, cols)
        pair_copy(c).start()

        @pl.when(c >= 1)
        def _():
            pair_sum(c - 1)

        @pl.when(c == 2)
        def _():
            gather_wait(4, 5)
            gather_send(6, 7)

        @pl.when(c == 4)
        def _():
            gather_wait(2, 3)
            gather_send(16, 17)

        @pl.when(c >= 3)
        def _():
            fold(c - 3)

        return carry

    lax.fori_loop(0, CHUNKS, out_step, 0)
    pair_sum(CHUNKS - 1)
    final = pltpu.make_async_copy(sum_v.at[:, :, y], red_out.at[0], own_sem.at[1])
    final.start()
    fold(CHUNKS - 3)
    gather_wait(8, 9, 12, 13)
    gather_send(10, 11, 14, 15)
    fold(CHUNKS - 2)
    gather_wait(16, 17)
    gather_send(18, 19)
    fold(CHUNKS - 1)
    gather_wait(6, 7, 10, 11, 14, 15, 18, 19)

    def ring_end(c, carry):
        for k in range(2, 6):
            ring_copy(c, k).wait_recv()
        for k in range(6):
            ring_copy(c, k).wait_send()
        pair_copy(c).wait_send()
        return carry

    lax.fori_loop(0, CHUNKS, ring_end, 0)
    final.wait()
    own_copy.wait()
    for event in range(len(ARRIVALS)):
        for s in range(2):
            outgoing(s, event).wait_send()


def layer(tokens, norm_gain, w_query, q_bias, w_key_value, kv_bias, w_out, prompt_lengths):
    rows, width = tokens.shape
    kc = width // KSTEPS
    q_width = w_query.shape[1]
    smem = pl.BlockSpec(memory_space=pltpu.SMEM)
    vmem = pl.BlockSpec(memory_space=pltpu.VMEM)
    hbm = pl.BlockSpec(memory_space=pl.ANY)
    streams = SIDE * SIDE
    heads = q_width // HEAD_DIM
    cols = width // (2 * CHUNKS)
    cos_table, sin_table = rope_tables(rows)
    bf16, f32 = jnp.bfloat16, jnp.float32
    dma = pltpu.SemaphoreType.DMA
    return pl.pallas_call(
        layer_kernel,
        out_shape=(
            jax.ShapeDtypeStruct((streams * PACKED, 2 * HEAD_DIM), bf16),
            jax.ShapeDtypeStruct((3, CHUNKS, 2, SHARE, cols), bf16),
        ),
        in_specs=[smem] + [vmem] * 5 + [hbm] * 4,
        out_specs=(hbm, hbm),
        scratch_shapes=[
            pltpu.VMEM((KSTEPS, rows, kc), bf16),
            pltpu.VMEM((width, 2 * HEAD_DIM), bf16),
            pltpu.VMEM((width, q_width), bf16),
            pltpu.VMEM((q_width, width), bf16),
            pltpu.VMEM((2, rows, HEAD_DIM), f32),
            pltpu.VMEM((rows, HEAD_DIM), f32),
            pltpu.VMEM((rows, 2 * HEAD_DIM), f32),
            pltpu.VMEM((rows, 2 * HEAD_DIM), bf16),
            pltpu.VMEM((PACKED, 2 * HEAD_DIM), bf16),
            pltpu.VMEM((rows, q_width), f32),
            pltpu.VMEM((heads, rows, HEAD_DIM), bf16),
            pltpu.VMEM((BLOCK, WINDOW), f32),
            pltpu.VMEM((heads * BLOCK, WINDOW), f32),
            pltpu.VMEM((heads * BLOCK, WINDOW), bf16),
            pltpu.VMEM((heads * BLOCK, HEAD_DIM), f32),
            pltpu.VMEM((rows, q_width), bf16),
            pltpu.VMEM((CHUNKS, 2, SIDE, 2, SHARE, cols), bf16),
            pltpu.VMEM((CHUNKS, 2, SIDE, SHARE, cols), bf16),
            pltpu.VMEM((CHUNKS, 2, SIDE, SHARE, cols), bf16),
            pltpu.VMEM((CHUNKS, 2, SHARE, cols), bf16),
            dma((KSTEPS,)), dma((KSTEPS,)), dma((KSTEPS,)), dma(()), dma((2,)),
            dma((2, len(ARRIVALS))), dma((2, len(ARRIVALS))),
            dma((CHUNKS,)), dma((CHUNKS,)), dma((CHUNKS, 6)), dma((CHUNKS, 6)),
        ],
        compiler_params=pltpu.CompilerParams(
            collective_id=0, has_side_effects=True, vmem_limit_bytes=56 << 20
        ),
        cost_estimate=pl.CostEstimate(
            flops=2 * rows * width * (2 * q_width + 2 * HEAD_DIM), transcendentals=0,
            bytes_accessed=2 * (rows * width + 2 * width * q_width + 2 * width * HEAD_DIM),
        ),
        name="layer",
    )(
        prompt_lengths.T, norm_gain, q_bias, kv_bias,
        jnp.asarray(cos_table), jnp.asarray(sin_table),
        tokens, w_query, w_key_value, w_out,
    )


def place_kernel(lengths_ref, prompts_ref, slots_ref, kv_ref, red_ref, tokens, out_ref, att_ref,
                 held, zero_v, red_v, tok_v, att_v, in_sem, red_sem, out_sem):
    requests, slot_rows = out_ref.shape[0], out_ref.shape[1]
    load = pltpu.make_async_copy(kv_ref, held, in_sem)
    load.start()
    me, tp = lax.axis_index("req"), lax.axis_index("tp")
    red_load = pltpu.make_async_copy(red_ref, red_v, red_sem.at[0])
    red_load.start()
    tok_load = pltpu.make_async_copy(
        tokens.at[pl.ds(pl.multiple_of(tp * SHARE, SHARE), SHARE)], tok_v, red_sem.at[1]
    )
    tok_load.start()
    zero_v[...] = jnp.zeros(zero_v.shape, zero_v.dtype)
    load.wait()

    def one(r, carry):
        prompt = prompts_ref[me * requests + r]
        stream = lax.div(prompt, PROMPTS_DEV)
        within = prompt - stream * PROMPTS_DEV
        start = stream * PACKED
        for j in range(PROMPTS_DEV - 1):
            padded = lax.div(lengths_ref[j, stream] + (ALIGN - 1), ALIGN) * ALIGN
            start = start + jnp.where(j < within, padded, 0)
        start = pl.multiple_of(start, ALIGN)
        live = lax.div(lengths_ref[within, stream] + (ALIGN - 1), ALIGN) * ALIGN
        live = pl.multiple_of(live, ALIGN)
        rest = pl.multiple_of(slot_rows - live, ALIGN)
        slot = slots_ref[0, r]

        @pl.when(live > 0)
        def _():
            pltpu.make_async_copy(
                held.at[pl.ds(start, live)], out_ref.at[slot, pl.ds(0, live)], out_sem.at[r]
            ).start()

        @pl.when(rest > 0)
        def _():
            pltpu.make_async_copy(
                zero_v.at[pl.ds(0, rest)], out_ref.at[slot, pl.ds(live, rest)], out_sem.at[r]
            ).start()

        return carry

    lax.fori_loop(0, requests, one, 0)
    red_load.wait()
    tok_load.wait()
    cols = red_v.shape[4]

    @pl.loop(0, SHARE // 16)
    def _(i):
        at = pl.ds(i * 16, 16)
        for c in range(CHUNKS):
            for h in range(2):
                place_at = slice((2 * c + h) * cols, (2 * c + h + 1) * cols)
                total = tok_v[at, place_at].astype(jnp.float32)
                for k in range(3):
                    total = total + red_v[k, c, h, at, :].astype(jnp.float32)
                att_v[at, place_at] = total.astype(jnp.bfloat16)

    att_store = pltpu.make_async_copy(att_v, att_ref, red_sem.at[2])
    att_store.start()

    def done(r, carry):
        pltpu.make_async_copy(zero_v, out_ref.at[slots_ref[0, r]], out_sem.at[r]).wait()
        return carry

    lax.fori_loop(0, requests, done, 0)
    att_store.wait()


def place(kv_all, reduced, tokens, prompt_lengths, request_prompt, cache_slot):
    requests = cache_slot.shape[1]
    slot_rows = ROWS // 2
    width = tokens.shape[1]
    smem = pl.BlockSpec(memory_space=pltpu.SMEM)
    hbm = pl.BlockSpec(memory_space=pl.ANY)
    bf16 = jnp.bfloat16
    return pl.pallas_call(
        place_kernel,
        out_shape=(
            jax.ShapeDtypeStruct((requests, slot_rows, 2 * HEAD_DIM), bf16),
            jax.ShapeDtypeStruct((SHARE, width), bf16),
        ),
        in_specs=[smem, smem, smem, hbm, hbm, hbm],
        out_specs=(hbm, hbm),
        scratch_shapes=[
            pltpu.VMEM(kv_all.shape, bf16),
            pltpu.VMEM((slot_rows, 2 * HEAD_DIM), bf16),
            pltpu.VMEM(reduced.shape, bf16),
            pltpu.VMEM((SHARE, width), bf16),
            pltpu.VMEM((SHARE, width), bf16),
            pltpu.SemaphoreType.DMA(()),
            pltpu.SemaphoreType.DMA((3,)),
            pltpu.SemaphoreType.DMA((requests,)),
        ],
        compiler_params=pltpu.CompilerParams(vmem_limit_bytes=56 << 20),
        name="place",
    )(prompt_lengths.T, request_prompt, cache_slot, kv_all, reduced, tokens)


def on_device(
    tokens, norm_gain, w_query, q_bias, w_key_value, kv_bias, w_out, prompt_lengths,
    request_prompt, cache_slot,
):
    kv_all, reduced = layer(
        tokens, norm_gain, w_query, q_bias, w_key_value, kv_bias, w_out, prompt_lengths
    )
    prompt_cache, attended = place(
        kv_all, reduced, tokens, prompt_lengths, request_prompt, cache_slot
    )
    return (attended, prompt_cache)


def solution(mesh):
    placed = (
        P("req", None),
        P(),
        P(None, "tp"),
        P("tp"),
        P(None, "tp"),
        P("tp"),
        P("tp", None),
        P(),
        P(),
        P("req", None),
    )
    return jax.shard_map(
        on_device,
        mesh=mesh,
        in_specs=placed,
        out_specs=(P(("req", "tp"), None), P("req", None, "tp")),
        check_vma=False,
    )
```

```python
import math

import jax
import jax.numpy as jnp
import numpy as np
from jax import lax
from jax.experimental import pallas as pl
from jax.experimental.pallas import tpu as pltpu
from jax.sharding import PartitionSpec as P

HEAD_DIM = 128
PROMPTS_DEV = 4
FAN = 12
ALIGN = 16

epsilon = 1e-06
rope_base = 1000000.0

SIDE = 4
TP = 8
ROWS = 512
BLOCK = 128
SHARE = 64
PACKED = ROWS + 2 * ALIGN
SPLIT = PACKED // 2
CUT = 144
KSTEPS = 4
CHUNKS = 5
WINDOW = 384
MESH = pl.DeviceIdType.MESH

FIRST = ((-1, 0, 0, SPLIT), (1, 0, 0, SPLIT), (2, 0, 0, CUT), (2, 0, CUT, SPLIT - CUT))
HELD = (0, -1, 1, 2)
ARRIVALS = FIRST + tuple(
    (a, b, lo, size)
    for a in HELD
    for b, lo, size in ((-1, 0, SPLIT), (1, 0, SPLIT), (2, 0, CUT), (2, CUT, SPLIT - CUT))
)


def rope_tables(rows):
    half_dim = HEAD_DIM // 2
    inverse_freq = rope_base ** (-(np.arange(half_dim, dtype=np.float64) * 2.0 / HEAD_DIM))
    angles = np.arange(rows, dtype=np.float64)[:, None] * inverse_freq[None, :]
    angles = np.concatenate([angles, angles], axis=1)
    return np.cos(angles).astype(np.float32), np.sin(angles).astype(np.float32)


def layer_kernel(
    lengths_ref, gain_ref, qb_ref, kvb_ref, cos_ref, sin_ref, tokens, w_q, w_kv, w_out,
    kv_out, red_out,
    a_v, wkv_v, wq_v, wo_v, cs_v, scale_v, kvacc_v, kv_v, pk_v, qacc_v, q_v, bias_v, score_v,
    power_v, norm_v, ctx_v, part_v, pair_v, sum_v, ring_v,
    tok_sem, wkv_sem, wq_sem, wo_sem, res_sem, own_sem, gsend, grecv, psend, precv, rsend, rrecv,
):
    req, tp = lax.axis_index("req"), lax.axis_index("tp")
    z, x = lax.div(req, SIDE), lax.rem(req, SIDE)
    y, core = lax.div(tp, 2), lax.rem(tp, 2)
    kc = a_v.shape[2]
    width = SIDE * kc

    def turn(at, by):
        return lax.rem(at + (by + SIDE), SIDE)

    def peer(dz=0, dx=0, dy=0, flip=False):
        there = (1 - core) if flip else core
        return {"req": turn(z, dz) * SIDE + turn(x, dx), "tp": turn(y, dy) * 2 + there}

    barrier = pltpu.get_barrier_semaphore()
    neighbours = [
        peer(dz=1), peer(dz=-1), peer(dx=1), peer(dx=-1), peer(dy=1), peer(dy=-1), peer(flip=True)
    ]
    for there in neighbours:
        pl.semaphore_signal(barrier, inc=1, device_id=there, device_id_type=MESH)

    def tok_copy(i):
        return pltpu.make_async_copy(tokens.at[:, pl.ds(i * kc, kc)], a_v.at[i], tok_sem.at[i])

    def wkv_copy(i):
        return pltpu.make_async_copy(
            w_kv.at[pl.ds(i * kc, kc)], wkv_v.at[pl.ds(i * kc, kc)], wkv_sem.at[i]
        )

    def wq_copy(i):
        return pltpu.make_async_copy(
            w_q.at[pl.ds(i * kc, kc)], wq_v.at[pl.ds(i * kc, kc)], wq_sem.at[i]
        )

    wo_copy = pltpu.make_async_copy(w_out, wo_v, wo_sem)
    for i in range(KSTEPS):
        tok_copy(i).start()
        wkv_copy(i).start()
    for i in range(KSTEPS):
        wq_copy(i).start()
    wo_copy.start()

    cols = part_v.shape[5]
    my_rows = pl.ds(pl.multiple_of(tp * SHARE, SHARE), SHARE)
    rest_copies = [
        pltpu.make_async_copy(
            tokens.at[my_rows, pl.ds(n * cols, cols)], red_out.at[3, n // 2, n % 2], res_sem.at[n]
        )
        for n in range(2 * CHUNKS)
    ]
    for copy in rest_copies:
        copy.start()

    lens = [lengths_ref[j, req] for j in range(PROMPTS_DEV)]
    starts = [0]
    for j in range(PROMPTS_DEV - 1):
        starts.append(starts[-1] + lens[j])

    base_cos = [cos_ref[pl.ds(starts[j], 1), :] for j in range(PROMPTS_DEV)]
    base_sin = [sin_ref[pl.ds(starts[j], 1), :] for j in range(PROMPTS_DEV)]

    def by_prompt(row, picks):
        out = picks[0]
        for j in range(1, PROMPTS_DEV):
            out = jnp.where(row >= starts[j], picks[j], out)
        return out

    @pl.loop(0, ROWS // 64)
    def _(i):
        at = pl.ds(i * 64, 64)
        row = lax.broadcasted_iota(jnp.int32, (64, HEAD_DIM), 0) + i * 64
        lane = lax.broadcasted_iota(jnp.int32, (64, HEAD_DIM), 1)
        bc, bs = by_prompt(row, base_cos), by_prompt(row, base_sin)
        ac, asn = cos_ref[at, :], sin_ref[at, :]
        cs_v[0, at, :] = ac * bc + asn * bs
        sine = asn * bc - ac * bs
        cs_v[1, at, :] = jnp.where(lane < HEAD_DIM // 2, -sine, sine)
        scale_v[at, :] = jnp.zeros((64, HEAD_DIM), jnp.float32)
        kvacc_v[at, :] = jnp.zeros((64, 2 * HEAD_DIM), jnp.float32)

    def rope(value, at):
        return value * cs_v[0, at, :] + pltpu.roll(value, HEAD_DIM // 2, 1) * cs_v[1, at, :]

    def kv_step(i, carry):
        tok_copy(i).wait()
        gain = gain_ref[pl.ds(i * kc, kc)].reshape(1, kc)

        @pl.loop(0, ROWS // 32)
        def _(j):
            at = pl.ds(j * 32, 32)
            part = a_v[i, at, :]
            wide = part.astype(jnp.float32)
            squares = scale_v[at, :]
            for g in range(kc // HEAD_DIM):
                piece = wide[:, g * HEAD_DIM:(g + 1) * HEAD_DIM]
                squares = squares + piece * piece
            scale_v[at, :] = squares
            a_v[i, at, :] = part * gain

        wkv_copy(i).wait()
        kvacc_v[...] += jnp.dot(
            a_v[i], wkv_v[pl.ds(i * kc, kc), :], preferred_element_type=jnp.float32
        )
        return carry

    lax.fori_loop(0, KSTEPS, kv_step, 0)

    kvb = kvb_ref[...].astype(jnp.float32).reshape(1, 2 * HEAD_DIM)

    @pl.loop(0, ROWS // 64)
    def _(i):
        at = pl.ds(i * 64, 64)
        mean = jnp.sum(scale_v[at, :], axis=1, keepdims=True) / width
        inverse = jnp.broadcast_to(lax.rsqrt(mean + epsilon), (64, HEAD_DIM))
        scale_v[at, :] = inverse
        keys = kvacc_v[at, :HEAD_DIM] * inverse + kvb[:, :HEAD_DIM]
        kv_v[at, :HEAD_DIM] = rope(keys, at).astype(jnp.bfloat16)
        values = kvacc_v[at, HEAD_DIM:] * inverse + kvb[:, HEAD_DIM:]
        kv_v[at, HEAD_DIM:] = values.astype(jnp.bfloat16)

    column = lax.broadcasted_iota(jnp.int32, (1, ROWS), 1)
    target = column
    for j in range(PROMPTS_DEV - 1):
        extra = lax.div(lens[j] + (ALIGN - 1), ALIGN) * ALIGN - lens[j]
        target = target + jnp.where(column >= starts[j + 1], extra, 0)
    for part in range(2):
        line = lax.broadcasted_iota(jnp.int32, (SPLIT, ROWS), 0) + part * SPLIT
        spread = jnp.where(line == target, 1.0, 0.0).astype(jnp.bfloat16)
        pk_v[part * SPLIT:(part + 1) * SPLIT, :] = jnp.dot(
            spread, kv_v[...], preferred_element_type=jnp.float32
        ).astype(jnp.bfloat16)

    pl.semaphore_wait(barrier, len(neighbours))

    def origin(s, a, b):
        dz, dx = (b, a) if s == 0 else (a, b)
        return turn(z, dz) * SIDE + turn(x, dx)

    def landing(s, a, b, lo, size):
        row = origin(s, a, b) * PACKED + (s * SPLIT + lo)
        return kv_out.at[pl.ds(pl.multiple_of(row, ALIGN), size)]

    def gather_copy(s, event, a, b, lo, size, ring, step):
        source = pk_v.at[pl.ds(s * SPLIT + lo, size)] if (a, b) == (0, 0) else landing(s, a, b, lo, size)
        along_x = (ring == 0) == (s == 0)
        there = peer(dx=step) if along_x else peer(dz=step)
        return pltpu.make_async_remote_copy(
            src_ref=source, dst_ref=landing(s, a, b, lo, size),
            send_sem=gsend.at[s, event], recv_sem=grecv.at[s, event],
            device_id=there, device_id_type=MESH,
        )

    def outgoing(s, event):
        ring = 0 if event < 4 else 1
        a, b, lo, size = ARRIVALS[event]
        kind = event % 4
        step = 1 if kind in (0, 2) else -1
        if ring == 0:
            a = a + step if kind < 2 else (-1 if kind == 2 else 1)
        else:
            b = b + step if kind < 2 else (-1 if kind == 2 else 1)
        return gather_copy(s, event, a, b, lo, size, ring, step)

    def gather_send(*events):
        for event in events:
            for s in range(2):
                outgoing(s, event).start()

    def gather_wait(*events):
        for event in events:
            for s in range(2):
                place_at = landing(s, *ARRIVALS[event])
                pltpu.make_async_remote_copy(
                    src_ref=place_at, dst_ref=place_at,
                    send_sem=gsend.at[s, event], recv_sem=grecv.at[s, event],
                    device_id=peer(dx=1), device_id_type=MESH,
                ).wait_recv()

    own_row = pl.multiple_of(req * PACKED, ALIGN)
    own_copy = pltpu.make_async_copy(pk_v, kv_out.at[pl.ds(own_row, PACKED)], own_sem.at[0])
    gather_send(0, 1, 4, 5)
    own_copy.start()

    def q_step(i, carry):
        wq_copy(i).wait()
        product = jnp.dot(
            a_v[i], wq_v[pl.ds(i * kc, kc), :], preferred_element_type=jnp.float32
        )

        @pl.when(i == 0)
        def _():
            qacc_v[...] = product

        @pl.when(i > 0)
        def _():
            qacc_v[...] += product

        return carry

    lax.fori_loop(0, KSTEPS, q_step, 0)
    heads = q_v.shape[0]
    qb = qb_ref[...].astype(jnp.float32).reshape(1, heads * HEAD_DIM)
    factor = math.log2(math.e) / math.sqrt(HEAD_DIM)

    @pl.loop(0, ROWS // 64)
    def _(i):
        at = pl.ds(i * 64, 64)
        inverse = scale_v[at, :]
        for h in range(heads):
            cols = slice(h * HEAD_DIM, (h + 1) * HEAD_DIM)
            turned = rope(qacc_v[at, cols] * inverse + qb[:, cols], at)
            q_v[h, at, :] = (turned * factor).astype(jnp.bfloat16)

    def attend_step(b, carry):
        q0 = pl.multiple_of(b * BLOCK, BLOCK)
        k0 = pl.multiple_of(lax.div(b, 3) * BLOCK, BLOCK)
        row = lax.broadcasted_iota(jnp.int32, (BLOCK, WINDOW), 0) + q0
        col = lax.broadcasted_iota(jnp.int32, (BLOCK, WINDOW), 1) + k0
        begin = by_prompt(row, starts)
        bias_v[...] = jnp.where((col <= row) & (col >= begin), 0.0, -1e30)
        stacked = q_v[:, pl.ds(q0, BLOCK), :].reshape(heads * BLOCK, HEAD_DIM)
        score_v[...] = lax.dot_general(
            stacked, kv_v[pl.ds(k0, WINDOW), :HEAD_DIM],
            (((1,), (1,)), ((), ())), preferred_element_type=jnp.float32,
        )
        for h in range(heads):
            at = slice(h * BLOCK, (h + 1) * BLOCK)
            scores = score_v[at, :] + bias_v[...]
            powers = jnp.exp2(scores - jnp.max(scores, axis=1, keepdims=True))
            total = jnp.sum(powers, axis=1, keepdims=True)
            power_v[at, :] = powers.astype(jnp.bfloat16)
            norm_v[at, :] = jnp.broadcast_to(1.0 / total, (BLOCK, HEAD_DIM))
        mixed = jnp.dot(
            power_v[...], kv_v[pl.ds(k0, WINDOW), HEAD_DIM:], preferred_element_type=jnp.float32
        ) * norm_v[...]
        for h in range(heads):
            ctx_v[pl.ds(q0, BLOCK), h * HEAD_DIM:(h + 1) * HEAD_DIM] = mixed[
                h * BLOCK:(h + 1) * BLOCK
            ].astype(jnp.bfloat16)
        return carry

    lax.fori_loop(0, ROWS // BLOCK, attend_step, 0)
    gather_wait(0, 1)
    gather_send(2, 3, 8, 9, 12, 13)

    right, left, across = turn(y, 1), turn(y, -1), turn(y, 2)

    def pair_copy(c):
        return pltpu.make_async_remote_copy(
            src_ref=part_v.at[c, :, :, 1 - core], dst_ref=pair_v.at[c],
            send_sem=psend.at[c], recv_sem=precv.at[c],
            device_id=peer(flip=True), device_id_type=MESH,
        )

    def ring_copy(c, k):
        source, landing_ref, dy = (
            (sum_v.at[c, 0, across], ring_v.at[c, 0], 1),
            (sum_v.at[c, 1, across], ring_v.at[c, 1], -1),
            (sum_v.at[c, 1, right], red_out.at[1, c, 1], 1),
            (sum_v.at[c, 0, left], red_out.at[2, c, 0], -1),
            (sum_v.at[c, 0, right], red_out.at[1, c, 0], 1),
            (sum_v.at[c, 1, left], red_out.at[2, c, 1], -1),
        )[k]
        return pltpu.make_async_remote_copy(
            src_ref=source, dst_ref=landing_ref, send_sem=rsend.at[c, k], recv_sem=rrecv.at[c, k],
            device_id=peer(dy=dy), device_id_type=MESH,
        )

    def pair_sum(c):
        pair_copy(c).wait_recv()

        @pl.loop(0, SIDE)
        def _(d):
            for h in range(2):
                sum_v[c, h, d] = part_v[c, h, d, core] + pair_v[c, h, d]

        for k in range(4):
            ring_copy(c, k).start()

    def fold(c):
        for h, chip in ((0, right), (1, left)):
            ring_copy(c, h).wait_recv()
            sum_v[c, h, chip] = sum_v[c, h, chip] + ring_v[c, h]
            ring_copy(c, 4 + h).start()

    wo_copy.wait()

    def out_step(c, carry):
        for h in range(2):
            at = pl.multiple_of((2 * c + h) * cols, cols)
            product = jnp.dot(
                ctx_v[...], wo_v[:, pl.ds(at, cols)], preferred_element_type=jnp.float32
            )
            part_v[c, h] = product.astype(jnp.bfloat16).reshape(SIDE, 2, SHARE, cols)
        pair_copy(c).start()

        @pl.when(c >= 1)
        def _():
            pair_sum(c - 1)

        @pl.when(c == 2)
        def _():
            gather_wait(4, 5)
            gather_send(6, 7)

        @pl.when(c == 4)
        def _():
            gather_wait(2, 3)
            gather_send(16, 17)

        @pl.when(c >= 3)
        def _():
            fold(c - 3)

        return carry

    lax.fori_loop(0, CHUNKS, out_step, 0)
    pair_sum(CHUNKS - 1)
    final = pltpu.make_async_copy(sum_v.at[:, :, y], red_out.at[0], own_sem.at[1])
    final.start()
    fold(CHUNKS - 3)
    gather_wait(8, 9, 12, 13)
    gather_send(10, 11, 14, 15)
    fold(CHUNKS - 2)
    gather_wait(16, 17)
    gather_send(18, 19)
    fold(CHUNKS - 1)
    gather_wait(6, 7, 10, 11, 14, 15, 18, 19)

    def ring_end(c, carry):
        for k in range(2, 6):
            ring_copy(c, k).wait_recv()
        for k in range(6):
            ring_copy(c, k).wait_send()
        pair_copy(c).wait_send()
        return carry

    lax.fori_loop(0, CHUNKS, ring_end, 0)
    final.wait()
    own_copy.wait()
    for copy in rest_copies:
        copy.wait()
    for event in range(len(ARRIVALS)):
        for s in range(2):
            outgoing(s, event).wait_send()


def layer(tokens, norm_gain, w_query, q_bias, w_key_value, kv_bias, w_out, prompt_lengths):
    rows, width = tokens.shape
    kc = width // KSTEPS
    q_width = w_query.shape[1]
    smem = pl.BlockSpec(memory_space=pltpu.SMEM)
    vmem = pl.BlockSpec(memory_space=pltpu.VMEM)
    hbm = pl.BlockSpec(memory_space=pl.ANY)
    streams = SIDE * SIDE
    heads = q_width // HEAD_DIM
    cols = width // (2 * CHUNKS)
    cos_table, sin_table = rope_tables(rows)
    bf16, f32 = jnp.bfloat16, jnp.float32
    dma = pltpu.SemaphoreType.DMA
    return pl.pallas_call(
        layer_kernel,
        out_shape=(
            pltpu.VMEM((streams * PACKED, 2 * HEAD_DIM), bf16),
            pltpu.VMEM((4, CHUNKS, 2, SHARE, cols), bf16),
        ),
        in_specs=[smem] + [vmem] * 5 + [hbm] * 4,
        out_specs=(hbm, hbm),
        scratch_shapes=[
            pltpu.VMEM((KSTEPS, rows, kc), bf16),
            pltpu.VMEM((width, 2 * HEAD_DIM), bf16),
            pltpu.VMEM((width, q_width), bf16),
            pltpu.VMEM((q_width, width), bf16),
            pltpu.VMEM((2, rows, HEAD_DIM), f32),
            pltpu.VMEM((rows, HEAD_DIM), f32),
            pltpu.VMEM((rows, 2 * HEAD_DIM), f32),
            pltpu.VMEM((rows, 2 * HEAD_DIM), bf16),
            pltpu.VMEM((PACKED, 2 * HEAD_DIM), bf16),
            pltpu.VMEM((rows, q_width), f32),
            pltpu.VMEM((heads, rows, HEAD_DIM), bf16),
            pltpu.VMEM((BLOCK, WINDOW), f32),
            pltpu.VMEM((heads * BLOCK, WINDOW), f32),
            pltpu.VMEM((heads * BLOCK, WINDOW), bf16),
            pltpu.VMEM((heads * BLOCK, HEAD_DIM), f32),
            pltpu.VMEM((rows, q_width), bf16),
            pltpu.VMEM((CHUNKS, 2, SIDE, 2, SHARE, cols), bf16),
            pltpu.VMEM((CHUNKS, 2, SIDE, SHARE, cols), bf16),
            pltpu.VMEM((CHUNKS, 2, SIDE, SHARE, cols), bf16),
            pltpu.VMEM((CHUNKS, 2, SHARE, cols), bf16),
            dma((KSTEPS,)), dma((KSTEPS,)), dma((KSTEPS,)), dma(()), dma((2 * CHUNKS,)), dma((2,)),
            dma((2, len(ARRIVALS))), dma((2, len(ARRIVALS))),
            dma((CHUNKS,)), dma((CHUNKS,)), dma((CHUNKS, 6)), dma((CHUNKS, 6)),
        ],
        compiler_params=pltpu.CompilerParams(
            collective_id=0, has_side_effects=True, vmem_limit_bytes=56 << 20
        ),
        cost_estimate=pl.CostEstimate(
            flops=2 * rows * width * (2 * q_width + 2 * HEAD_DIM), transcendentals=0,
            bytes_accessed=2 * (rows * width + 2 * width * q_width + 2 * width * HEAD_DIM),
        ),
        name="layer",
    )(
        prompt_lengths.T, norm_gain, q_bias, kv_bias,
        jnp.asarray(cos_table), jnp.asarray(sin_table),
        tokens, w_query, w_key_value, w_out,
    )


def place_kernel(lengths_ref, prompts_ref, slots_ref, kv_ref, red_ref, out_ref, att_ref,
                 zero_v, att_v, att_sem, out_sem):
    requests, slot_rows = out_ref.shape[0], out_ref.shape[1]
    me = lax.axis_index("req")
    zero_v[...] = jnp.zeros(zero_v.shape, zero_v.dtype)

    def one(r, carry):
        prompt = prompts_ref[me * requests + r]
        stream = lax.div(prompt, PROMPTS_DEV)
        within = prompt - stream * PROMPTS_DEV
        start = stream * PACKED
        for j in range(PROMPTS_DEV - 1):
            padded = lax.div(lengths_ref[j, stream] + (ALIGN - 1), ALIGN) * ALIGN
            start = start + jnp.where(j < within, padded, 0)
        start = pl.multiple_of(start, ALIGN)
        live = lax.div(lengths_ref[within, stream] + (ALIGN - 1), ALIGN) * ALIGN
        live = pl.multiple_of(live, ALIGN)
        rest = pl.multiple_of(slot_rows - live, ALIGN)
        slot = slots_ref[0, r]

        @pl.when(live > 0)
        def _():
            pltpu.make_async_copy(
                kv_ref.at[pl.ds(start, live)], out_ref.at[slot, pl.ds(0, live)], out_sem.at[r]
            ).start()

        @pl.when(rest > 0)
        def _():
            pltpu.make_async_copy(
                zero_v.at[pl.ds(0, rest)], out_ref.at[slot, pl.ds(live, rest)], out_sem.at[r]
            ).start()

        return carry

    lax.fori_loop(0, requests, one, 0)
    cols = red_ref.shape[4]

    @pl.loop(0, SHARE // 16)
    def _(i):
        at = pl.ds(i * 16, 16)
        for c in range(CHUNKS):
            for h in range(2):
                place_at = slice((2 * c + h) * cols, (2 * c + h + 1) * cols)
                total = red_ref[3, c, h, at, :].astype(jnp.float32)
                for k in range(3):
                    total = total + red_ref[k, c, h, at, :].astype(jnp.float32)
                att_v[at, place_at] = total.astype(jnp.bfloat16)

    att_store = pltpu.make_async_copy(att_v, att_ref, att_sem)
    att_store.start()

    def done(r, carry):
        pltpu.make_async_copy(zero_v, out_ref.at[slots_ref[0, r]], out_sem.at[r]).wait()
        return carry

    lax.fori_loop(0, requests, done, 0)
    att_store.wait()


def place(kv_all, reduced, width, prompt_lengths, request_prompt, cache_slot):
    requests = cache_slot.shape[1]
    vmem = pl.BlockSpec(memory_space=pltpu.VMEM)
    slot_rows = ROWS // 2
    smem = pl.BlockSpec(memory_space=pltpu.SMEM)
    hbm = pl.BlockSpec(memory_space=pl.ANY)
    bf16 = jnp.bfloat16
    return pl.pallas_call(
        place_kernel,
        out_shape=(
            jax.ShapeDtypeStruct((requests, slot_rows, 2 * HEAD_DIM), bf16),
            jax.ShapeDtypeStruct((SHARE, width), bf16),
        ),
        in_specs=[smem, smem, smem, vmem, vmem],
        out_specs=(hbm, hbm),
        scratch_shapes=[
            pltpu.VMEM((slot_rows, 2 * HEAD_DIM), bf16),
            pltpu.VMEM((SHARE, width), bf16),
            pltpu.SemaphoreType.DMA(()),
            pltpu.SemaphoreType.DMA((requests,)),
        ],
        compiler_params=pltpu.CompilerParams(vmem_limit_bytes=16 << 20),
        name="place",
    )(prompt_lengths.T, request_prompt, cache_slot, kv_all, reduced)


def on_device(
    tokens, norm_gain, w_query, q_bias, w_key_value, kv_bias, w_out, prompt_lengths,
    request_prompt, cache_slot,
):
    kv_all, reduced = layer(
        tokens, norm_gain, w_query, q_bias, w_key_value, kv_bias, w_out, prompt_lengths
    )
    prompt_cache, attended = place(
        kv_all, reduced, tokens.shape[1], prompt_lengths, request_prompt, cache_slot
    )
    return (attended, prompt_cache)


def solution(mesh):
    placed = (
        P("req", None),
        P(),
        P(None, "tp"),
        P("tp"),
        P(None, "tp"),
        P("tp"),
        P("tp", None),
        P(),
        P(),
        P("req", None),
    )
    return jax.shard_map(
        on_device,
        mesh=mesh,
        in_specs=placed,
        out_specs=(P(("req", "tp"), None), P("req", None, "tp")),
        check_vma=False,
    )
```

```python
import math

import jax
import jax.numpy as jnp
import numpy as np
from jax import lax
from jax.experimental import pallas as pl
from jax.experimental.pallas import tpu as pltpu
from jax.sharding import PartitionSpec as P

HEAD_DIM = 128
PROMPTS_DEV = 4
FAN = 12
ALIGN = 16

epsilon = 1e-06
rope_base = 1000000.0

SIDE = 4
TP = 8
ROWS = 512
BLOCK = 128
SHARE = 64
PACKED = ROWS + 2 * ALIGN
SPLIT = PACKED // 2
CUT = 144
KSTEPS = 4
CHUNKS = 5
WINDOW = 384
MESH = pl.DeviceIdType.MESH

FIRST = ((-1, 0, 0, SPLIT), (1, 0, 0, SPLIT), (2, 0, 0, CUT), (2, 0, CUT, SPLIT - CUT))
HELD = (0, -1, 1, 2)
ARRIVALS = FIRST + tuple(
    (a, b, lo, size)
    for a in HELD
    for b, lo, size in ((-1, 0, SPLIT), (1, 0, SPLIT), (2, 0, CUT), (2, CUT, SPLIT - CUT))
)


def rope_tables(rows):
    half_dim = HEAD_DIM // 2
    inverse_freq = rope_base ** (-(np.arange(half_dim, dtype=np.float64) * 2.0 / HEAD_DIM))
    angles = np.arange(rows, dtype=np.float64)[:, None] * inverse_freq[None, :]
    angles = np.concatenate([angles, angles], axis=1)
    return np.cos(angles).astype(np.float32), np.sin(angles).astype(np.float32)


def layer_kernel(
    lengths_ref, gain_ref, qb_ref, kvb_ref, cos_ref, sin_ref, tokens, w_q, w_kv, w_out,
    kv_out, red_out,
    a_v, wkv_v, wq_v, wo_v, cs_v, scale_v, kvacc_v, kv_v, pk_v, qacc_v, q_v, bias_v, score_v,
    power_v, norm_v, ctx_v, part_v, pair_v, sum_v, ring_v,
    tok_sem, wkv_sem, wq_sem, wo_sem, res_sem, own_sem, gsend, grecv, psend, precv, rsend, rrecv,
):
    req, tp = lax.axis_index("req"), lax.axis_index("tp")
    z, x = lax.div(req, SIDE), lax.rem(req, SIDE)
    y, core = lax.div(tp, 2), lax.rem(tp, 2)
    kc = a_v.shape[2]
    width = SIDE * kc

    def turn(at, by):
        return lax.rem(at + (by + SIDE), SIDE)

    def peer(dz=0, dx=0, dy=0, flip=False):
        there = (1 - core) if flip else core
        return {"req": turn(z, dz) * SIDE + turn(x, dx), "tp": turn(y, dy) * 2 + there}

    barrier = pltpu.get_barrier_semaphore()
    neighbours = [
        peer(dz=1), peer(dz=-1), peer(dx=1), peer(dx=-1), peer(dy=1), peer(dy=-1), peer(flip=True)
    ]
    for there in neighbours:
        pl.semaphore_signal(barrier, inc=1, device_id=there, device_id_type=MESH)

    def tok_copy(i):
        return pltpu.make_async_copy(tokens.at[:, pl.ds(i * kc, kc)], a_v.at[i], tok_sem.at[i])

    def wkv_copy(i):
        return pltpu.make_async_copy(
            w_kv.at[pl.ds(i * kc, kc)], wkv_v.at[pl.ds(i * kc, kc)], wkv_sem.at[i]
        )

    def wq_copy(i):
        return pltpu.make_async_copy(
            w_q.at[pl.ds(i * kc, kc)], wq_v.at[pl.ds(i * kc, kc)], wq_sem.at[i]
        )

    wo_copy = pltpu.make_async_copy(w_out, wo_v, wo_sem)
    for i in range(KSTEPS):
        tok_copy(i).start()
        wkv_copy(i).start()
    for i in range(KSTEPS):
        wq_copy(i).start()
    wo_copy.start()

    cols = part_v.shape[5]
    my_rows = pl.ds(pl.multiple_of(tp * SHARE, SHARE), SHARE)
    rest_copies = [
        pltpu.make_async_copy(
            tokens.at[my_rows, pl.ds(n * cols, cols)], red_out.at[3, n // 2, n % 2], res_sem.at[n]
        )
        for n in range(2 * CHUNKS)
    ]
    for copy in rest_copies:
        copy.start()

    lens = [lengths_ref[j, req] for j in range(PROMPTS_DEV)]
    starts = [0]
    for j in range(PROMPTS_DEV - 1):
        starts.append(starts[-1] + lens[j])

    base_cos = [cos_ref[pl.ds(starts[j], 1), :] for j in range(PROMPTS_DEV)]
    base_sin = [sin_ref[pl.ds(starts[j], 1), :] for j in range(PROMPTS_DEV)]

    def by_prompt(row, picks):
        out = picks[0]
        for j in range(1, PROMPTS_DEV):
            out = jnp.where(row >= starts[j], picks[j], out)
        return out

    @pl.loop(0, ROWS // 64)
    def _(i):
        at = pl.ds(i * 64, 64)
        row = lax.broadcasted_iota(jnp.int32, (64, HEAD_DIM), 0) + i * 64
        lane = lax.broadcasted_iota(jnp.int32, (64, HEAD_DIM), 1)
        bc, bs = by_prompt(row, base_cos), by_prompt(row, base_sin)
        ac, asn = cos_ref[at, :], sin_ref[at, :]
        cs_v[0, at, :] = ac * bc + asn * bs
        sine = asn * bc - ac * bs
        cs_v[1, at, :] = jnp.where(lane < HEAD_DIM // 2, -sine, sine)
        scale_v[at, :] = jnp.zeros((64, HEAD_DIM), jnp.float32)
        kvacc_v[at, :] = jnp.zeros((64, 2 * HEAD_DIM), jnp.float32)

    def rope(value, at):
        return value * cs_v[0, at, :] + pltpu.roll(value, HEAD_DIM // 2, 1) * cs_v[1, at, :]

    def kv_step(i, carry):
        tok_copy(i).wait()
        gain = gain_ref[pl.ds(i * kc, kc)].reshape(1, kc)

        @pl.loop(0, ROWS // 32)
        def _(j):
            at = pl.ds(j * 32, 32)
            part = a_v[i, at, :]
            wide = part.astype(jnp.float32)
            squares = scale_v[at, :]
            for g in range(kc // HEAD_DIM):
                piece = wide[:, g * HEAD_DIM:(g + 1) * HEAD_DIM]
                squares = squares + piece * piece
            scale_v[at, :] = squares
            a_v[i, at, :] = part * gain

        wkv_copy(i).wait()
        kvacc_v[...] += jnp.dot(
            a_v[i], wkv_v[pl.ds(i * kc, kc), :], preferred_element_type=jnp.float32
        )
        return carry

    lax.fori_loop(0, KSTEPS, kv_step, 0)

    kvb = kvb_ref[...].astype(jnp.float32).reshape(1, 2 * HEAD_DIM)

    @pl.loop(0, ROWS // 64)
    def _(i):
        at = pl.ds(i * 64, 64)
        mean = jnp.sum(scale_v[at, :], axis=1, keepdims=True) / width
        inverse = jnp.broadcast_to(lax.rsqrt(mean + epsilon), (64, HEAD_DIM))
        scale_v[at, :] = inverse
        keys = kvacc_v[at, :HEAD_DIM] * inverse + kvb[:, :HEAD_DIM]
        kv_v[at, :HEAD_DIM] = rope(keys, at).astype(jnp.bfloat16)
        values = kvacc_v[at, HEAD_DIM:] * inverse + kvb[:, HEAD_DIM:]
        kv_v[at, HEAD_DIM:] = values.astype(jnp.bfloat16)

    column = lax.broadcasted_iota(jnp.int32, (1, ROWS), 1)
    target = column
    for j in range(PROMPTS_DEV - 1):
        extra = lax.div(lens[j] + (ALIGN - 1), ALIGN) * ALIGN - lens[j]
        target = target + jnp.where(column >= starts[j + 1], extra, 0)
    for part in range(2):
        line = lax.broadcasted_iota(jnp.int32, (SPLIT, ROWS), 0) + part * SPLIT
        spread = jnp.where(line == target, 1.0, 0.0).astype(jnp.bfloat16)
        pk_v[part * SPLIT:(part + 1) * SPLIT, :] = jnp.dot(
            spread, kv_v[...], preferred_element_type=jnp.float32
        ).astype(jnp.bfloat16)

    pl.semaphore_wait(barrier, len(neighbours))

    def origin(s, a, b):
        dz, dx = (b, a) if s == 0 else (a, b)
        return turn(z, dz) * SIDE + turn(x, dx)

    def landing(s, a, b, lo, size):
        row = origin(s, a, b) * PACKED + (s * SPLIT + lo)
        return kv_out.at[pl.ds(pl.multiple_of(row, ALIGN), size)]

    def gather_copy(s, event, a, b, lo, size, ring, step):
        source = pk_v.at[pl.ds(s * SPLIT + lo, size)] if (a, b) == (0, 0) else landing(s, a, b, lo, size)
        along_x = (ring == 0) == (s == 0)
        there = peer(dx=step) if along_x else peer(dz=step)
        return pltpu.make_async_remote_copy(
            src_ref=source, dst_ref=landing(s, a, b, lo, size),
            send_sem=gsend.at[s, event], recv_sem=grecv.at[s, event],
            device_id=there, device_id_type=MESH,
        )

    def outgoing(s, event):
        ring = 0 if event < 4 else 1
        a, b, lo, size = ARRIVALS[event]
        kind = event % 4
        step = 1 if kind in (0, 2) else -1
        if ring == 0:
            a = a + step if kind < 2 else (-1 if kind == 2 else 1)
        else:
            b = b + step if kind < 2 else (-1 if kind == 2 else 1)
        return gather_copy(s, event, a, b, lo, size, ring, step)

    def gather_send(*events):
        for event in events:
            for s in range(2):
                outgoing(s, event).start()

    def gather_wait(*events):
        for event in events:
            for s in range(2):
                place_at = landing(s, *ARRIVALS[event])
                pltpu.make_async_remote_copy(
                    src_ref=place_at, dst_ref=place_at,
                    send_sem=gsend.at[s, event], recv_sem=grecv.at[s, event],
                    device_id=peer(dx=1), device_id_type=MESH,
                ).wait_recv()

    own_row = pl.multiple_of(req * PACKED, ALIGN)
    own_copy = pltpu.make_async_copy(pk_v, kv_out.at[pl.ds(own_row, PACKED)], own_sem.at[0])
    gather_send(0, 1)
    own_copy.start()

    heads = q_v.shape[0]
    qb = qb_ref[...].astype(jnp.float32).reshape(1, heads * HEAD_DIM)
    factor = math.log2(math.e) / math.sqrt(HEAD_DIM)
    right, left, across = turn(y, 1), turn(y, -1), turn(y, 2)

    def queries(count, chip_of, first):
        def q_step(i, carry):
            if first:
                wq_copy(i).wait()
            held = [
                a_v[i, pl.ds(pl.multiple_of(chip_of(n) * BLOCK, BLOCK), BLOCK), :]
                for n in range(count)
            ]
            product = jnp.dot(
                jnp.concatenate(held, axis=0) if count > 1 else held[0],
                wq_v[pl.ds(i * kc, kc), :], preferred_element_type=jnp.float32,
            )
            at = slice(0, count * BLOCK)

            @pl.when(i == 0)
            def _():
                qacc_v[at, :] = product

            @pl.when(i > 0)
            def _():
                qacc_v[at, :] += product

            return carry

        lax.fori_loop(0, KSTEPS, q_step, 0)

    def attend(count, chip_of):
        def block_step(n, carry):
            chip = chip_of(n)
            q0 = pl.multiple_of(chip * BLOCK, BLOCK)
            k0 = pl.multiple_of(lax.div(chip, 3) * BLOCK, BLOCK)
            for part in range(2):
                from_row = pl.ds(pl.multiple_of(n * BLOCK + part * 64, 64), 64)
                at = pl.ds(pl.multiple_of(q0 + part * 64, 64), 64)
                inverse = scale_v[at, :]
                for h in range(heads):
                    lanes = slice(h * HEAD_DIM, (h + 1) * HEAD_DIM)
                    turned = rope(qacc_v[from_row, lanes] * inverse + qb[:, lanes], at)
                    q_v[h, part * 64:(part + 1) * 64, :] = (turned * factor).astype(jnp.bfloat16)
            row = lax.broadcasted_iota(jnp.int32, (BLOCK, WINDOW), 0) + q0
            col = lax.broadcasted_iota(jnp.int32, (BLOCK, WINDOW), 1) + k0
            begin = by_prompt(row, starts)
            bias_v[...] = jnp.where((col <= row) & (col >= begin), 0.0, -1e30)
            score_v[...] = lax.dot_general(
                q_v[...].reshape(heads * BLOCK, HEAD_DIM), kv_v[pl.ds(k0, WINDOW), :HEAD_DIM],
                (((1,), (1,)), ((), ())), preferred_element_type=jnp.float32,
            )
            for h in range(heads):
                at = slice(h * BLOCK, (h + 1) * BLOCK)
                scores = score_v[at, :] + bias_v[...]
                powers = jnp.exp2(scores - jnp.max(scores, axis=1, keepdims=True))
                total = jnp.sum(powers, axis=1, keepdims=True)
                power_v[at, :] = powers.astype(jnp.bfloat16)
                norm_v[at, :] = jnp.broadcast_to(1.0 / total, (BLOCK, HEAD_DIM))
            mixed = jnp.dot(
                power_v[...], kv_v[pl.ds(k0, WINDOW), HEAD_DIM:],
                preferred_element_type=jnp.float32,
            ) * norm_v[...]
            to_row = pl.ds(pl.multiple_of(n * BLOCK, BLOCK), BLOCK)
            for h in range(heads):
                ctx_v[to_row, h * HEAD_DIM:(h + 1) * HEAD_DIM] = mixed[
                    h * BLOCK:(h + 1) * BLOCK
                ].astype(jnp.bfloat16)
            return carry

        lax.fori_loop(0, count, block_step, 0)

    chips = (across, right, left, y)

    def pair_copy(c, slot):
        return pltpu.make_async_remote_copy(
            src_ref=part_v.at[c, :, chips[slot], 1 - core], dst_ref=pair_v.at[c, :, chips[slot]],
            send_sem=psend.at[c, slot], recv_sem=precv.at[c, slot],
            device_id=peer(flip=True), device_id_type=MESH,
        )

    def project(c, slots):
        for h in range(2):
            at = pl.multiple_of((2 * c + h) * cols, cols)
            product = jnp.dot(
                ctx_v[0:len(slots) * BLOCK, :], wo_v[:, pl.ds(at, cols)],
                preferred_element_type=jnp.float32,
            ).astype(jnp.bfloat16)
            for n, slot in enumerate(slots):
                part_v[c, h, chips[slot]] = product[n * BLOCK:(n + 1) * BLOCK].reshape(
                    2, SHARE, cols
                )
        for slot in slots:
            pair_copy(c, slot).start()

    def pair_sum(c, slot):
        pair_copy(c, slot).wait_recv()
        chip = chips[slot]
        for h in range(2):
            sum_v[c, h, chip] = part_v[c, h, chip, core] + pair_v[c, h, chip]

    def ring_copy(c, k):
        source, landing_ref, dy = (
            (sum_v.at[c, 0, across], ring_v.at[c, 0], 1),
            (sum_v.at[c, 1, across], ring_v.at[c, 1], -1),
            (sum_v.at[c, 1, right], red_out.at[1, c, 1], 1),
            (sum_v.at[c, 0, left], red_out.at[2, c, 0], -1),
            (sum_v.at[c, 0, right], red_out.at[1, c, 0], 1),
            (sum_v.at[c, 1, left], red_out.at[2, c, 1], -1),
        )[k]
        return pltpu.make_async_remote_copy(
            src_ref=source, dst_ref=landing_ref, send_sem=rsend.at[c, k], recv_sem=rrecv.at[c, k],
            device_id=peer(dy=dy), device_id_type=MESH,
        )

    def send_across(c):
        pair_sum(c, 0)
        ring_copy(c, 0).start()
        ring_copy(c, 1).start()

    def send_beside(c):
        for slot in (1, 2):
            pair_sum(c, slot)
            ring_copy(c, 1 + slot).start()
        for h, chip in ((0, right), (1, left)):
            ring_copy(c, h).wait_recv()
            sum_v[c, h, chip] = sum_v[c, h, chip] + ring_v[c, h]
            ring_copy(c, 4 + h).start()

    def across_of(n):
        return across

    def beside_of(n):
        return turn(y, 1 + 2 * n)

    def own_of(n):
        return y

    queries(1, across_of, True)
    attend(1, across_of)
    wo_copy.wait()

    def across_step(c, carry):
        project(c, (0,))

        @pl.when(c >= 1)
        def _():
            send_across(c - 1)

        @pl.when(c == 1)
        def _():
            gather_wait(0, 1)
            gather_send(2, 3, 4, 5)

        return carry

    lax.fori_loop(0, CHUNKS, across_step, 0)
    gather_send(8, 9, 12, 13)
    queries(2, beside_of, False)
    send_across(CHUNKS - 1)
    gather_wait(2, 3)
    gather_send(16, 17)
    attend(2, beside_of)

    def beside_step(c, carry):
        project(c, (1, 2))

        @pl.when(c >= 1)
        def _():
            send_beside(c - 1)

        @pl.when(c == 1)
        def _():
            gather_wait(4, 5)
            gather_send(6, 7)

        @pl.when(c == 3)
        def _():
            gather_wait(8, 9)
            gather_send(10, 11)

        return carry

    lax.fori_loop(0, CHUNKS, beside_step, 0)
    queries(1, own_of, False)
    send_beside(CHUNKS - 1)
    gather_wait(12, 13)
    gather_send(14, 15)
    attend(1, own_of)

    def own_step(c, carry):
        project(c, (3,))

        @pl.when(c >= 1)
        def _():
            pair_sum(c - 1, 3)

        return carry

    lax.fori_loop(0, CHUNKS, own_step, 0)
    pair_sum(CHUNKS - 1, 3)
    final = pltpu.make_async_copy(sum_v.at[:, :, y], red_out.at[0], own_sem.at[1])
    final.start()
    gather_wait(16, 17)
    gather_send(18, 19)
    gather_wait(6, 7, 10, 11, 14, 15, 18, 19)

    def ring_end(c, carry):
        for k in range(2, 6):
            ring_copy(c, k).wait_recv()
        for k in range(6):
            ring_copy(c, k).wait_send()
        for slot in range(len(chips)):
            pair_copy(c, slot).wait_send()
        return carry

    lax.fori_loop(0, CHUNKS, ring_end, 0)
    final.wait()
    own_copy.wait()
    for copy in rest_copies:
        copy.wait()
    for event in range(len(ARRIVALS)):
        for s in range(2):
            outgoing(s, event).wait_send()


def layer(tokens, norm_gain, w_query, q_bias, w_key_value, kv_bias, w_out, prompt_lengths):
    rows, width = tokens.shape
    kc = width // KSTEPS
    q_width = w_query.shape[1]
    smem = pl.BlockSpec(memory_space=pltpu.SMEM)
    vmem = pl.BlockSpec(memory_space=pltpu.VMEM)
    hbm = pl.BlockSpec(memory_space=pl.ANY)
    streams = SIDE * SIDE
    heads = q_width // HEAD_DIM
    cols = width // (2 * CHUNKS)
    cos_table, sin_table = rope_tables(rows)
    bf16, f32 = jnp.bfloat16, jnp.float32
    dma = pltpu.SemaphoreType.DMA
    return pl.pallas_call(
        layer_kernel,
        out_shape=(
            pltpu.VMEM((streams * PACKED, 2 * HEAD_DIM), bf16),
            pltpu.VMEM((4, CHUNKS, 2, SHARE, cols), bf16),
        ),
        in_specs=[smem] + [vmem] * 5 + [hbm] * 4,
        out_specs=(hbm, hbm),
        scratch_shapes=[
            pltpu.VMEM((KSTEPS, rows, kc), bf16),
            pltpu.VMEM((width, 2 * HEAD_DIM), bf16),
            pltpu.VMEM((width, q_width), bf16),
            pltpu.VMEM((q_width, width), bf16),
            pltpu.VMEM((2, rows, HEAD_DIM), f32),
            pltpu.VMEM((rows, HEAD_DIM), f32),
            pltpu.VMEM((rows, 2 * HEAD_DIM), f32),
            pltpu.VMEM((rows, 2 * HEAD_DIM), bf16),
            pltpu.VMEM((PACKED, 2 * HEAD_DIM), bf16),
            pltpu.VMEM((2 * BLOCK, q_width), f32),
            pltpu.VMEM((heads, BLOCK, HEAD_DIM), bf16),
            pltpu.VMEM((BLOCK, WINDOW), f32),
            pltpu.VMEM((heads * BLOCK, WINDOW), f32),
            pltpu.VMEM((heads * BLOCK, WINDOW), bf16),
            pltpu.VMEM((heads * BLOCK, HEAD_DIM), f32),
            pltpu.VMEM((2 * BLOCK, q_width), bf16),
            pltpu.VMEM((CHUNKS, 2, SIDE, 2, SHARE, cols), bf16),
            pltpu.VMEM((CHUNKS, 2, SIDE, SHARE, cols), bf16),
            pltpu.VMEM((CHUNKS, 2, SIDE, SHARE, cols), bf16),
            pltpu.VMEM((CHUNKS, 2, SHARE, cols), bf16),
            dma((KSTEPS,)), dma((KSTEPS,)), dma((KSTEPS,)), dma(()), dma((2 * CHUNKS,)), dma((2,)),
            dma((2, len(ARRIVALS))), dma((2, len(ARRIVALS))),
            dma((CHUNKS, SIDE)), dma((CHUNKS, SIDE)), dma((CHUNKS, 6)), dma((CHUNKS, 6)),
        ],
        compiler_params=pltpu.CompilerParams(
            collective_id=0, has_side_effects=True, vmem_limit_bytes=56 << 20
        ),
        cost_estimate=pl.CostEstimate(
            flops=2 * rows * width * (2 * q_width + 2 * HEAD_DIM), transcendentals=0,
            bytes_accessed=2 * (rows * width + 2 * width * q_width + 2 * width * HEAD_DIM),
        ),
        name="layer",
    )(
        prompt_lengths.T, norm_gain, q_bias, kv_bias,
        jnp.asarray(cos_table), jnp.asarray(sin_table),
        tokens, w_query, w_key_value, w_out,
    )


def place_kernel(lengths_ref, prompts_ref, slots_ref, kv_ref, red_ref, out_ref, att_ref,
                 zero_v, att_v, att_sem, out_sem):
    requests, slot_rows = out_ref.shape[0], out_ref.shape[1]
    me = lax.axis_index("req")
    zero_v[...] = jnp.zeros(zero_v.shape, zero_v.dtype)

    def one(r, carry):
        prompt = prompts_ref[me * requests + r]
        stream = lax.div(prompt, PROMPTS_DEV)
        within = prompt - stream * PROMPTS_DEV
        start = stream * PACKED
        for j in range(PROMPTS_DEV - 1):
            padded = lax.div(lengths_ref[j, stream] + (ALIGN - 1), ALIGN) * ALIGN
            start = start + jnp.where(j < within, padded, 0)
        start = pl.multiple_of(start, ALIGN)
        live = lax.div(lengths_ref[within, stream] + (ALIGN - 1), ALIGN) * ALIGN
        live = pl.multiple_of(live, ALIGN)
        rest = pl.multiple_of(slot_rows - live, ALIGN)
        slot = slots_ref[0, r]

        @pl.when(live > 0)
        def _():
            pltpu.make_async_copy(
                kv_ref.at[pl.ds(start, live)], out_ref.at[slot, pl.ds(0, live)], out_sem.at[r]
            ).start()

        @pl.when(rest > 0)
        def _():
            pltpu.make_async_copy(
                zero_v.at[pl.ds(0, rest)], out_ref.at[slot, pl.ds(live, rest)], out_sem.at[r]
            ).start()

        return carry

    lax.fori_loop(0, requests, one, 0)
    cols = red_ref.shape[4]

    @pl.loop(0, SHARE // 16)
    def _(i):
        at = pl.ds(i * 16, 16)
        for c in range(CHUNKS):
            for h in range(2):
                place_at = slice((2 * c + h) * cols, (2 * c + h + 1) * cols)
                total = red_ref[3, c, h, at, :].astype(jnp.float32)
                for k in range(3):
                    total = total + red_ref[k, c, h, at, :].astype(jnp.float32)
                att_v[at, place_at] = total.astype(jnp.bfloat16)

    att_store = pltpu.make_async_copy(att_v, att_ref, att_sem)
    att_store.start()

    def done(r, carry):
        pltpu.make_async_copy(zero_v, out_ref.at[slots_ref[0, r]], out_sem.at[r]).wait()
        return carry

    lax.fori_loop(0, requests, done, 0)
    att_store.wait()


def place(kv_all, reduced, width, prompt_lengths, request_prompt, cache_slot):
    requests = cache_slot.shape[1]
    vmem = pl.BlockSpec(memory_space=pltpu.VMEM)
    slot_rows = ROWS // 2
    smem = pl.BlockSpec(memory_space=pltpu.SMEM)
    hbm = pl.BlockSpec(memory_space=pl.ANY)
    bf16 = jnp.bfloat16
    return pl.pallas_call(
        place_kernel,
        out_shape=(
            jax.ShapeDtypeStruct((requests, slot_rows, 2 * HEAD_DIM), bf16),
            jax.ShapeDtypeStruct((SHARE, width), bf16),
        ),
        in_specs=[smem, smem, smem, vmem, vmem],
        out_specs=(hbm, hbm),
        scratch_shapes=[
            pltpu.VMEM((slot_rows, 2 * HEAD_DIM), bf16),
            pltpu.VMEM((SHARE, width), bf16),
            pltpu.SemaphoreType.DMA(()),
            pltpu.SemaphoreType.DMA((requests,)),
        ],
        compiler_params=pltpu.CompilerParams(vmem_limit_bytes=16 << 20),
        name="place",
    )(prompt_lengths.T, request_prompt, cache_slot, kv_all, reduced)


def on_device(
    tokens, norm_gain, w_query, q_bias, w_key_value, kv_bias, w_out, prompt_lengths,
    request_prompt, cache_slot,
):
    kv_all, reduced = layer(
        tokens, norm_gain, w_query, q_bias, w_key_value, kv_bias, w_out, prompt_lengths
    )
    prompt_cache, attended = place(
        kv_all, reduced, tokens.shape[1], prompt_lengths, request_prompt, cache_slot
    )
    return (attended, prompt_cache)


def solution(mesh):
    placed = (
        P("req", None),
        P(),
        P(None, "tp"),
        P("tp"),
        P(None, "tp"),
        P("tp"),
        P("tp", None),
        P(),
        P(),
        P("req", None),
    )
    return jax.shard_map(
        on_device,
        mesh=mesh,
        in_specs=placed,
        out_specs=(P(("req", "tp"), None), P("req", None, "tp")),
        check_vma=False,
    )
```

```python
import math

import jax
import jax.numpy as jnp
import numpy as np
from jax import lax
from jax.experimental import pallas as pl
from jax.experimental.pallas import tpu as pltpu
from jax.sharding import PartitionSpec as P

HEAD_DIM = 128
PROMPTS_DEV = 4
FAN = 12
ALIGN = 16

epsilon = 1e-06
rope_base = 1000000.0

SIDE = 4
TP = 8
ROWS = 512
BLOCK = 128
SHARE = 64
PACKED = ROWS + 2 * ALIGN
SPLIT = PACKED // 2
CUT = 144
KSTEPS = 10
CHUNKS = 5
WINDOW = 384
MESH = pl.DeviceIdType.MESH

FIRST = ((-1, 0, 0, SPLIT), (1, 0, 0, SPLIT), (2, 0, 0, CUT), (2, 0, CUT, SPLIT - CUT))
HELD = (0, -1, 1, 2)
ARRIVALS = FIRST + tuple(
    (a, b, lo, size)
    for a in HELD
    for b, lo, size in ((-1, 0, SPLIT), (1, 0, SPLIT), (2, 0, CUT), (2, CUT, SPLIT - CUT))
)


def rope_tables(rows):
    half_dim = HEAD_DIM // 2
    inverse_freq = rope_base ** (-(np.arange(half_dim, dtype=np.float64) * 2.0 / HEAD_DIM))
    angles = np.arange(rows, dtype=np.float64)[:, None] * inverse_freq[None, :]
    angles = np.concatenate([angles, angles], axis=1)
    return np.cos(angles).astype(np.float32), np.sin(angles).astype(np.float32)


def layer_kernel(
    lengths_ref, gain_ref, qb_ref, kvb_ref, cos_ref, sin_ref, tokens, w_q, w_kv, w_out,
    kv_out, red_out,
    a_v, wkv_v, wq_v, wo_v, cs_v, scale_v, kvacc_v, kv_v, pk_v, qacc_v, q_v, bias_v, score_v,
    power_v, norm_v, ctx_v, part_v, pair_v, sum_v, ring_v,
    tok_sem, wkv_sem, wq_sem, wo_sem, res_sem, own_sem, gsend, grecv, psend, precv, rsend, rrecv,
):
    req, tp = lax.axis_index("req"), lax.axis_index("tp")
    z, x = lax.div(req, SIDE), lax.rem(req, SIDE)
    y, core = lax.div(tp, 2), lax.rem(tp, 2)
    kc = a_v.shape[2]
    width = KSTEPS * kc

    def turn(at, by):
        return lax.rem(at + (by + SIDE), SIDE)

    def peer(dz=0, dx=0, dy=0, flip=False):
        there = (1 - core) if flip else core
        return {"req": turn(z, dz) * SIDE + turn(x, dx), "tp": turn(y, dy) * 2 + there}

    barrier = pltpu.get_barrier_semaphore()
    neighbours = [
        peer(dz=1), peer(dz=-1), peer(dx=1), peer(dx=-1), peer(dy=1), peer(dy=-1), peer(flip=True)
    ]
    for there in neighbours:
        pl.semaphore_signal(barrier, inc=1, device_id=there, device_id_type=MESH)

    def tok_copy(i):
        return pltpu.make_async_copy(tokens.at[:, pl.ds(i * kc, kc)], a_v.at[i], tok_sem.at[i])

    def wkv_copy(i):
        return pltpu.make_async_copy(
            w_kv.at[pl.ds(i * kc, kc)], wkv_v.at[pl.ds(i * kc, kc)], wkv_sem.at[i]
        )

    def wq_copy(i):
        return pltpu.make_async_copy(
            w_q.at[pl.ds(i * kc, kc)], wq_v.at[pl.ds(i * kc, kc)], wq_sem.at[i]
        )

    wo_copy = pltpu.make_async_copy(w_out, wo_v, wo_sem)
    for i in range(KSTEPS):
        tok_copy(i).start()
        wkv_copy(i).start()
    for i in range(KSTEPS):
        wq_copy(i).start()
    wo_copy.start()

    cols = part_v.shape[5]
    my_rows = pl.ds(pl.multiple_of(tp * SHARE, SHARE), SHARE)
    rest_copies = [
        pltpu.make_async_copy(
            tokens.at[my_rows, pl.ds(n * cols, cols)], red_out.at[3, n // 2, n % 2], res_sem.at[n]
        )
        for n in range(2 * CHUNKS)
    ]
    for copy in rest_copies:
        copy.start()

    lens = [lengths_ref[j, req] for j in range(PROMPTS_DEV)]
    starts = [0]
    for j in range(PROMPTS_DEV - 1):
        starts.append(starts[-1] + lens[j])

    base_cos = [cos_ref[pl.ds(starts[j], 1), :] for j in range(PROMPTS_DEV)]
    base_sin = [sin_ref[pl.ds(starts[j], 1), :] for j in range(PROMPTS_DEV)]

    def by_prompt(row, picks):
        out = picks[0]
        for j in range(1, PROMPTS_DEV):
            out = jnp.where(row >= starts[j], picks[j], out)
        return out

    @pl.loop(0, ROWS // 64)
    def _(i):
        at = pl.ds(i * 64, 64)
        row = lax.broadcasted_iota(jnp.int32, (64, HEAD_DIM), 0) + i * 64
        lane = lax.broadcasted_iota(jnp.int32, (64, HEAD_DIM), 1)
        bc, bs = by_prompt(row, base_cos), by_prompt(row, base_sin)
        ac, asn = cos_ref[at, :], sin_ref[at, :]
        cs_v[0, at, :] = ac * bc + asn * bs
        sine = asn * bc - ac * bs
        cs_v[1, at, :] = jnp.where(lane < HEAD_DIM // 2, -sine, sine)
        scale_v[at, :] = jnp.zeros((64, HEAD_DIM), jnp.float32)
        kvacc_v[at, :] = jnp.zeros((64, 2 * HEAD_DIM), jnp.float32)

    def rope(value, at):
        return value * cs_v[0, at, :] + pltpu.roll(value, HEAD_DIM // 2, 1) * cs_v[1, at, :]

    def kv_step(i, carry):
        tok_copy(i).wait()
        gain = gain_ref[pl.ds(i * kc, kc)].reshape(1, kc)

        @pl.loop(0, ROWS // 64)
        def _(j):
            at = pl.ds(j * 64, 64)
            part = a_v[i, at, :]
            wide = part.astype(jnp.float32)
            squares = scale_v[at, :]
            for g in range(kc // HEAD_DIM):
                piece = wide[:, g * HEAD_DIM:(g + 1) * HEAD_DIM]
                squares = squares + piece * piece
            scale_v[at, :] = squares
            a_v[i, at, :] = part * gain

        wkv_copy(i).wait()
        kvacc_v[...] += jnp.dot(
            a_v[i], wkv_v[pl.ds(i * kc, kc), :], preferred_element_type=jnp.float32
        )
        return carry

    lax.fori_loop(0, KSTEPS, kv_step, 0)

    kvb = kvb_ref[...].astype(jnp.float32).reshape(1, 2 * HEAD_DIM)

    @pl.loop(0, ROWS // 128)
    def _(i):
        at = pl.ds(i * 128, 128)
        mean = jnp.sum(scale_v[at, :], axis=1, keepdims=True) / width
        inverse = jnp.broadcast_to(lax.rsqrt(mean + epsilon), (128, HEAD_DIM))
        scale_v[at, :] = inverse
        keys = kvacc_v[at, :HEAD_DIM] * inverse + kvb[:, :HEAD_DIM]
        kv_v[at, :HEAD_DIM] = rope(keys, at).astype(jnp.bfloat16)
        values = kvacc_v[at, HEAD_DIM:] * inverse + kvb[:, HEAD_DIM:]
        kv_v[at, HEAD_DIM:] = values.astype(jnp.bfloat16)

    column = lax.broadcasted_iota(jnp.int32, (1, ROWS), 1)
    target = column
    for j in range(PROMPTS_DEV - 1):
        extra = lax.div(lens[j] + (ALIGN - 1), ALIGN) * ALIGN - lens[j]
        target = target + jnp.where(column >= starts[j + 1], extra, 0)
    for part in range(2):
        line = lax.broadcasted_iota(jnp.int32, (SPLIT, ROWS), 0) + part * SPLIT
        spread = jnp.where(line == target, 1.0, 0.0).astype(jnp.bfloat16)
        pk_v[part * SPLIT:(part + 1) * SPLIT, :] = jnp.dot(
            spread, kv_v[...], preferred_element_type=jnp.float32
        ).astype(jnp.bfloat16)

    pl.semaphore_wait(barrier, len(neighbours))

    def origin(s, a, b):
        dz, dx = (b, a) if s == 0 else (a, b)
        return turn(z, dz) * SIDE + turn(x, dx)

    def landing(s, a, b, lo, size):
        row = origin(s, a, b) * PACKED + (s * SPLIT + lo)
        return kv_out.at[pl.ds(pl.multiple_of(row, ALIGN), size)]

    def gather_copy(s, event, a, b, lo, size, ring, step):
        source = pk_v.at[pl.ds(s * SPLIT + lo, size)] if (a, b) == (0, 0) else landing(s, a, b, lo, size)
        along_x = (ring == 0) == (s == 0)
        there = peer(dx=step) if along_x else peer(dz=step)
        return pltpu.make_async_remote_copy(
            src_ref=source, dst_ref=landing(s, a, b, lo, size),
            send_sem=gsend.at[s, event], recv_sem=grecv.at[s, event],
            device_id=there, device_id_type=MESH,
        )

    def outgoing(s, event):
        ring = 0 if event < 4 else 1
        a, b, lo, size = ARRIVALS[event]
        kind = event % 4
        step = 1 if kind in (0, 2) else -1
        if ring == 0:
            a = a + step if kind < 2 else (-1 if kind == 2 else 1)
        else:
            b = b + step if kind < 2 else (-1 if kind == 2 else 1)
        return gather_copy(s, event, a, b, lo, size, ring, step)

    def gather_send(*events):
        for event in events:
            for s in range(2):
                outgoing(s, event).start()

    def gather_wait(*events):
        for event in events:
            for s in range(2):
                place_at = landing(s, *ARRIVALS[event])
                pltpu.make_async_remote_copy(
                    src_ref=place_at, dst_ref=place_at,
                    send_sem=gsend.at[s, event], recv_sem=grecv.at[s, event],
                    device_id=peer(dx=1), device_id_type=MESH,
                ).wait_recv()

    own_row = pl.multiple_of(req * PACKED, ALIGN)
    own_copy = pltpu.make_async_copy(pk_v, kv_out.at[pl.ds(own_row, PACKED)], own_sem.at[0])
    gather_send(0, 1)
    own_copy.start()

    heads = q_v.shape[0]
    qb = qb_ref[...].astype(jnp.float32).reshape(1, heads * HEAD_DIM)
    factor = math.log2(math.e) / math.sqrt(HEAD_DIM)
    right, left, across = turn(y, 1), turn(y, -1), turn(y, 2)

    def queries(count, chip_of, first):
        def q_step(i, carry):
            if first:
                wq_copy(i).wait()
            held = [
                a_v[i, pl.ds(pl.multiple_of(chip_of(n) * BLOCK, BLOCK), BLOCK), :]
                for n in range(count)
            ]
            product = jnp.dot(
                jnp.concatenate(held, axis=0) if count > 1 else held[0],
                wq_v[pl.ds(i * kc, kc), :], preferred_element_type=jnp.float32,
            )
            at = slice(0, count * BLOCK)

            @pl.when(i == 0)
            def _():
                qacc_v[at, :] = product

            @pl.when(i > 0)
            def _():
                qacc_v[at, :] += product

            return carry

        lax.fori_loop(0, KSTEPS, q_step, 0)

    def attend(count, chip_of):
        def block_step(n, carry):
            chip = chip_of(n)
            q0 = pl.multiple_of(chip * BLOCK, BLOCK)
            k0 = pl.multiple_of(lax.div(chip, 3) * BLOCK, BLOCK)
            for part in range(2):
                from_row = pl.ds(pl.multiple_of(n * BLOCK + part * 64, 64), 64)
                at = pl.ds(pl.multiple_of(q0 + part * 64, 64), 64)
                inverse = scale_v[at, :]
                for h in range(heads):
                    lanes = slice(h * HEAD_DIM, (h + 1) * HEAD_DIM)
                    turned = rope(qacc_v[from_row, lanes] * inverse + qb[:, lanes], at)
                    q_v[h, part * 64:(part + 1) * 64, :] = (turned * factor).astype(jnp.bfloat16)
            row = lax.broadcasted_iota(jnp.int32, (BLOCK, WINDOW), 0) + q0
            col = lax.broadcasted_iota(jnp.int32, (BLOCK, WINDOW), 1) + k0
            begin = by_prompt(row, starts)
            bias_v[...] = jnp.where((col <= row) & (col >= begin), 0.0, -1e30)
            score_v[...] = lax.dot_general(
                q_v[...].reshape(heads * BLOCK, HEAD_DIM), kv_v[pl.ds(k0, WINDOW), :HEAD_DIM],
                (((1,), (1,)), ((), ())), preferred_element_type=jnp.float32,
            )
            for h in range(heads):
                at = slice(h * BLOCK, (h + 1) * BLOCK)
                scores = score_v[at, :] + bias_v[...]
                powers = jnp.exp2(scores - jnp.max(scores, axis=1, keepdims=True))
                total = jnp.sum(powers, axis=1, keepdims=True)
                power_v[at, :] = powers.astype(jnp.bfloat16)
                norm_v[at, :] = jnp.broadcast_to(1.0 / total, (BLOCK, HEAD_DIM))
            mixed = jnp.dot(
                power_v[...], kv_v[pl.ds(k0, WINDOW), HEAD_DIM:],
                preferred_element_type=jnp.float32,
            ) * norm_v[...]
            to_row = pl.ds(pl.multiple_of(n * BLOCK, BLOCK), BLOCK)
            for h in range(heads):
                ctx_v[to_row, h * HEAD_DIM:(h + 1) * HEAD_DIM] = mixed[
                    h * BLOCK:(h + 1) * BLOCK
                ].astype(jnp.bfloat16)
            return carry

        lax.fori_loop(0, count, block_step, 0)

    chips = (across, right, left, y)

    def pair_copy(c, slot):
        return pltpu.make_async_remote_copy(
            src_ref=part_v.at[c, :, chips[slot], 1 - core], dst_ref=pair_v.at[c, :, chips[slot]],
            send_sem=psend.at[c, slot], recv_sem=precv.at[c, slot],
            device_id=peer(flip=True), device_id_type=MESH,
        )

    def project(c, slots):
        for h in range(2):
            at = pl.multiple_of((2 * c + h) * cols, cols)
            product = jnp.dot(
                ctx_v[0:len(slots) * BLOCK, :], wo_v[:, pl.ds(at, cols)],
                preferred_element_type=jnp.float32,
            ).astype(jnp.bfloat16)
            for n, slot in enumerate(slots):
                part_v[c, h, chips[slot]] = product[n * BLOCK:(n + 1) * BLOCK].reshape(
                    2, SHARE, cols
                )
        for slot in slots:
            pair_copy(c, slot).start()

    def pair_sum(c, slot):
        pair_copy(c, slot).wait_recv()
        chip = chips[slot]
        for h in range(2):
            sum_v[c, h, chip] = part_v[c, h, chip, core] + pair_v[c, h, chip]

    def ring_copy(c, k):
        source, landing_ref, dy = (
            (sum_v.at[c, 0, across], ring_v.at[c, 0], 1),
            (sum_v.at[c, 1, across], ring_v.at[c, 1], -1),
            (sum_v.at[c, 1, right], red_out.at[1, c, 1], 1),
            (sum_v.at[c, 0, left], red_out.at[2, c, 0], -1),
            (sum_v.at[c, 0, right], red_out.at[1, c, 0], 1),
            (sum_v.at[c, 1, left], red_out.at[2, c, 1], -1),
        )[k]
        return pltpu.make_async_remote_copy(
            src_ref=source, dst_ref=landing_ref, send_sem=rsend.at[c, k], recv_sem=rrecv.at[c, k],
            device_id=peer(dy=dy), device_id_type=MESH,
        )

    def send_across(c):
        pair_sum(c, 0)
        ring_copy(c, 0).start()
        ring_copy(c, 1).start()

    def send_beside(c):
        for slot in (1, 2):
            pair_sum(c, slot)
            ring_copy(c, 1 + slot).start()
        for h, chip in ((0, right), (1, left)):
            ring_copy(c, h).wait_recv()
            sum_v[c, h, chip] = sum_v[c, h, chip] + ring_v[c, h]
            ring_copy(c, 4 + h).start()

    def across_of(n):
        return across

    def beside_of(n):
        return turn(y, 1 + 2 * n)

    def own_of(n):
        return y

    queries(1, across_of, True)
    attend(1, across_of)
    wo_copy.wait()

    def across_step(c, carry):
        project(c, (0,))

        @pl.when(c >= 1)
        def _():
            send_across(c - 1)

        @pl.when(c == 1)
        def _():
            gather_wait(0, 1)
            gather_send(2, 3, 4, 5)

        return carry

    lax.fori_loop(0, CHUNKS, across_step, 0)
    gather_send(8, 9, 12, 13)
    queries(2, beside_of, False)
    send_across(CHUNKS - 1)
    gather_wait(2, 3)
    gather_send(16, 17)
    attend(2, beside_of)

    def beside_step(c, carry):
        project(c, (1, 2))

        @pl.when(c >= 1)
        def _():
            send_beside(c - 1)

        @pl.when(c == 1)
        def _():
            gather_wait(4, 5)
            gather_send(6, 7)

        @pl.when(c == 3)
        def _():
            gather_wait(8, 9)
            gather_send(10, 11)

        return carry

    lax.fori_loop(0, CHUNKS, beside_step, 0)
    queries(1, own_of, False)
    send_beside(CHUNKS - 1)
    gather_wait(12, 13)
    gather_send(14, 15)
    attend(1, own_of)

    def own_step(c, carry):
        project(c, (3,))

        @pl.when(c >= 1)
        def _():
            pair_sum(c - 1, 3)

        return carry

    lax.fori_loop(0, CHUNKS, own_step, 0)
    pair_sum(CHUNKS - 1, 3)
    final = pltpu.make_async_copy(sum_v.at[:, :, y], red_out.at[0], own_sem.at[1])
    final.start()
    gather_wait(16, 17)
    gather_send(18, 19)
    gather_wait(6, 7, 10, 11, 14, 15, 18, 19)

    def ring_end(c, carry):
        for k in range(2, 6):
            ring_copy(c, k).wait_recv()
        for k in range(6):
            ring_copy(c, k).wait_send()
        for slot in range(len(chips)):
            pair_copy(c, slot).wait_send()
        return carry

    lax.fori_loop(0, CHUNKS, ring_end, 0)
    final.wait()
    own_copy.wait()
    for copy in rest_copies:
        copy.wait()
    for event in range(len(ARRIVALS)):
        for s in range(2):
            outgoing(s, event).wait_send()


def layer(tokens, norm_gain, w_query, q_bias, w_key_value, kv_bias, w_out, prompt_lengths):
    rows, width = tokens.shape
    kc = width // KSTEPS
    q_width = w_query.shape[1]
    smem = pl.BlockSpec(memory_space=pltpu.SMEM)
    vmem = pl.BlockSpec(memory_space=pltpu.VMEM)
    hbm = pl.BlockSpec(memory_space=pl.ANY)
    streams = SIDE * SIDE
    heads = q_width // HEAD_DIM
    cols = width // (2 * CHUNKS)
    cos_table, sin_table = rope_tables(rows)
    bf16, f32 = jnp.bfloat16, jnp.float32
    dma = pltpu.SemaphoreType.DMA
    return pl.pallas_call(
        layer_kernel,
        out_shape=(
            pltpu.VMEM((streams * PACKED, 2 * HEAD_DIM), bf16),
            pltpu.VMEM((4, CHUNKS, 2, SHARE, cols), bf16),
        ),
        in_specs=[smem] + [vmem] * 5 + [hbm] * 4,
        out_specs=(hbm, hbm),
        scratch_shapes=[
            pltpu.VMEM((KSTEPS, rows, kc), bf16),
            pltpu.VMEM((width, 2 * HEAD_DIM), bf16),
            pltpu.VMEM((width, q_width), bf16),
            pltpu.VMEM((q_width, width), bf16),
            pltpu.VMEM((2, rows, HEAD_DIM), f32),
            pltpu.VMEM((rows, HEAD_DIM), f32),
            pltpu.VMEM((rows, 2 * HEAD_DIM), f32),
            pltpu.VMEM((rows, 2 * HEAD_DIM), bf16),
            pltpu.VMEM((PACKED, 2 * HEAD_DIM), bf16),
            pltpu.VMEM((2 * BLOCK, q_width), f32),
            pltpu.VMEM((heads, BLOCK, HEAD_DIM), bf16),
            pltpu.VMEM((BLOCK, WINDOW), f32),
            pltpu.VMEM((heads * BLOCK, WINDOW), f32),
            pltpu.VMEM((heads * BLOCK, WINDOW), bf16),
            pltpu.VMEM((heads * BLOCK, HEAD_DIM), f32),
            pltpu.VMEM((2 * BLOCK, q_width), bf16),
            pltpu.VMEM((CHUNKS, 2, SIDE, 2, SHARE, cols), bf16),
            pltpu.VMEM((CHUNKS, 2, SIDE, SHARE, cols), bf16),
            pltpu.VMEM((CHUNKS, 2, SIDE, SHARE, cols), bf16),
            pltpu.VMEM((CHUNKS, 2, SHARE, cols), bf16),
            dma((KSTEPS,)), dma((KSTEPS,)), dma((KSTEPS,)), dma(()), dma((2 * CHUNKS,)), dma((2,)),
            dma((2, len(ARRIVALS))), dma((2, len(ARRIVALS))),
            dma((CHUNKS, SIDE)), dma((CHUNKS, SIDE)), dma((CHUNKS, 6)), dma((CHUNKS, 6)),
        ],
        compiler_params=pltpu.CompilerParams(
            collective_id=0, has_side_effects=True, vmem_limit_bytes=56 << 20
        ),
        cost_estimate=pl.CostEstimate(
            flops=2 * rows * width * (2 * q_width + 2 * HEAD_DIM), transcendentals=0,
            bytes_accessed=2 * (rows * width + 2 * width * q_width + 2 * width * HEAD_DIM),
        ),
        name="layer",
    )(
        prompt_lengths.T, norm_gain, q_bias, kv_bias,
        jnp.asarray(cos_table), jnp.asarray(sin_table),
        tokens, w_query, w_key_value, w_out,
    )


def place_kernel(lengths_ref, prompts_ref, slots_ref, kv_ref, red_ref, out_ref, att_ref,
                 zero_v, att_v, att_sem, out_sem):
    requests, slot_rows = out_ref.shape[0], out_ref.shape[1]
    me = lax.axis_index("req")
    zero_v[...] = jnp.zeros(zero_v.shape, zero_v.dtype)

    def one(r, carry):
        prompt = prompts_ref[me * requests + r]
        stream = lax.div(prompt, PROMPTS_DEV)
        within = prompt - stream * PROMPTS_DEV
        start = stream * PACKED
        for j in range(PROMPTS_DEV - 1):
            padded = lax.div(lengths_ref[j, stream] + (ALIGN - 1), ALIGN) * ALIGN
            start = start + jnp.where(j < within, padded, 0)
        start = pl.multiple_of(start, ALIGN)
        live = lax.div(lengths_ref[within, stream] + (ALIGN - 1), ALIGN) * ALIGN
        live = pl.multiple_of(live, ALIGN)
        rest = pl.multiple_of(slot_rows - live, ALIGN)
        slot = slots_ref[0, r]

        @pl.when(live > 0)
        def _():
            pltpu.make_async_copy(
                kv_ref.at[pl.ds(start, live)], out_ref.at[slot, pl.ds(0, live)], out_sem.at[r]
            ).start()

        @pl.when(rest > 0)
        def _():
            pltpu.make_async_copy(
                zero_v.at[pl.ds(0, rest)], out_ref.at[slot, pl.ds(live, rest)], out_sem.at[r]
            ).start()

        return carry

    lax.fori_loop(0, requests, one, 0)
    cols = red_ref.shape[4]

    @pl.loop(0, SHARE // 16)
    def _(i):
        at = pl.ds(i * 16, 16)
        for c in range(CHUNKS):
            for h in range(2):
                place_at = slice((2 * c + h) * cols, (2 * c + h + 1) * cols)
                total = red_ref[3, c, h, at, :].astype(jnp.float32)
                for k in range(3):
                    total = total + red_ref[k, c, h, at, :].astype(jnp.float32)
                att_v[at, place_at] = total.astype(jnp.bfloat16)

    att_store = pltpu.make_async_copy(att_v, att_ref, att_sem)
    att_store.start()

    def done(r, carry):
        pltpu.make_async_copy(zero_v, out_ref.at[slots_ref[0, r]], out_sem.at[r]).wait()
        return carry

    lax.fori_loop(0, requests, done, 0)
    att_store.wait()


def place(kv_all, reduced, width, prompt_lengths, request_prompt, cache_slot):
    requests = cache_slot.shape[1]
    vmem = pl.BlockSpec(memory_space=pltpu.VMEM)
    slot_rows = ROWS // 2
    smem = pl.BlockSpec(memory_space=pltpu.SMEM)
    hbm = pl.BlockSpec(memory_space=pl.ANY)
    bf16 = jnp.bfloat16
    return pl.pallas_call(
        place_kernel,
        out_shape=(
            jax.ShapeDtypeStruct((requests, slot_rows, 2 * HEAD_DIM), bf16),
            jax.ShapeDtypeStruct((SHARE, width), bf16),
        ),
        in_specs=[smem, smem, smem, vmem, vmem],
        out_specs=(hbm, hbm),
        scratch_shapes=[
            pltpu.VMEM((slot_rows, 2 * HEAD_DIM), bf16),
            pltpu.VMEM((SHARE, width), bf16),
            pltpu.SemaphoreType.DMA(()),
            pltpu.SemaphoreType.DMA((requests,)),
        ],
        compiler_params=pltpu.CompilerParams(vmem_limit_bytes=16 << 20),
        name="place",
    )(prompt_lengths.T, request_prompt, cache_slot, kv_all, reduced)


def on_device(
    tokens, norm_gain, w_query, q_bias, w_key_value, kv_bias, w_out, prompt_lengths,
    request_prompt, cache_slot,
):
    kv_all, reduced = layer(
        tokens, norm_gain, w_query, q_bias, w_key_value, kv_bias, w_out, prompt_lengths
    )
    prompt_cache, attended = place(
        kv_all, reduced, tokens.shape[1], prompt_lengths, request_prompt, cache_slot
    )
    return (attended, prompt_cache)


def solution(mesh):
    placed = (
        P("req", None),
        P(),
        P(None, "tp"),
        P("tp"),
        P(None, "tp"),
        P("tp"),
        P("tp", None),
        P(),
        P(),
        P("req", None),
    )
    return jax.shard_map(
        on_device,
        mesh=mesh,
        in_specs=placed,
        out_specs=(P(("req", "tp"), None), P("req", None, "tp")),
        check_vma=False,
    )
```

```python
import math

import jax
import jax.numpy as jnp
import numpy as np
from jax import lax
from jax.experimental import pallas as pl
from jax.experimental.pallas import tpu as pltpu
from jax.sharding import PartitionSpec as P

HEAD_DIM = 128
PROMPTS_DEV = 4
FAN = 12
ALIGN = 16

epsilon = 1e-06
rope_base = 1000000.0

SIDE = 4
TP = 8
ROWS = 512
BLOCK = 128
SHARE = 64
PACKED = ROWS + 2 * ALIGN
SPLIT = PACKED // 2
CUT = 144
KSTEPS = 10
QSTEPS = 2
CHUNKS = 5
WINDOW = 384
MESH = pl.DeviceIdType.MESH

FIRST = ((-1, 0, 0, SPLIT), (1, 0, 0, SPLIT), (2, 0, 0, CUT), (2, 0, CUT, SPLIT - CUT))
HELD = (0, -1, 1, 2)
ARRIVALS = FIRST + tuple(
    (a, b, lo, size)
    for a in HELD
    for b, lo, size in ((-1, 0, SPLIT), (1, 0, SPLIT), (2, 0, CUT), (2, CUT, SPLIT - CUT))
)


def rope_tables(rows):
    half_dim = HEAD_DIM // 2
    inverse_freq = rope_base ** (-(np.arange(half_dim, dtype=np.float64) * 2.0 / HEAD_DIM))
    angles = np.arange(rows, dtype=np.float64)[:, None] * inverse_freq[None, :]
    angles = np.concatenate([angles, angles], axis=1)
    return np.cos(angles).astype(np.float32), np.sin(angles).astype(np.float32)


def layer_kernel(
    lengths_ref, gain_ref, qb_ref, kvb_ref, cos_ref, sin_ref, tokens, w_q, w_kv, w_out,
    kv_out, red_out,
    a_v, wkv_v, wq_v, wo_v, cs_v, scale_v, kvacc_v, kv_v, pk_v, qacc_v, q_v, bias_v, score_v,
    power_v, norm_v, ctx_v, part_v, pair_v, sum_v, ring_v,
    tok_sem, wkv_sem, wq_sem, wo_sem, res_sem, own_sem, gsend, grecv, psend, precv, rsend, rrecv,
):
    req, tp = lax.axis_index("req"), lax.axis_index("tp")
    z, x = lax.div(req, SIDE), lax.rem(req, SIDE)
    y, core = lax.div(tp, 2), lax.rem(tp, 2)
    width = a_v.shape[1]
    kc = width // KSTEPS
    qc = width // QSTEPS

    def turn(at, by):
        return lax.rem(at + (by + SIDE), SIDE)

    def peer(dz=0, dx=0, dy=0, flip=False):
        there = (1 - core) if flip else core
        return {"req": turn(z, dz) * SIDE + turn(x, dx), "tp": turn(y, dy) * 2 + there}

    barrier = pltpu.get_barrier_semaphore()
    neighbours = [
        peer(dz=1), peer(dz=-1), peer(dx=1), peer(dx=-1), peer(dy=1), peer(dy=-1), peer(flip=True)
    ]
    for there in neighbours:
        pl.semaphore_signal(barrier, inc=1, device_id=there, device_id_type=MESH)

    def tok_copy(i):
        return pltpu.make_async_copy(
            tokens.at[:, pl.ds(i * kc, kc)], a_v.at[:, pl.ds(i * kc, kc)], tok_sem.at[i]
        )

    def wkv_copy(i):
        return pltpu.make_async_copy(
            w_kv.at[pl.ds(i * kc, kc)], wkv_v.at[pl.ds(i * kc, kc)], wkv_sem.at[i]
        )

    def wq_copy(i):
        return pltpu.make_async_copy(
            w_q.at[pl.ds(i * kc, kc)], wq_v.at[pl.ds(i * kc, kc)], wq_sem.at[i]
        )

    wo_copy = pltpu.make_async_copy(w_out, wo_v, wo_sem)
    for i in range(KSTEPS):
        tok_copy(i).start()
        wkv_copy(i).start()
    for i in range(KSTEPS):
        wq_copy(i).start()
    wo_copy.start()

    cols = part_v.shape[5]
    my_rows = pl.ds(pl.multiple_of(tp * SHARE, SHARE), SHARE)
    rest_copies = [
        pltpu.make_async_copy(
            tokens.at[my_rows, pl.ds(n * cols, cols)], red_out.at[3, n // 2, n % 2], res_sem.at[n]
        )
        for n in range(2 * CHUNKS)
    ]
    for copy in rest_copies:
        copy.start()

    lens = [lengths_ref[j, req] for j in range(PROMPTS_DEV)]
    starts = [0]
    for j in range(PROMPTS_DEV - 1):
        starts.append(starts[-1] + lens[j])

    base_cos = [cos_ref[pl.ds(starts[j], 1), :] for j in range(PROMPTS_DEV)]
    base_sin = [sin_ref[pl.ds(starts[j], 1), :] for j in range(PROMPTS_DEV)]

    def by_prompt(row, picks):
        out = picks[0]
        for j in range(1, PROMPTS_DEV):
            out = jnp.where(row >= starts[j], picks[j], out)
        return out

    @pl.loop(0, ROWS // 64)
    def _(i):
        at = pl.ds(i * 64, 64)
        row = lax.broadcasted_iota(jnp.int32, (64, HEAD_DIM), 0) + i * 64
        lane = lax.broadcasted_iota(jnp.int32, (64, HEAD_DIM), 1)
        bc, bs = by_prompt(row, base_cos), by_prompt(row, base_sin)
        ac, asn = cos_ref[at, :], sin_ref[at, :]
        cs_v[0, at, :] = ac * bc + asn * bs
        sine = asn * bc - ac * bs
        cs_v[1, at, :] = jnp.where(lane < HEAD_DIM // 2, -sine, sine)
        scale_v[at, :] = jnp.zeros((64, HEAD_DIM), jnp.float32)
        kvacc_v[at, :] = jnp.zeros((64, 2 * HEAD_DIM), jnp.float32)

    def rope(value, at):
        return value * cs_v[0, at, :] + pltpu.roll(value, HEAD_DIM // 2, 1) * cs_v[1, at, :]

    def kv_step(i, carry):
        tok_copy(i).wait()
        lanes = pl.ds(pl.multiple_of(i * kc, kc), kc)
        gain = gain_ref[lanes].reshape(1, kc)

        @pl.loop(0, ROWS // 64)
        def _(j):
            at = pl.ds(j * 64, 64)
            part = a_v[at, lanes]
            wide = part.astype(jnp.float32)
            squares = scale_v[at, :]
            for g in range(kc // HEAD_DIM):
                piece = wide[:, g * HEAD_DIM:(g + 1) * HEAD_DIM]
                squares = squares + piece * piece
            scale_v[at, :] = squares
            a_v[at, lanes] = part * gain

        wkv_copy(i).wait()
        kvacc_v[...] += jnp.dot(
            a_v[:, lanes], wkv_v[lanes, :], preferred_element_type=jnp.float32
        )
        return carry

    lax.fori_loop(0, KSTEPS, kv_step, 0)

    kvb = kvb_ref[...].astype(jnp.float32).reshape(1, 2 * HEAD_DIM)

    @pl.loop(0, ROWS // 128)
    def _(i):
        at = pl.ds(i * 128, 128)
        mean = jnp.sum(scale_v[at, :], axis=1, keepdims=True) / width
        inverse = jnp.broadcast_to(lax.rsqrt(mean + epsilon), (128, HEAD_DIM))
        scale_v[at, :] = inverse
        keys = kvacc_v[at, :HEAD_DIM] * inverse + kvb[:, :HEAD_DIM]
        kv_v[at, :HEAD_DIM] = rope(keys, at).astype(jnp.bfloat16)
        values = kvacc_v[at, HEAD_DIM:] * inverse + kvb[:, HEAD_DIM:]
        kv_v[at, HEAD_DIM:] = values.astype(jnp.bfloat16)

    column = lax.broadcasted_iota(jnp.int32, (1, ROWS), 1)
    target = column
    for j in range(PROMPTS_DEV - 1):
        extra = lax.div(lens[j] + (ALIGN - 1), ALIGN) * ALIGN - lens[j]
        target = target + jnp.where(column >= starts[j + 1], extra, 0)
    for part in range(2):
        line = lax.broadcasted_iota(jnp.int32, (SPLIT, ROWS), 0) + part * SPLIT
        spread = jnp.where(line == target, 1.0, 0.0).astype(jnp.bfloat16)
        pk_v[part * SPLIT:(part + 1) * SPLIT, :] = jnp.dot(
            spread, kv_v[...], preferred_element_type=jnp.float32
        ).astype(jnp.bfloat16)

    pl.semaphore_wait(barrier, len(neighbours))

    def origin(s, a, b):
        dz, dx = (b, a) if s == 0 else (a, b)
        return turn(z, dz) * SIDE + turn(x, dx)

    def landing(s, a, b, lo, size):
        row = origin(s, a, b) * PACKED + (s * SPLIT + lo)
        return kv_out.at[pl.ds(pl.multiple_of(row, ALIGN), size)]

    def gather_copy(s, event, a, b, lo, size, ring, step):
        source = pk_v.at[pl.ds(s * SPLIT + lo, size)] if (a, b) == (0, 0) else landing(s, a, b, lo, size)
        along_x = (ring == 0) == (s == 0)
        there = peer(dx=step) if along_x else peer(dz=step)
        return pltpu.make_async_remote_copy(
            src_ref=source, dst_ref=landing(s, a, b, lo, size),
            send_sem=gsend.at[s, event], recv_sem=grecv.at[s, event],
            device_id=there, device_id_type=MESH,
        )

    def outgoing(s, event):
        ring = 0 if event < 4 else 1
        a, b, lo, size = ARRIVALS[event]
        kind = event % 4
        step = 1 if kind in (0, 2) else -1
        if ring == 0:
            a = a + step if kind < 2 else (-1 if kind == 2 else 1)
        else:
            b = b + step if kind < 2 else (-1 if kind == 2 else 1)
        return gather_copy(s, event, a, b, lo, size, ring, step)

    def gather_send(*events):
        for event in events:
            for s in range(2):
                outgoing(s, event).start()

    def gather_wait(*events):
        for event in events:
            for s in range(2):
                place_at = landing(s, *ARRIVALS[event])
                pltpu.make_async_remote_copy(
                    src_ref=place_at, dst_ref=place_at,
                    send_sem=gsend.at[s, event], recv_sem=grecv.at[s, event],
                    device_id=peer(dx=1), device_id_type=MESH,
                ).wait_recv()

    own_row = pl.multiple_of(req * PACKED, ALIGN)
    own_copy = pltpu.make_async_copy(pk_v, kv_out.at[pl.ds(own_row, PACKED)], own_sem.at[0])
    gather_send(0, 1, 4, 5)
    own_copy.start()

    heads = q_v.shape[0]
    qb = qb_ref[...].astype(jnp.float32).reshape(1, heads * HEAD_DIM)
    factor = math.log2(math.e) / math.sqrt(HEAD_DIM)
    right, left, across = turn(y, 1), turn(y, -1), turn(y, 2)

    def queries(count, chip_of, first):
        def q_step(i, carry):
            if first:
                for j in range(KSTEPS // QSTEPS):
                    wq_copy(i * (KSTEPS // QSTEPS) + j).wait()
            lanes = pl.ds(pl.multiple_of(i * qc, qc), qc)
            held = [
                a_v[pl.ds(pl.multiple_of(chip_of(n) * BLOCK, BLOCK), BLOCK), lanes]
                for n in range(count)
            ]
            product = jnp.dot(
                jnp.concatenate(held, axis=0) if count > 1 else held[0],
                wq_v[lanes, :], preferred_element_type=jnp.float32,
            )
            at = slice(0, count * BLOCK)

            @pl.when(i == 0)
            def _():
                qacc_v[at, :] = product

            @pl.when(i > 0)
            def _():
                qacc_v[at, :] += product

            return carry

        lax.fori_loop(0, QSTEPS, q_step, 0)

    def attend(count, chip_of):
        def block_step(n, carry):
            chip = chip_of(n)
            q0 = pl.multiple_of(chip * BLOCK, BLOCK)
            k0 = pl.multiple_of(lax.div(chip, 3) * BLOCK, BLOCK)
            for part in range(2):
                from_row = pl.ds(pl.multiple_of(n * BLOCK + part * 64, 64), 64)
                at = pl.ds(pl.multiple_of(q0 + part * 64, 64), 64)
                inverse = scale_v[at, :]
                for h in range(heads):
                    lanes = slice(h * HEAD_DIM, (h + 1) * HEAD_DIM)
                    turned = rope(qacc_v[from_row, lanes] * inverse + qb[:, lanes], at)
                    q_v[h, part * 64:(part + 1) * 64, :] = (turned * factor).astype(jnp.bfloat16)
            row = lax.broadcasted_iota(jnp.int32, (BLOCK, WINDOW), 0) + q0
            col = lax.broadcasted_iota(jnp.int32, (BLOCK, WINDOW), 1) + k0
            begin = by_prompt(row, starts)
            bias_v[...] = jnp.where((col <= row) & (col >= begin), 0.0, -1e30)
            score_v[...] = lax.dot_general(
                q_v[...].reshape(heads * BLOCK, HEAD_DIM), kv_v[pl.ds(k0, WINDOW), :HEAD_DIM],
                (((1,), (1,)), ((), ())), preferred_element_type=jnp.float32,
            )
            for h in range(heads):
                at = slice(h * BLOCK, (h + 1) * BLOCK)
                scores = score_v[at, :] + bias_v[...]
                powers = jnp.exp2(scores - jnp.max(scores, axis=1, keepdims=True))
                total = jnp.sum(powers, axis=1, keepdims=True)
                power_v[at, :] = powers.astype(jnp.bfloat16)
                norm_v[at, :] = jnp.broadcast_to(1.0 / total, (BLOCK, HEAD_DIM))
            mixed = jnp.dot(
                power_v[...], kv_v[pl.ds(k0, WINDOW), HEAD_DIM:],
                preferred_element_type=jnp.float32,
            ) * norm_v[...]
            to_row = pl.ds(pl.multiple_of(n * BLOCK, BLOCK), BLOCK)
            for h in range(heads):
                ctx_v[to_row, h * HEAD_DIM:(h + 1) * HEAD_DIM] = mixed[
                    h * BLOCK:(h + 1) * BLOCK
                ].astype(jnp.bfloat16)
            return carry

        lax.fori_loop(0, count, block_step, 0)

    chips = (across, right, left, y)

    def pair_copy(c, slot):
        return pltpu.make_async_remote_copy(
            src_ref=part_v.at[c, :, chips[slot], 1 - core], dst_ref=pair_v.at[c, :, chips[slot]],
            send_sem=psend.at[c, slot], recv_sem=precv.at[c, slot],
            device_id=peer(flip=True), device_id_type=MESH,
        )

    def project(c, slots):
        for h in range(2):
            at = pl.multiple_of((2 * c + h) * cols, cols)
            product = jnp.dot(
                ctx_v[0:len(slots) * BLOCK, :], wo_v[:, pl.ds(at, cols)],
                preferred_element_type=jnp.float32,
            ).astype(jnp.bfloat16)
            for n, slot in enumerate(slots):
                part_v[c, h, chips[slot]] = product[n * BLOCK:(n + 1) * BLOCK].reshape(
                    2, SHARE, cols
                )
        for slot in slots:
            pair_copy(c, slot).start()

    def pair_sum(c, slot):
        pair_copy(c, slot).wait_recv()
        chip = chips[slot]
        for h in range(2):
            sum_v[c, h, chip] = part_v[c, h, chip, core] + pair_v[c, h, chip]

    def ring_copy(c, k):
        source, landing_ref, dy = (
            (sum_v.at[c, 0, across], ring_v.at[c, 0], 1),
            (sum_v.at[c, 1, across], ring_v.at[c, 1], -1),
            (sum_v.at[c, 1, right], red_out.at[1, c, 1], 1),
            (sum_v.at[c, 0, left], red_out.at[2, c, 0], -1),
            (sum_v.at[c, 0, right], red_out.at[1, c, 0], 1),
            (sum_v.at[c, 1, left], red_out.at[2, c, 1], -1),
        )[k]
        return pltpu.make_async_remote_copy(
            src_ref=source, dst_ref=landing_ref, send_sem=rsend.at[c, k], recv_sem=rrecv.at[c, k],
            device_id=peer(dy=dy), device_id_type=MESH,
        )

    def send_across(c):
        pair_sum(c, 0)
        ring_copy(c, 0).start()
        ring_copy(c, 1).start()

    def send_beside(c):
        for slot in (1, 2):
            pair_sum(c, slot)
            ring_copy(c, 1 + slot).start()
        for h, chip in ((0, right), (1, left)):
            ring_copy(c, h).wait_recv()
            sum_v[c, h, chip] = sum_v[c, h, chip] + ring_v[c, h]
            ring_copy(c, 4 + h).start()

    def across_of(n):
        return across

    def beside_of(n):
        return turn(y, 1 + 2 * n)

    def own_of(n):
        return y

    queries(1, across_of, True)
    attend(1, across_of)
    wo_copy.wait()

    def across_step(c, carry):
        project(c, (0,))

        @pl.when(c >= 1)
        def _():
            send_across(c - 1)

        return carry

    lax.fori_loop(0, CHUNKS, across_step, 0)
    queries(2, beside_of, False)
    send_across(CHUNKS - 1)
    gather_wait(0, 1)
    gather_send(2, 3, 8, 9, 12, 13)
    attend(2, beside_of)

    def beside_step(c, carry):
        project(c, (1, 2))

        @pl.when(c >= 1)
        def _():
            send_beside(c - 1)

        return carry

    lax.fori_loop(0, CHUNKS, beside_step, 0)
    send_beside(CHUNKS - 1)
    gather_wait(2, 3)
    gather_send(16, 17)
    gather_wait(4, 5)
    gather_send(6, 7)
    queries(1, own_of, False)
    gather_wait(8, 9, 12, 13)
    gather_send(10, 11, 14, 15)
    attend(1, own_of)

    def own_step(c, carry):
        project(c, (3,))

        @pl.when(c >= 1)
        def _():
            pair_sum(c - 1, 3)

        return carry

    lax.fori_loop(0, CHUNKS, own_step, 0)
    pair_sum(CHUNKS - 1, 3)
    final = pltpu.make_async_copy(sum_v.at[:, :, y], red_out.at[0], own_sem.at[1])
    final.start()
    gather_wait(16, 17)
    gather_send(18, 19)
    gather_wait(6, 7, 10, 11, 14, 15, 18, 19)

    def ring_end(c, carry):
        for k in range(2, 6):
            ring_copy(c, k).wait_recv()
        for k in range(6):
            ring_copy(c, k).wait_send()
        for slot in range(len(chips)):
            pair_copy(c, slot).wait_send()
        return carry

    lax.fori_loop(0, CHUNKS, ring_end, 0)
    final.wait()
    own_copy.wait()
    for copy in rest_copies:
        copy.wait()
    for event in range(len(ARRIVALS)):
        for s in range(2):
            outgoing(s, event).wait_send()


def layer(tokens, norm_gain, w_query, q_bias, w_key_value, kv_bias, w_out, prompt_lengths):
    rows, width = tokens.shape
    q_width = w_query.shape[1]
    smem = pl.BlockSpec(memory_space=pltpu.SMEM)
    vmem = pl.BlockSpec(memory_space=pltpu.VMEM)
    hbm = pl.BlockSpec(memory_space=pl.ANY)
    streams = SIDE * SIDE
    heads = q_width // HEAD_DIM
    cols = width // (2 * CHUNKS)
    cos_table, sin_table = rope_tables(rows)
    bf16, f32 = jnp.bfloat16, jnp.float32
    dma = pltpu.SemaphoreType.DMA
    return pl.pallas_call(
        layer_kernel,
        out_shape=(
            pltpu.VMEM((streams * PACKED, 2 * HEAD_DIM), bf16),
            pltpu.VMEM((4, CHUNKS, 2, SHARE, cols), bf16),
        ),
        in_specs=[smem] + [vmem] * 5 + [hbm] * 4,
        out_specs=(hbm, hbm),
        scratch_shapes=[
            pltpu.VMEM((rows, width), bf16),
            pltpu.VMEM((width, 2 * HEAD_DIM), bf16),
            pltpu.VMEM((width, q_width), bf16),
            pltpu.VMEM((q_width, width), bf16),
            pltpu.VMEM((2, rows, HEAD_DIM), f32),
            pltpu.VMEM((rows, HEAD_DIM), f32),
            pltpu.VMEM((rows, 2 * HEAD_DIM), f32),
            pltpu.VMEM((rows, 2 * HEAD_DIM), bf16),
            pltpu.VMEM((PACKED, 2 * HEAD_DIM), bf16),
            pltpu.VMEM((2 * BLOCK, q_width), f32),
            pltpu.VMEM((heads, BLOCK, HEAD_DIM), bf16),
            pltpu.VMEM((BLOCK, WINDOW), f32),
            pltpu.VMEM((heads * BLOCK, WINDOW), f32),
            pltpu.VMEM((heads * BLOCK, WINDOW), bf16),
            pltpu.VMEM((heads * BLOCK, HEAD_DIM), f32),
            pltpu.VMEM((2 * BLOCK, q_width), bf16),
            pltpu.VMEM((CHUNKS, 2, SIDE, 2, SHARE, cols), bf16),
            pltpu.VMEM((CHUNKS, 2, SIDE, SHARE, cols), bf16),
            pltpu.VMEM((CHUNKS, 2, SIDE, SHARE, cols), bf16),
            pltpu.VMEM((CHUNKS, 2, SHARE, cols), bf16),
            dma((KSTEPS,)), dma((KSTEPS,)), dma((KSTEPS,)), dma(()), dma((2 * CHUNKS,)), dma((2,)),
            dma((2, len(ARRIVALS))), dma((2, len(ARRIVALS))),
            dma((CHUNKS, SIDE)), dma((CHUNKS, SIDE)), dma((CHUNKS, 6)), dma((CHUNKS, 6)),
        ],
        compiler_params=pltpu.CompilerParams(
            collective_id=0, has_side_effects=True, vmem_limit_bytes=56 << 20
        ),
        cost_estimate=pl.CostEstimate(
            flops=2 * rows * width * (2 * q_width + 2 * HEAD_DIM), transcendentals=0,
            bytes_accessed=2 * (rows * width + 2 * width * q_width + 2 * width * HEAD_DIM),
        ),
        name="layer",
    )(
        prompt_lengths.T, norm_gain, q_bias, kv_bias,
        jnp.asarray(cos_table), jnp.asarray(sin_table),
        tokens, w_query, w_key_value, w_out,
    )


def place_kernel(lengths_ref, prompts_ref, slots_ref, kv_ref, red_ref, out_ref, att_ref,
                 zero_v, att_v, att_sem, out_sem):
    requests, slot_rows = out_ref.shape[0], out_ref.shape[1]
    me = lax.axis_index("req")
    zero_v[...] = jnp.zeros(zero_v.shape, zero_v.dtype)

    def one(r, carry):
        prompt = prompts_ref[me * requests + r]
        stream = lax.div(prompt, PROMPTS_DEV)
        within = prompt - stream * PROMPTS_DEV
        start = stream * PACKED
        for j in range(PROMPTS_DEV - 1):
            padded = lax.div(lengths_ref[j, stream] + (ALIGN - 1), ALIGN) * ALIGN
            start = start + jnp.where(j < within, padded, 0)
        start = pl.multiple_of(start, ALIGN)
        live = lax.div(lengths_ref[within, stream] + (ALIGN - 1), ALIGN) * ALIGN
        live = pl.multiple_of(live, ALIGN)
        rest = pl.multiple_of(slot_rows - live, ALIGN)
        slot = slots_ref[0, r]

        @pl.when(live > 0)
        def _():
            pltpu.make_async_copy(
                kv_ref.at[pl.ds(start, live)], out_ref.at[slot, pl.ds(0, live)], out_sem.at[r]
            ).start()

        @pl.when(rest > 0)
        def _():
            pltpu.make_async_copy(
                zero_v.at[pl.ds(0, rest)], out_ref.at[slot, pl.ds(live, rest)], out_sem.at[r]
            ).start()

        return carry

    lax.fori_loop(0, requests, one, 0)
    cols = red_ref.shape[4]

    @pl.loop(0, SHARE // 16)
    def _(i):
        at = pl.ds(i * 16, 16)
        for c in range(CHUNKS):
            for h in range(2):
                place_at = slice((2 * c + h) * cols, (2 * c + h + 1) * cols)
                total = red_ref[3, c, h, at, :].astype(jnp.float32)
                for k in range(3):
                    total = total + red_ref[k, c, h, at, :].astype(jnp.float32)
                att_v[at, place_at] = total.astype(jnp.bfloat16)

    att_store = pltpu.make_async_copy(att_v, att_ref, att_sem)
    att_store.start()

    def done(r, carry):
        pltpu.make_async_copy(zero_v, out_ref.at[slots_ref[0, r]], out_sem.at[r]).wait()
        return carry

    lax.fori_loop(0, requests, done, 0)
    att_store.wait()


def place(kv_all, reduced, width, prompt_lengths, request_prompt, cache_slot):
    requests = cache_slot.shape[1]
    vmem = pl.BlockSpec(memory_space=pltpu.VMEM)
    slot_rows = ROWS // 2
    smem = pl.BlockSpec(memory_space=pltpu.SMEM)
    hbm = pl.BlockSpec(memory_space=pl.ANY)
    bf16 = jnp.bfloat16
    return pl.pallas_call(
        place_kernel,
        out_shape=(
            jax.ShapeDtypeStruct((requests, slot_rows, 2 * HEAD_DIM), bf16),
            jax.ShapeDtypeStruct((SHARE, width), bf16),
        ),
        in_specs=[smem, smem, smem, vmem, vmem],
        out_specs=(hbm, hbm),
        scratch_shapes=[
            pltpu.VMEM((slot_rows, 2 * HEAD_DIM), bf16),
            pltpu.VMEM((SHARE, width), bf16),
            pltpu.SemaphoreType.DMA(()),
            pltpu.SemaphoreType.DMA((requests,)),
        ],
        compiler_params=pltpu.CompilerParams(vmem_limit_bytes=16 << 20),
        name="place",
    )(prompt_lengths.T, request_prompt, cache_slot, kv_all, reduced)


def on_device(
    tokens, norm_gain, w_query, q_bias, w_key_value, kv_bias, w_out, prompt_lengths,
    request_prompt, cache_slot,
):
    kv_all, reduced = layer(
        tokens, norm_gain, w_query, q_bias, w_key_value, kv_bias, w_out, prompt_lengths
    )
    prompt_cache, attended = place(
        kv_all, reduced, tokens.shape[1], prompt_lengths, request_prompt, cache_slot
    )
    return (attended, prompt_cache)


def solution(mesh):
    placed = (
        P("req", None),
        P(),
        P(None, "tp"),
        P("tp"),
        P(None, "tp"),
        P("tp"),
        P("tp", None),
        P(),
        P(),
        P("req", None),
    )
    return jax.shard_map(
        on_device,
        mesh=mesh,
        in_specs=placed,
        out_specs=(P(("req", "tp"), None), P("req", None, "tp")),
        check_vma=False,
    )
```

```python
import math

import jax
import jax.numpy as jnp
import numpy as np
from jax import lax
from jax.experimental import pallas as pl
from jax.experimental.pallas import tpu as pltpu
from jax.sharding import PartitionSpec as P

HEAD_DIM = 128
PROMPTS_DEV = 4
FAN = 12
ALIGN = 16

epsilon = 1e-06
rope_base = 1000000.0

SIDE = 4
TP = 8
ROWS = 512
BLOCK = 128
SHARE = 64
PACKED = ROWS + 2 * ALIGN
SPLIT = PACKED // 2
CUT = 144
KSTEPS = 10
QSTEPS = 2
CHUNKS = 5
WINDOW = 384
MESH = pl.DeviceIdType.MESH

FIRST = ((-1, 0, 0, SPLIT), (1, 0, 0, SPLIT), (2, 0, 0, CUT), (2, 0, CUT, SPLIT - CUT))
HELD = (0, -1, 1, 2)
ARRIVALS = FIRST + tuple(
    (a, b, lo, size)
    for a in HELD
    for b, lo, size in ((-1, 0, SPLIT), (1, 0, SPLIT), (2, 0, CUT), (2, CUT, SPLIT - CUT))
)


def rope_tables(rows):
    half_dim = HEAD_DIM // 2
    inverse_freq = rope_base ** (-(np.arange(half_dim, dtype=np.float64) * 2.0 / HEAD_DIM))
    angles = np.arange(rows, dtype=np.float64)[:, None] * inverse_freq[None, :]
    angles = np.concatenate([angles, angles], axis=1)
    return np.cos(angles).astype(np.float32), np.sin(angles).astype(np.float32)


def layer_kernel(
    lengths_ref, gain_ref, qb_ref, kvb_ref, cos_ref, sin_ref, tokens, w_q, w_kv, w_out,
    kv_out, red_out,
    a_v, wkv_v, wq_v, wo_v, cs_v, scale_v, kvacc_v, kv_v, pk_v, qacc_v, q_v, bias_v, score_v,
    power_v, norm_v, ctx_v, part_v, pair_v, sum_v, ring_v,
    tok_sem, wkv_sem, wq_sem, wo_sem, res_sem, own_sem, gsend, grecv, psend, precv, rsend, rrecv,
):
    req, tp = lax.axis_index("req"), lax.axis_index("tp")
    z, x = lax.div(req, SIDE), lax.rem(req, SIDE)
    y, core = lax.div(tp, 2), lax.rem(tp, 2)
    width = a_v.shape[1]
    kc = width // KSTEPS
    qc = width // QSTEPS

    def turn(at, by):
        return lax.rem(at + (by + SIDE), SIDE)

    def peer(dz=0, dx=0, dy=0, flip=False):
        there = (1 - core) if flip else core
        return {"req": turn(z, dz) * SIDE + turn(x, dx), "tp": turn(y, dy) * 2 + there}

    barrier = pltpu.get_barrier_semaphore()
    neighbours = [
        peer(dz=1), peer(dz=-1), peer(dx=1), peer(dx=-1), peer(dy=1), peer(dy=-1), peer(flip=True)
    ]
    for there in neighbours:
        pl.semaphore_signal(barrier, inc=1, device_id=there, device_id_type=MESH)

    def tok_copy(i):
        return pltpu.make_async_copy(
            tokens.at[:, pl.ds(i * kc, kc)], a_v.at[:, pl.ds(i * kc, kc)], tok_sem.at[i]
        )

    def wkv_copy(i):
        return pltpu.make_async_copy(
            w_kv.at[pl.ds(i * kc, kc)], wkv_v.at[pl.ds(i * kc, kc)], wkv_sem.at[i]
        )

    def wq_copy(i):
        return pltpu.make_async_copy(
            w_q.at[pl.ds(i * kc, kc)], wq_v.at[pl.ds(i * kc, kc)], wq_sem.at[i]
        )

    wo_copy = pltpu.make_async_copy(w_out, wo_v, wo_sem)
    for i in range(KSTEPS):
        tok_copy(i).start()
        wkv_copy(i).start()
    for i in range(KSTEPS):
        wq_copy(i).start()
    wo_copy.start()

    cols = part_v.shape[5]
    my_rows = pl.ds(pl.multiple_of(tp * SHARE, SHARE), SHARE)
    rest_copies = [
        pltpu.make_async_copy(
            tokens.at[my_rows, pl.ds(n * cols, cols)], red_out.at[3, n // 2, n % 2], res_sem.at[n]
        )
        for n in range(2 * CHUNKS)
    ]
    for copy in rest_copies:
        copy.start()

    lens = [lengths_ref[j, req] for j in range(PROMPTS_DEV)]
    starts = [0]
    for j in range(PROMPTS_DEV - 1):
        starts.append(starts[-1] + lens[j])

    base_cos = [cos_ref[pl.ds(starts[j], 1), :] for j in range(PROMPTS_DEV)]
    base_sin = [sin_ref[pl.ds(starts[j], 1), :] for j in range(PROMPTS_DEV)]

    def by_prompt(row, picks):
        out = picks[0]
        for j in range(1, PROMPTS_DEV):
            out = jnp.where(row >= starts[j], picks[j], out)
        return out

    @pl.loop(0, ROWS // 64)
    def _(i):
        at = pl.ds(i * 64, 64)
        row = lax.broadcasted_iota(jnp.int32, (64, HEAD_DIM), 0) + i * 64
        lane = lax.broadcasted_iota(jnp.int32, (64, HEAD_DIM), 1)
        bc, bs = by_prompt(row, base_cos), by_prompt(row, base_sin)
        ac, asn = cos_ref[at, :], sin_ref[at, :]
        cs_v[0, at, :] = ac * bc + asn * bs
        sine = asn * bc - ac * bs
        cs_v[1, at, :] = jnp.where(lane < HEAD_DIM // 2, -sine, sine)
        scale_v[at, :] = jnp.zeros((64, HEAD_DIM), jnp.float32)
        kvacc_v[at, :] = jnp.zeros((64, 2 * HEAD_DIM), jnp.float32)

    def rope(value, at):
        return value * cs_v[0, at, :] + pltpu.roll(value, HEAD_DIM // 2, 1) * cs_v[1, at, :]

    def kv_step(i, carry):
        tok_copy(i).wait()
        lanes = pl.ds(pl.multiple_of(i * kc, kc), kc)
        gain = gain_ref[lanes].reshape(1, kc)

        @pl.loop(0, ROWS // 64)
        def _(j):
            at = pl.ds(j * 64, 64)
            part = a_v[at, lanes]
            wide = part.astype(jnp.float32)
            squares = scale_v[at, :]
            for g in range(kc // HEAD_DIM):
                piece = wide[:, g * HEAD_DIM:(g + 1) * HEAD_DIM]
                squares = squares + piece * piece
            scale_v[at, :] = squares
            a_v[at, lanes] = part * gain

        wkv_copy(i).wait()
        kvacc_v[...] += jnp.dot(
            a_v[:, lanes], wkv_v[lanes, :], preferred_element_type=jnp.float32
        )
        return carry

    lax.fori_loop(0, KSTEPS, kv_step, 0)

    kvb = kvb_ref[...].astype(jnp.float32).reshape(1, 2 * HEAD_DIM)

    @pl.loop(0, ROWS // 128)
    def _(i):
        at = pl.ds(i * 128, 128)
        mean = jnp.sum(scale_v[at, :], axis=1, keepdims=True) / width
        inverse = jnp.broadcast_to(lax.rsqrt(mean + epsilon), (128, HEAD_DIM))
        scale_v[at, :] = inverse
        keys = kvacc_v[at, :HEAD_DIM] * inverse + kvb[:, :HEAD_DIM]
        kv_v[at, :HEAD_DIM] = rope(keys, at).astype(jnp.bfloat16)
        values = kvacc_v[at, HEAD_DIM:] * inverse + kvb[:, HEAD_DIM:]
        kv_v[at, HEAD_DIM:] = values.astype(jnp.bfloat16)

    column = lax.broadcasted_iota(jnp.int32, (1, ROWS), 1)
    target = column
    for j in range(PROMPTS_DEV - 1):
        extra = lax.div(lens[j] + (ALIGN - 1), ALIGN) * ALIGN - lens[j]
        target = target + jnp.where(column >= starts[j + 1], extra, 0)
    for part in range(2):
        line = lax.broadcasted_iota(jnp.int32, (SPLIT, ROWS), 0) + part * SPLIT
        spread = jnp.where(line == target, 1.0, 0.0).astype(jnp.bfloat16)
        pk_v[part * SPLIT:(part + 1) * SPLIT, :] = jnp.dot(
            spread, kv_v[...], preferred_element_type=jnp.float32
        ).astype(jnp.bfloat16)

    pl.semaphore_wait(barrier, len(neighbours))

    def origin(s, a, b):
        dz, dx = (b, a) if s == 0 else (a, b)
        return turn(z, dz) * SIDE + turn(x, dx)

    def landing(s, a, b, lo, size):
        row = origin(s, a, b) * PACKED + (s * SPLIT + lo)
        return kv_out.at[pl.ds(pl.multiple_of(row, ALIGN), size)]

    def gather_copy(s, event, a, b, lo, size, ring, step):
        source = pk_v.at[pl.ds(s * SPLIT + lo, size)] if (a, b) == (0, 0) else landing(s, a, b, lo, size)
        along_x = (ring == 0) == (s == 0)
        there = peer(dx=step) if along_x else peer(dz=step)
        return pltpu.make_async_remote_copy(
            src_ref=source, dst_ref=landing(s, a, b, lo, size),
            send_sem=gsend.at[s, event], recv_sem=grecv.at[s, event],
            device_id=there, device_id_type=MESH,
        )

    def outgoing(s, event):
        ring = 0 if event < 4 else 1
        a, b, lo, size = ARRIVALS[event]
        kind = event % 4
        step = 1 if kind in (0, 2) else -1
        if ring == 0:
            a = a + step if kind < 2 else (-1 if kind == 2 else 1)
        else:
            b = b + step if kind < 2 else (-1 if kind == 2 else 1)
        return gather_copy(s, event, a, b, lo, size, ring, step)

    def gather_send(*events):
        for event in events:
            for s in range(2):
                outgoing(s, event).start()

    def gather_wait(*events):
        for event in events:
            for s in range(2):
                place_at = landing(s, *ARRIVALS[event])
                pltpu.make_async_remote_copy(
                    src_ref=place_at, dst_ref=place_at,
                    send_sem=gsend.at[s, event], recv_sem=grecv.at[s, event],
                    device_id=peer(dx=1), device_id_type=MESH,
                ).wait_recv()

    own_row = pl.multiple_of(req * PACKED, ALIGN)
    own_copy = pltpu.make_async_copy(pk_v, kv_out.at[pl.ds(own_row, PACKED)], own_sem.at[0])
    gather_send(0, 1, 4, 5)
    own_copy.start()

    heads = q_v.shape[0]
    qb = qb_ref[...].astype(jnp.float32).reshape(1, heads * HEAD_DIM)
    factor = math.log2(math.e) / math.sqrt(HEAD_DIM)
    right, left, across = turn(y, 1), turn(y, -1), turn(y, 2)

    def queries(count, chip_of, first):
        def q_step(i, carry):
            if first:
                for j in range(KSTEPS // QSTEPS):
                    wq_copy(i * (KSTEPS // QSTEPS) + j).wait()
            lanes = pl.ds(pl.multiple_of(i * qc, qc), qc)
            held = [
                a_v[pl.ds(pl.multiple_of(chip_of(n) * BLOCK, BLOCK), BLOCK), lanes]
                for n in range(count)
            ]
            product = jnp.dot(
                jnp.concatenate(held, axis=0) if count > 1 else held[0],
                wq_v[lanes, :], preferred_element_type=jnp.float32,
            )
            at = slice(0, count * BLOCK)

            @pl.when(i == 0)
            def _():
                qacc_v[at, :] = product

            @pl.when(i > 0)
            def _():
                qacc_v[at, :] += product

            return carry

        lax.fori_loop(0, QSTEPS, q_step, 0)

    def attend(count, chip_of):
        def block_step(n, carry):
            chip = chip_of(n)
            q0 = pl.multiple_of(chip * BLOCK, BLOCK)
            k0 = pl.multiple_of(lax.div(chip, 3) * BLOCK, BLOCK)
            for part in range(2):
                from_row = pl.ds(pl.multiple_of(n * BLOCK + part * 64, 64), 64)
                at = pl.ds(pl.multiple_of(q0 + part * 64, 64), 64)
                inverse = scale_v[at, :]
                for h in range(heads):
                    lanes = slice(h * HEAD_DIM, (h + 1) * HEAD_DIM)
                    turned = rope(qacc_v[from_row, lanes] * inverse + qb[:, lanes], at)
                    q_v[h, part * 64:(part + 1) * 64, :] = (turned * factor).astype(jnp.bfloat16)
            row = lax.broadcasted_iota(jnp.int32, (BLOCK, WINDOW), 0) + q0
            col = lax.broadcasted_iota(jnp.int32, (BLOCK, WINDOW), 1) + k0
            begin = by_prompt(row, starts)
            bias_v[...] = jnp.where((col <= row) & (col >= begin), 0.0, -1e30)
            score_v[...] = lax.dot_general(
                q_v[...].reshape(heads * BLOCK, HEAD_DIM), kv_v[pl.ds(k0, WINDOW), :HEAD_DIM],
                (((1,), (1,)), ((), ())), preferred_element_type=jnp.float32,
            )
            for h in range(heads):
                at = slice(h * BLOCK, (h + 1) * BLOCK)
                scores = score_v[at, :] + bias_v[...]
                powers = jnp.exp2(scores - jnp.max(scores, axis=1, keepdims=True))
                total = jnp.sum(powers, axis=1, keepdims=True)
                power_v[at, :] = powers.astype(jnp.bfloat16)
                norm_v[at, :] = jnp.broadcast_to(1.0 / total, (BLOCK, HEAD_DIM))
            mixed = jnp.dot(
                power_v[...], kv_v[pl.ds(k0, WINDOW), HEAD_DIM:],
                preferred_element_type=jnp.float32,
            ) * norm_v[...]
            to_row = pl.ds(pl.multiple_of(n * BLOCK, BLOCK), BLOCK)
            for h in range(heads):
                ctx_v[to_row, h * HEAD_DIM:(h + 1) * HEAD_DIM] = mixed[
                    h * BLOCK:(h + 1) * BLOCK
                ].astype(jnp.bfloat16)
            return carry

        lax.fori_loop(0, count, block_step, 0)

    chips = (across, right, left, y)

    def pair_copy(c, slot):
        return pltpu.make_async_remote_copy(
            src_ref=part_v.at[c, :, chips[slot], 1 - core], dst_ref=pair_v.at[c, :, chips[slot]],
            send_sem=psend.at[c, slot], recv_sem=precv.at[c, slot],
            device_id=peer(flip=True), device_id_type=MESH,
        )

    def project(c, slots):
        for h in range(2):
            at = pl.multiple_of((2 * c + h) * cols, cols)
            product = jnp.dot(
                ctx_v[0:len(slots) * BLOCK, :], wo_v[:, pl.ds(at, cols)],
                preferred_element_type=jnp.float32,
            ).astype(jnp.bfloat16)
            for n, slot in enumerate(slots):
                part_v[c, h, chips[slot]] = product[n * BLOCK:(n + 1) * BLOCK].reshape(
                    2, SHARE, cols
                )
        for slot in slots:
            pair_copy(c, slot).start()

    def pair_sum(c, slot):
        pair_copy(c, slot).wait_recv()
        chip = chips[slot]
        for h in range(2):
            sum_v[c, h, chip] = part_v[c, h, chip, core] + pair_v[c, h, chip]

    def ring_copy(c, k):
        source, landing_ref, dy = (
            (sum_v.at[c, 0, across], ring_v.at[c, 0], 1),
            (sum_v.at[c, 1, across], ring_v.at[c, 1], -1),
            (sum_v.at[c, 1, right], red_out.at[1, c, 1], 1),
            (sum_v.at[c, 0, left], red_out.at[2, c, 0], -1),
            (sum_v.at[c, 0, right], red_out.at[1, c, 0], 1),
            (sum_v.at[c, 1, left], red_out.at[2, c, 1], -1),
        )[k]
        return pltpu.make_async_remote_copy(
            src_ref=source, dst_ref=landing_ref, send_sem=rsend.at[c, k], recv_sem=rrecv.at[c, k],
            device_id=peer(dy=dy), device_id_type=MESH,
        )

    def send_across(c):
        pair_sum(c, 0)
        ring_copy(c, 0).start()
        ring_copy(c, 1).start()

    def send_beside(c):
        for slot in (1, 2):
            pair_sum(c, slot)
            ring_copy(c, 1 + slot).start()
        for h, chip in ((0, right), (1, left)):
            ring_copy(c, h).wait_recv()
            sum_v[c, h, chip] = sum_v[c, h, chip] + ring_v[c, h]
            ring_copy(c, 4 + h).start()

    def across_of(n):
        return across

    def beside_of(n):
        return turn(y, 1 + 2 * n)

    def own_of(n):
        return y

    queries(1, across_of, True)
    attend(1, across_of)
    wo_copy.wait()

    def across_step(c, carry):
        project(c, (0,))

        @pl.when(c >= 1)
        def _():
            send_across(c - 1)

        return carry

    lax.fori_loop(0, CHUNKS, across_step, 0)
    queries(2, beside_of, False)
    send_across(CHUNKS - 1)
    attend(2, beside_of)
    gather_wait(0, 1)
    gather_send(2, 3, 8, 9, 12, 13)

    def beside_step(c, carry):
        project(c, (1, 2))

        @pl.when(c >= 1)
        def _():
            send_beside(c - 1)

        return carry

    lax.fori_loop(0, CHUNKS, beside_step, 0)
    send_beside(CHUNKS - 1)
    gather_wait(2, 3)
    gather_send(16, 17)
    gather_wait(4, 5)
    gather_send(6, 7)
    queries(1, own_of, False)
    gather_wait(8, 9, 12, 13)
    gather_send(10, 11, 14, 15)
    attend(1, own_of)

    def own_step(c, carry):
        project(c, (3,))

        @pl.when(c >= 1)
        def _():
            pair_sum(c - 1, 3)

        return carry

    lax.fori_loop(0, CHUNKS, own_step, 0)
    pair_sum(CHUNKS - 1, 3)
    final = pltpu.make_async_copy(sum_v.at[:, :, y], red_out.at[0], own_sem.at[1])
    final.start()
    gather_wait(16, 17)
    gather_send(18, 19)
    gather_wait(6, 7, 10, 11, 14, 15, 18, 19)

    def ring_end(c, carry):
        for k in range(2, 6):
            ring_copy(c, k).wait_recv()
        for k in range(6):
            ring_copy(c, k).wait_send()
        for slot in range(len(chips)):
            pair_copy(c, slot).wait_send()
        return carry

    lax.fori_loop(0, CHUNKS, ring_end, 0)
    final.wait()
    own_copy.wait()
    for copy in rest_copies:
        copy.wait()
    for event in range(len(ARRIVALS)):
        for s in range(2):
            outgoing(s, event).wait_send()


def layer(tokens, norm_gain, w_query, q_bias, w_key_value, kv_bias, w_out, prompt_lengths):
    rows, width = tokens.shape
    q_width = w_query.shape[1]
    smem = pl.BlockSpec(memory_space=pltpu.SMEM)
    vmem = pl.BlockSpec(memory_space=pltpu.VMEM)
    hbm = pl.BlockSpec(memory_space=pl.ANY)
    streams = SIDE * SIDE
    heads = q_width // HEAD_DIM
    cols = width // (2 * CHUNKS)
    cos_table, sin_table = rope_tables(rows)
    bf16, f32 = jnp.bfloat16, jnp.float32
    dma = pltpu.SemaphoreType.DMA
    return pl.pallas_call(
        layer_kernel,
        out_shape=(
            pltpu.VMEM((streams * PACKED, 2 * HEAD_DIM), bf16),
            pltpu.VMEM((4, CHUNKS, 2, SHARE, cols), bf16),
        ),
        in_specs=[smem] + [vmem] * 5 + [hbm] * 4,
        out_specs=(hbm, hbm),
        scratch_shapes=[
            pltpu.VMEM((rows, width), bf16),
            pltpu.VMEM((width, 2 * HEAD_DIM), bf16),
            pltpu.VMEM((width, q_width), bf16),
            pltpu.VMEM((q_width, width), bf16),
            pltpu.VMEM((2, rows, HEAD_DIM), f32),
            pltpu.VMEM((rows, HEAD_DIM), f32),
            pltpu.VMEM((rows, 2 * HEAD_DIM), f32),
            pltpu.VMEM((rows, 2 * HEAD_DIM), bf16),
            pltpu.VMEM((PACKED, 2 * HEAD_DIM), bf16),
            pltpu.VMEM((2 * BLOCK, q_width), f32),
            pltpu.VMEM((heads, BLOCK, HEAD_DIM), bf16),
            pltpu.VMEM((BLOCK, WINDOW), f32),
            pltpu.VMEM((heads * BLOCK, WINDOW), f32),
            pltpu.VMEM((heads * BLOCK, WINDOW), bf16),
            pltpu.VMEM((heads * BLOCK, HEAD_DIM), f32),
            pltpu.VMEM((2 * BLOCK, q_width), bf16),
            pltpu.VMEM((CHUNKS, 2, SIDE, 2, SHARE, cols), bf16),
            pltpu.VMEM((CHUNKS, 2, SIDE, SHARE, cols), bf16),
            pltpu.VMEM((CHUNKS, 2, SIDE, SHARE, cols), bf16),
            pltpu.VMEM((CHUNKS, 2, SHARE, cols), bf16),
            dma((KSTEPS,)), dma((KSTEPS,)), dma((KSTEPS,)), dma(()), dma((2 * CHUNKS,)), dma((2,)),
            dma((2, len(ARRIVALS))), dma((2, len(ARRIVALS))),
            dma((CHUNKS, SIDE)), dma((CHUNKS, SIDE)), dma((CHUNKS, 6)), dma((CHUNKS, 6)),
        ],
        compiler_params=pltpu.CompilerParams(
            collective_id=0, has_side_effects=True, vmem_limit_bytes=56 << 20
        ),
        cost_estimate=pl.CostEstimate(
            flops=2 * rows * width * (2 * q_width + 2 * HEAD_DIM), transcendentals=0,
            bytes_accessed=2 * (rows * width + 2 * width * q_width + 2 * width * HEAD_DIM),
        ),
        name="layer",
    )(
        prompt_lengths.T, norm_gain, q_bias, kv_bias,
        jnp.asarray(cos_table), jnp.asarray(sin_table),
        tokens, w_query, w_key_value, w_out,
    )


def place_kernel(lengths_ref, prompts_ref, slots_ref, kv_ref, red_ref, out_ref, att_ref,
                 zero_v, att_v, att_sem, out_sem):
    requests, slot_rows = out_ref.shape[0], out_ref.shape[1]
    me = lax.axis_index("req")
    zero_v[...] = jnp.zeros(zero_v.shape, zero_v.dtype)

    def one(r, carry):
        prompt = prompts_ref[me * requests + r]
        stream = lax.div(prompt, PROMPTS_DEV)
        within = prompt - stream * PROMPTS_DEV
        start = stream * PACKED
        for j in range(PROMPTS_DEV - 1):
            padded = lax.div(lengths_ref[j, stream] + (ALIGN - 1), ALIGN) * ALIGN
            start = start + jnp.where(j < within, padded, 0)
        start = pl.multiple_of(start, ALIGN)
        live = lax.div(lengths_ref[within, stream] + (ALIGN - 1), ALIGN) * ALIGN
        live = pl.multiple_of(live, ALIGN)
        rest = pl.multiple_of(slot_rows - live, ALIGN)
        slot = slots_ref[0, r]

        @pl.when(live > 0)
        def _():
            pltpu.make_async_copy(
                kv_ref.at[pl.ds(start, live)], out_ref.at[slot, pl.ds(0, live)], out_sem.at[r]
            ).start()

        @pl.when(rest > 0)
        def _():
            pltpu.make_async_copy(
                zero_v.at[pl.ds(0, rest)], out_ref.at[slot, pl.ds(live, rest)], out_sem.at[r]
            ).start()

        return carry

    lax.fori_loop(0, requests, one, 0)
    cols = red_ref.shape[4]

    @pl.loop(0, SHARE // 16)
    def _(i):
        at = pl.ds(i * 16, 16)
        for c in range(CHUNKS):
            for h in range(2):
                place_at = slice((2 * c + h) * cols, (2 * c + h + 1) * cols)
                total = red_ref[3, c, h, at, :].astype(jnp.float32)
                for k in range(3):
                    total = total + red_ref[k, c, h, at, :].astype(jnp.float32)
                att_v[at, place_at] = total.astype(jnp.bfloat16)

    att_store = pltpu.make_async_copy(att_v, att_ref, att_sem)
    att_store.start()

    def done(r, carry):
        pltpu.make_async_copy(zero_v, out_ref.at[slots_ref[0, r]], out_sem.at[r]).wait()
        return carry

    lax.fori_loop(0, requests, done, 0)
    att_store.wait()


def place(kv_all, reduced, width, prompt_lengths, request_prompt, cache_slot):
    requests = cache_slot.shape[1]
    vmem = pl.BlockSpec(memory_space=pltpu.VMEM)
    slot_rows = ROWS // 2
    smem = pl.BlockSpec(memory_space=pltpu.SMEM)
    hbm = pl.BlockSpec(memory_space=pl.ANY)
    bf16 = jnp.bfloat16
    return pl.pallas_call(
        place_kernel,
        out_shape=(
            jax.ShapeDtypeStruct((requests, slot_rows, 2 * HEAD_DIM), bf16),
            jax.ShapeDtypeStruct((SHARE, width), bf16),
        ),
        in_specs=[smem, smem, smem, vmem, vmem],
        out_specs=(hbm, hbm),
        scratch_shapes=[
            pltpu.VMEM((slot_rows, 2 * HEAD_DIM), bf16),
            pltpu.VMEM((SHARE, width), bf16),
            pltpu.SemaphoreType.DMA(()),
            pltpu.SemaphoreType.DMA((requests,)),
        ],
        compiler_params=pltpu.CompilerParams(vmem_limit_bytes=16 << 20),
        name="place",
    )(prompt_lengths.T, request_prompt, cache_slot, kv_all, reduced)


def on_device(
    tokens, norm_gain, w_query, q_bias, w_key_value, kv_bias, w_out, prompt_lengths,
    request_prompt, cache_slot,
):
    kv_all, reduced = layer(
        tokens, norm_gain, w_query, q_bias, w_key_value, kv_bias, w_out, prompt_lengths
    )
    prompt_cache, attended = place(
        kv_all, reduced, tokens.shape[1], prompt_lengths, request_prompt, cache_slot
    )
    return (attended, prompt_cache)


def solution(mesh):
    placed = (
        P("req", None),
        P(),
        P(None, "tp"),
        P("tp"),
        P(None, "tp"),
        P("tp"),
        P("tp", None),
        P(),
        P(),
        P("req", None),
    )
    return jax.shard_map(
        on_device,
        mesh=mesh,
        in_specs=placed,
        out_specs=(P(("req", "tp"), None), P("req", None, "tp")),
        check_vma=False,
    )
```
